128 devices in a mesh: row: 8 (over y, core), col: 16 (over x, z).
Axes of the slice: x: 4, y: 4, z: 4, core: 2. Of those that a mesh axis runs over, the one named last changes fastest.
Arguments:
- prompt_token_states: bfloat16 [3584, 5120], P('col', 'row'), may hold values from -960 to 960
- gain: bfloat16 [5120], P('row'), may hold values from 0.25 to 1.75
- projection_weight: bfloat16 [5120, 2, 5120], P('col', None, 'row'), may hold values from -0.078125 to 0.078125
- adapter_down_maps: bfloat16 [16, 5120, 256], P('col', 'row'), may hold values from -0.078125 to 0.078125
- adapter_up_maps: bfloat16 [16, 2, 128, 5120], P('col', None, None, 'row'), may hold values from -0.5 to 0.5
- prompt_token_length: int32 [12], replicated, may hold values from 1 to 537, 3584 in all
- prompt_of_request: int32 [144], replicated, may hold values from 0 to 11, never falling along the last dimension, each value on 1 to 16 neighbouring positions
- adapter_of_request: int32 [144], replicated, may hold values from 0 to 63, as said below
- adapter_slot_index: int32 [64], replicated, may hold values from -1 to 15, as said below
Outputs:
- query_rows: bfloat16 [3584, 16, 5120], P('col', None, 'row')
- value_rows: bfloat16 [3584, 16, 5120], P('col', None, 'row')
The draws below stay inside these ranges and needn't reach their ends.
Inputs may be any that keep to these rules, and one draw needn't show every extreme that they name: `adapter_of_request`: every request names a loaded adapter (adapter_slot_index not -1), and every slot 0 to 15 is named by some request. `adapter_slot_index`: the values other than -1 are 0 to 15, each once; the others are -1. `prompt_of_request`: requests of one prompt stand together, prompts in rising order; each prompt has 1 to 16 requests.
All inputs are finite; a program needn't handle non-finite values.
Results may differ from the reference program's by a relative error of at most 0.0057.
Values may be sent and summed in bfloat16 or wider, within the bound.
A program may use at most 128 MiB of HBM per device.

```python
import math
import jax
import jax.numpy as jnp
import numpy as np
from jax import lax

MODEL_WIDTH = 5120
ADAPTER_RANK = 128
SLOTS = 16
PROMPTS = 12
REQS = 144
PTOK = 3584
LMAX = 537
LIVE_ADAPTERS = 16
ADAPTERS = 64
N_COL = 16


def adapter_order(key):
    middle = 1 + jax.random.permutation(jax.random.fold_in(key, 11), ADAPTERS - 2)
    ends = jnp.array([ADAPTERS - 1, 0], dtype=jnp.int32)
    order = jnp.concatenate([ends, middle.astype(jnp.int32)])
    live_part = order[:LIVE_ADAPTERS][jax.random.permutation(jax.random.fold_in(key, 15), LIVE_ADAPTERS)]
    return jnp.concatenate([live_part, order[LIVE_ADAPTERS:]]).astype(jnp.int32)


def draw_adapter_slot_index(key, part):
    order = adapter_order(key)
    place = jnp.argsort(order).astype(jnp.int32)
    return jnp.where(place < LIVE_ADAPTERS, place, -1).astype(jnp.int32)


def draw_adapter_of_request(key, part):
    order = adapter_order(key)
    cover = jax.random.permutation(jax.random.fold_in(key, 12), LIVE_ADAPTERS)
    others = jax.random.randint(jax.random.fold_in(key, 13), (REQS,), 0, LIVE_ADAPTERS)
    index = jnp.arange(REQS)
    chosen = jnp.where(index < LIVE_ADAPTERS, cover[jnp.minimum(index, LIVE_ADAPTERS - 1)], others)
    shuffle = jax.random.permutation(jax.random.fold_in(key, 14), REQS)
    return order[chosen[shuffle]].astype(jnp.int32)


def draw_prompt_token_states(key, part):
    first = jax.random.fold_in(key, 1)
    second = jax.random.fold_in(key, 2)
    columns = 10.0 ** (jnp.arange(MODEL_WIDTH, dtype=jnp.float32) / MODEL_WIDTH)
    mixed = jnp.clip(jax.random.normal(first, (PTOK, MODEL_WIDTH), jnp.float32), -4.0, 4.0)
    rows = jnp.exp(jax.random.uniform(second, (PTOK, 1), jnp.float32, 0.0, math.log(10.0)))
    columns = columns[None, :]
    return (mixed * rows * columns).astype(jnp.bfloat16)


def shard_levels(own_key, shape, cuts, least, largest):
    level, own = 1.0, jax.random.fold_in(own_key, 6)
    for axis_at, parts in cuts:
        heights = jnp.exp(jax.random.uniform(jax.random.fold_in(own, axis_at), (parts,), jnp.float32, least / len(cuts), largest / len(cuts)))
        level = level * jnp.repeat(heights, shape[axis_at] // parts).reshape([-1 if axis == axis_at else 1 for axis in range(len(shape))])
    return level


def split_up(number_of, total, most, lean):
    loads = [(1 << 20) // math.isqrt(standing ** lean) + 1 for standing in range(2, number_of + 1)]
    rest, given = total - most - (number_of - 1), [1] * (number_of - 1)
    while rest > 0:
        free = [i for i in range(number_of - 1) if given[i] < most]
        whole, budget = sum([loads[i] for i in free]), rest
        for i in free:
            addition = min(most - given[i], max(1, budget * loads[i] // whole), rest)
            given[i] = given[i] + addition
            rest = rest - addition
    return np.array([most] + given)


def uneven(rng, count, total, reach, lean):
    if count == 2:
        one = jax.random.randint(rng, (), max(1, total - reach), min(reach, total - 1) + 1)
        return jnp.stack([one, total - one])
    tallies = jnp.asarray(split_up(count, total, reach, lean), jnp.int32)
    couples = (count - 1) // 2
    giver, sink = tallies[1:1 + 2 * couples:2], tallies[2:2 + 2 * couples:2]
    slack = jnp.minimum(giver - 1, reach - sink)
    moved = jax.random.randint(jax.random.fold_in(rng, 1), (couples,), 0, 1 << 20) % (slack + 1)
    tallies = tallies.at[1:1 + 2 * couples:2].set(giver - moved).at[2:2 + 2 * couples:2].set(sink + moved)
    return tallies[jax.random.permutation(jax.random.fold_in(rng, 2), count)]


def centred(rng, dims, width, most, split=(), kind=jnp.bfloat16):
    level = shard_levels(rng, dims, split, -0.22, 0.18) if split else 1.0
    values = jax.random.normal(rng, dims, jnp.float32) * width * level
    return jnp.minimum(jnp.maximum(values, -most), most).astype(kind)


def setup_inputs(seed: int = 0) -> dict:
    splits = jax.random.split(jax.random.key(seed), 10)
    prompt_token_states = draw_prompt_token_states(jax.random.fold_in(splits[9], 71), 0)
    gain = jnp.clip(1.0 + 0.15 * jax.random.normal(splits[1], (MODEL_WIDTH,), jnp.float32), 0.25, 1.75).astype(jnp.bfloat16)
    projection_weight = centred(splits[2], (MODEL_WIDTH, 2, MODEL_WIDTH), MODEL_WIDTH ** -0.5, 0.078125, ((0, 16), (2, 8)))
    adapter_down_maps = centred(splits[3], (LIVE_ADAPTERS, MODEL_WIDTH, 2 * ADAPTER_RANK), MODEL_WIDTH ** -0.5, 0.078125, ((0, 16), (1, 8)))
    adapter_up_maps = centred(splits[4], (LIVE_ADAPTERS, 2, ADAPTER_RANK, MODEL_WIDTH), ADAPTER_RANK ** -0.5, 0.5, ((0, 16), (3, 8)))
    prompt_token_length = uneven(splits[5], PROMPTS, PTOK, LMAX, 1).astype(jnp.int32)
    prompt_of_request = jnp.searchsorted(jnp.cumsum(uneven(splits[6], PROMPTS, REQS, SLOTS, 1)), jnp.arange(REQS), side="right").astype(jnp.int32)
    adapter_of_request = draw_adapter_of_request(jax.random.fold_in(splits[9], 71), 0)
    adapter_slot_index = draw_adapter_slot_index(jax.random.fold_in(splits[9], 71), 0)
    return dict(prompt_token_states=prompt_token_states, gain=gain, projection_weight=projection_weight, adapter_down_maps=adapter_down_maps, adapter_up_maps=adapter_up_maps, prompt_token_length=prompt_token_length, prompt_of_request=prompt_of_request, adapter_of_request=adapter_of_request, adapter_slot_index=adapter_slot_index)


def request_table(prompt_of_request, adapter_of_request, adapter_slot_index, prompts, slots, loaded_adapters):
    n_req = prompt_of_request.shape[0]
    before = lax.optimization_barrier(jnp.sum((prompt_of_request[None, :] < prompt_of_request[:, None]).astype(jnp.int32), axis=1))
    position = jnp.arange(n_req, dtype=jnp.int32) - before
    adapter_hot = adapter_of_request[:, None] == jnp.arange(adapter_slot_index.shape[0], dtype=jnp.int32)[None, :]
    slot_index = lax.optimization_barrier(jnp.sum(jnp.where(adapter_hot, adapter_slot_index[None, :], 0), axis=1))
    prompt_hot = (prompt_of_request[:, None] == jnp.arange(prompts, dtype=jnp.int32)[None, :]).astype(jnp.float32)
    place_hot = (position[:, None] == jnp.arange(slots, dtype=jnp.int32)[None, :]).astype(jnp.float32)
    slot_hot = (slot_index[:, None] == jnp.arange(loaded_adapters, dtype=jnp.int32)[None, :]).astype(jnp.float32)
    paired = (place_hot[:, :, None] * slot_hot[:, None, :]).reshape(n_req, slots * loaded_adapters)
    return jnp.dot(prompt_hot.T, paired, precision=lax.Precision.HIGHEST)

def reference(prompt_token_states, gain, projection_weight, adapter_down_maps, adapter_up_maps, prompt_token_length, prompt_of_request, adapter_of_request, adapter_slot_index):
    states = prompt_token_states.astype(jnp.float32)
    scale_rows = lax.rsqrt(lax.optimization_barrier(jnp.mean(states * states, axis=1, keepdims=True)) + 1e-05)
    normalized_states = (states * scale_rows * gain.astype(jnp.float32)[None, :]).astype(jnp.bfloat16)
    base = jnp.dot(normalized_states, projection_weight.reshape(MODEL_WIDTH, 2 * MODEL_WIDTH), preferred_element_type=jnp.float32)
    low_rank_rows = jnp.einsum('bf,lfm->blm', normalized_states.astype(jnp.float32), adapter_down_maps.astype(jnp.float32)).astype(jnp.bfloat16)
    table = request_table(prompt_of_request, adapter_of_request, adapter_slot_index, PROMPTS, SLOTS, LIVE_ADAPTERS)
    ends = jnp.cumsum(prompt_token_length)
    token_index = jnp.arange(PTOK, dtype=jnp.int32)
    prompt_of = lax.optimization_barrier(jnp.sum((token_index[:, None] >= ends[None, :]).astype(jnp.int32), axis=1))
    prompt_hot = (prompt_of[:, None] == jnp.arange(PROMPTS, dtype=jnp.int32)[None, :]).astype(jnp.float32)
    pick = jnp.dot(prompt_hot, table, precision=lax.Precision.HIGHEST).reshape(PTOK, SLOTS, LIVE_ADAPTERS)
    adapter_up_weight = adapter_up_maps.astype(jnp.float32)
    block_rows = PTOK // N_COL

    def one_block(block):
        start = (block * block_rows).astype(jnp.int32)
        rank_block = lax.dynamic_slice_in_dim(low_rank_rows, start, block_rows, 0).astype(jnp.float32)
        rank_block = rank_block.reshape(block_rows, LIVE_ADAPTERS, 2, ADAPTER_RANK)
        delta = jnp.einsum('pqsm,qsmn->pqsn', rank_block, adapter_up_weight).astype(jnp.bfloat16)
        delta = delta.reshape(block_rows, LIVE_ADAPTERS, 2 * MODEL_WIDTH).astype(jnp.float32)
        pick_block = lax.dynamic_slice_in_dim(pick, start, block_rows, 0)
        base_block = lax.dynamic_slice_in_dim(base, start, block_rows, 0)
        live = lax.optimization_barrier(jnp.sum(pick_block, axis=2))
        mixed = live[:, :, None] * base_block[:, None, :] + jnp.einsum('tka,taf->tkf', pick_block, delta)
        return mixed.astype(jnp.bfloat16)
    mixed = lax.map(one_block, jnp.arange(N_COL, dtype=jnp.int32)).reshape(PTOK, SLOTS, 2 * MODEL_WIDTH)
    return (mixed[:, :, :MODEL_WIDTH], mixed[:, :, MODEL_WIDTH:])
```

```python
import functools

import jax
import jax.numpy as jnp
from jax import lax
from jax.experimental import pallas as pl
from jax.experimental.pallas import tpu as pltpu
from jax.sharding import PartitionSpec as P

F32 = jnp.float32
BF16 = jnp.bfloat16
MESH = pl.DeviceIdType.MESH

SLOTS = 16
TOK = 224
HALF = 112
FEAT = 640
BLK = 320
PAD = 384
OUT = 640
RANK = 128
GROUPS = 14

X1S, X1R = 0, 0
D1S, D1R = 4, 4
SS = 8
RA = 15
WAP, WBP, WAM, WBM, WRP, WRM = 22, 23, 24, 25, 26, 27
X2P, X2M, X2RP, X2RM = 28, 29, 30, 31
XC = 32
D2P, D2M, D2RP, D2RM = 37, 38, 39, 40
RR_ = 41
PR_ = 44
U1P, U1M, U1RP, U1RM = 47, 48, 49, 50
U0P, U0M, U0RP, U0RM = 51, 52, 53, 54
V1P, V1M, V1R = 55, 59, 63
V0P, V0M, V0R = 67, 71, 75
NSEM = 79
LW, LU, LS, LB = 0, 1, 2, 3


def to_col(row, n):
    same = lax.broadcasted_iota(jnp.int32, (n, n), 0) == lax.broadcasted_iota(jnp.int32, (n, n), 1)
    return jnp.sum(jnp.where(same, jnp.broadcast_to(row, (n, n)), 0.0), axis=1, keepdims=True)


def iota(shape, axis):
    return lax.broadcasted_iota(jnp.int32, shape, axis)


def targets(len_ref, por_ref, aor_ref, asi_ref, first_token):
    lens = len_ref[...].astype(F32)
    por = por_ref[...].astype(F32)
    aor = aor_ref[...].astype(F32)
    asi = asi_ref[...].astype(F32)
    n_prompt = lens.shape[1]
    n_req = por.shape[1]
    n_lib = asi.shape[1]
    before = jnp.sum(
        jnp.where(to_col(por, n_req) < por, 1.0, 0.0), axis=0, keepdims=True
    )
    position = iota((1, n_req), 1).astype(F32) - before
    hot = iota((n_lib, n_req), 0).astype(F32) == aor
    slot = jnp.sum(
        jnp.where(hot, jnp.broadcast_to(to_col(asi, n_lib), (n_lib, n_req)), 0.0),
        axis=0,
        keepdims=True,
    )
    by_prompt = jnp.where(iota((16, n_req), 0).astype(F32) == por, slot + 1.0, 0.0)
    by_place = jnp.where(iota((16, n_req), 0).astype(F32) == position, 1.0, 0.0)
    table = lax.dot_general(
        by_prompt.astype(BF16),
        by_place.astype(BF16),
        (((1,), (1,)), ((), ())),
        preferred_element_type=F32,
    )
    spread = jnp.where(iota((16, 256), 0) == iota((16, 256), 1) % 16, 1.0, 0.0)
    table = jnp.dot(table.astype(BF16), spread.astype(BF16), preferred_element_type=F32)
    ends = jnp.sum(
        jnp.where(
            iota((n_prompt, n_prompt), 0) <= iota((n_prompt, n_prompt), 1),
            jnp.broadcast_to(to_col(lens, n_prompt), (n_prompt, n_prompt)),
            0.0,
        ),
        axis=0,
        keepdims=True,
    )
    in_group = iota((16, 256), 1) // 16
    token = (first_token + 16 * iota((16, 256), 0) + in_group).astype(F32)
    prompt = jnp.zeros((16, 256), F32)
    for p in range(n_prompt):
        prompt += jnp.where(token >= ends[:, p : p + 1], 1.0, 0.0)
    chosen = jnp.zeros((16, 256), F32)
    for p in range(n_prompt):
        chosen += jnp.where(prompt == float(p), jnp.broadcast_to(table[p : p + 1, :], (16, 256)), 0.0)
    return jnp.where(chosen > 0.5, (chosen - 1.0) * 16.0 + in_group.astype(F32), -1.0)


def exchange(
    x_ref, gain_ref, w_ref, d_ref, up_ref, len_ref, por_ref, aor_ref, asi_ref,
    up_all, rank_all, base_out, pick_out,
    xg, xb, wb, db, pb, pr, pown, rb, rr, rown, rfin, ss_own, ss_all, bfin, pick,
    ssem, rsem, lsem,
):
    r = lax.axis_index("row")
    c = lax.axis_index("col")
    y, core = lax.div(r, 2), lax.rem(r, 2)
    x, z = lax.div(c, 4), lax.rem(c, 4)

    def dev(x_, y_, z_, core_):
        return (y_ * 2 + core_, x_ * 4 + z_)

    def mod4(v):
        return lax.rem(v + 8, 4)

    def rc(src, dst, i, to, j=None):
        return pltpu.make_async_remote_copy(
            src_ref=src,
            dst_ref=dst,
            send_sem=ssem.at[i],
            recv_sem=rsem.at[i if j is None else j],
            device_id=to,
            device_id_type=MESH,
        )

    xp, xm = mod4(x + 1), mod4(x - 1)
    yp, ym = mod4(y + 1), mod4(y - 1)
    zp, zm = mod4(z + 1), mod4(z - 1)
    x2, y2 = mod4(x + 2), mod4(y + 2)
    to_xp, to_xm = dev(xp, y, z, core), dev(xm, y, z, core)
    to_yp, to_ym = dev(x, yp, z, core), dev(x, ym, z, core)
    to_zp, to_zm = dev(x, y, zp, core), dev(x, y, zm, core)
    to_other = dev(x, y, z, 1 - core)
    sends = []

    def go(cp):
        cp.start()
        sends.append(cp)
        return cp

    barrier = pltpu.get_barrier_semaphore()

    def greet(i, carry):
        k = lax.rem(y * 8 + z * 2 + core + i, 32)
        pl.semaphore_signal(
            barrier,
            inc=1,
            device_id=dev(x, lax.div(k, 8), lax.rem(lax.div(k, 2), 4), lax.rem(k, 2)),
            device_id_type=MESH,
        )
        return carry

    lax.fori_loop(1, 32, greet, 0)
    pl.semaphore_signal(barrier, inc=1, device_id=to_xp, device_id_type=MESH)
    pl.semaphore_signal(barrier, inc=1, device_id=to_xm, device_id_type=MESH)

    states = x_ref[...].astype(F32)
    xg[...] = (states * gain_ref[...].astype(F32)).astype(BF16)
    ss_own[...] = lax.dot_general(
        jnp.ones((8, FEAT), F32),
        states * states,
        (((1,), (1,)), ((), ())),
        precision=lax.Precision.HIGHEST,
        preferred_element_type=F32,
    )
    odd = lax.rem(z, 2)
    off = pl.multiple_of(64 * odd, 64)
    pad_at = pl.multiple_of(BLK * (1 - odd), 64)
    for b in range(4):
        for j in range(2):
            wb[j, b, pl.ds(pad_at, 64), :] = jnp.zeros((64, OUT), BF16)
        db[b, pl.ds(pad_at, 64), :] = jnp.zeros((64, 512), BF16)

    pl.semaphore_wait(barrier, 33)

    def u1(xo, a, n):
        return up_all.at[xo, z, 1, pl.ds(a, n), :]

    def u0(zo, a, n):
        return up_all.at[x, zo, 0, pl.ds(a, n), :]

    c_u1p = go(rc(up_ref.at[1], u1(x, 0, 128), U1P, to_xp))
    c_u1m = go(rc(up_ref.at[1], u1(x, 0, 128), U1M, to_xm))

    def wslot(xo, a):
        return wb.at[:, xo, pl.ds(pl.multiple_of(off + a, 32), 160), :]

    c_wap = go(rc(w_ref.at[:, pl.ds(0, 160), :], wslot(x, 0), WAP, to_xp))
    c_wbm = go(rc(w_ref.at[:, pl.ds(160, 160), :], wslot(x, 160), WBM, to_xm))
    c_wbp = go(rc(w_ref.at[:, pl.ds(160, 160), :], wslot(x, 160), WBP, to_xp))
    c_wam = go(rc(w_ref.at[:, pl.ds(0, 160), :], wslot(x, 0), WAM, to_xm))

    some = []
    for h in range(2):
        for k in range(2):
            zd = 2 * core + h
            src = xg.at[pl.ds(HALF * k, HALF), pl.ds(256 * h, PAD)]
            dst = xb.at[z, pl.ds(HALF * k, HALF), pl.ds(pl.multiple_of(PAD * y, 128), PAD)]
            own = jnp.logical_and(zd == z, core == k)
            cp = rc(src, dst, X1S + 2 * h + k, dev(x, y, zd, k), X1R + z)
            some.append((own, cp))

            @pl.when(jnp.logical_not(own))
            def _():
                cp.start()

            @pl.when(own)
            def _():
                pltpu.make_async_copy(src, dst, rsem.at[X1R + z]).start()

    for h in range(2):
        for k in range(2):
            zd = 2 * core + h
            src = d_ref.at[pl.ds(BLK * h, BLK), pl.ds(RANK * k, RANK)]
            dst = db.at[y, pl.ds(64 * h, BLK), pl.ds(pl.multiple_of(RANK * x, 128), RANK)]
            own = jnp.logical_and(jnp.logical_and(zd == z, core == k), y == z)
            cp = rc(src, dst, D1S + 2 * h + k, dev(x, z, zd, k), D1R + y)
            some.append((own, cp))

            @pl.when(jnp.logical_not(own))
            def _():
                cp.start()

            @pl.when(own)
            def _():
                pltpu.make_async_copy(src, dst, rsem.at[D1R + y]).start()

    c_ss = []
    for i in range(1, 8):
        rd = lax.rem(r + i, 8)
        c_ss.append(go(rc(ss_own, ss_all.at[i - 1], SS + i - 1, (rd, c))))

    c_u0p = go(rc(up_ref.at[0], u0(z, 0, 128), U0P, to_zp))
    c_u0m = go(rc(up_ref.at[0], u0(z, 0, 128), U0M, to_zm))

    def v1(xo, zo):
        return up_all.at[xo, zo, 1]

    def v0(xo, zo):
        return up_all.at[xo, zo, 0]

    c_v1 = {}
    c_v0 = {}

    def send_v1(k, src):
        xo = mod4(x + k)
        c_v1[k] = (
            go(rc(src, v1(xo, z), V1P + k, to_zp)),
            go(rc(src, v1(xo, z), V1M + k, to_zm)),
        )

    def relay_v1(k):
        xo = mod4(x + k)
        if k < 2:
            c_v1[k][0].wait_recv()
            cp = go(rc(v1(xo, zm), v1(xo, zm), V1R + k, to_zp))
        else:
            c_v1[k][1].wait_recv()
            cp = go(rc(v1(xo, zp), v1(xo, zp), V1R + k, to_zm))
        c_v1[k] = c_v1[k] + (cp,)

    def send_v0(k, src):
        zo = mod4(z + k)
        c_v0[k] = (
            go(rc(src, v0(x, zo), V0P + k, to_xp)),
            go(rc(src, v0(x, zo), V0M + k, to_xm)),
        )

    def relay_v0(k):
        zo = mod4(z + k)
        if k < 2:
            c_v0[k][0].wait_recv()
            cp = go(rc(v0(xm, zo), v0(xm, zo), V0R + k, to_xp))
        else:
            c_v0[k][1].wait_recv()
            cp = go(rc(v0(xp, zo), v0(xp, zo), V0R + k, to_xm))
        c_v0[k] = c_v0[k] + (cp,)

    def finish(cs, k):
        if k < 2:
            cs[k][1].wait_recv()
        else:
            cs[k][0].wait_recv()
        cs[k][2].wait_recv()

    send_v1(0, up_ref.at[1])

    l_w = pltpu.make_async_copy(w_ref, wb.at[:, x, pl.ds(off, BLK), :], lsem.at[LW])
    l_w.start()
    l_u = pltpu.make_async_copy(up_ref, up_all.at[x, z], lsem.at[LU])
    l_u.start()

    def unit(yo, a, n):
        return xb.at[
            pl.ds(a, n),
            pl.ds(pl.multiple_of(HALF * core, 16), HALF),
            pl.ds(pl.multiple_of(PAD * yo, 128), PAD),
        ]

    for zs in range(4):
        piece = xb.at[
            zs,
            pl.ds(pl.multiple_of(HALF * core, 16), HALF),
            pl.ds(pl.multiple_of(PAD * y, 128), PAD),
        ]
        rc(piece, piece, X1S, to_other, X1R + zs).wait_recv()
    c_x2p = go(rc(unit(y, 0, 4), unit(y, 0, 4), X2P, to_yp))
    c_x2m = go(rc(unit(y, 0, 4), unit(y, 0, 4), X2M, to_ym))
    c_xc = [go(rc(unit(y, 0, 4), unit(y, 0, 4), XC, to_other))]

    tgt = targets(len_ref, por_ref, aor_ref, asi_ref, c * TOK)
    for g in range(GROUPS):
        hit = jnp.where(
            iota((256, 256), 0).astype(F32) == tgt[g : g + 1, :], 1.0, 0.0
        )
        pick[g] = hit.T.astype(BF16)

    c_u1p.wait_recv()
    c_u1m.wait_recv()
    c_u1rp = go(rc(u1(xm, 0, 64), u1(xm, 0, 64), U1RP, to_xp))
    c_u1rm = go(rc(u1(xp, 64, 64), u1(xp, 64, 64), U1RM, to_xm))
    send_v1(1, v1(xp, z))
    send_v1(3, v1(xm, z))
    c_u0p.wait_recv()
    c_u0m.wait_recv()
    c_u0rp = go(rc(u0(zm, 0, 64), u0(zm, 0, 64), U0RP, to_zp))
    c_u0rm = go(rc(u0(zp, 64, 64), u0(zp, 64, 64), U0RM, to_zm))
    l_pick = pltpu.make_async_copy(pick, pick_out, lsem.at[LS])
    l_pick.start()

    c_x2p.wait_recv()
    c_x2rp = go(rc(unit(ym, 0, 2), unit(ym, 0, 2), X2RP, to_yp))
    c_xc.append(go(rc(unit(ym, 0, 4), unit(ym, 0, 4), XC + 1, to_other)))
    c_x2m.wait_recv()
    c_x2rm = go(rc(unit(yp, 2, 2), unit(yp, 2, 2), X2RM, to_ym))
    c_xc.append(go(rc(unit(yp, 0, 4), unit(yp, 0, 4), XC + 2, to_other)))

    c_wap.wait_recv()
    c_wrp = go(rc(wslot(xm, 0), wslot(xm, 0), WRP, to_xp))
    c_wbm.wait_recv()
    c_wrm = go(rc(wslot(xp, 160), wslot(xp, 160), WRM, to_xm))

    def dpart(xo, a, n):
        return db.at[pl.ds(a, n), pl.ds(off, BLK), pl.ds(pl.multiple_of(RANK * xo, 128), RANK)]

    for ys in range(4):
        piece = db.at[ys, pl.ds(off, BLK), pl.ds(pl.multiple_of(RANK * x, 128), RANK)]
        rc(piece, piece, D1S, to_other, D1R + ys).wait_recv()
    c_d2p = go(rc(dpart(x, 0, 4), dpart(x, 0, 4), D2P, to_xp))
    c_d2m = go(rc(dpart(x, 0, 4), dpart(x, 0, 4), D2M, to_xm))

    relay_v1(0)
    c_x2rp.wait_recv()
    c_xc.append(go(rc(unit(y2, 0, 2), unit(y2, 0, 2), XC + 3, to_other)))
    c_x2rm.wait_recv()
    c_xc.append(go(rc(unit(y2, 2, 2), unit(y2, 2, 2), XC + 4, to_other)))
    c_u0rp.wait_recv()
    c_u0rm.wait_recv()
    c_u1rp.wait_recv()
    c_u1rm.wait_recv()
    send_v1(2, v1(x2, z))
    relay_v1(1)
    relay_v1(3)

    c_d2p.wait_recv()
    c_d2rp = go(rc(dpart(xm, 0, 2), dpart(xm, 0, 2), D2RP, to_xp))
    c_d2m.wait_recv()
    c_d2rm = go(rc(dpart(xp, 2, 2), dpart(xp, 2, 2), D2RM, to_xm))
    send_v0(0, up_ref.at[0])
    send_v0(1, v0(x, zp))
    send_v0(3, v0(x, zm))
    send_v0(2, v0(x, mod4(z + 2)))

    for cp in c_xc:
        cp.wait_recv()
    l_w.wait()
    c_wbp.wait_recv()
    c_wam.wait_recv()
    c_wrp.wait_recv()
    c_wrm.wait_recv()

    c_pr = []
    for k in (2, 1, 3):
        rows = xb[mod4(z + k)]
        for j in range(2):
            pb[k - 1, j] = jnp.dot(
                rows, wb[j].reshape(4 * PAD, OUT), preferred_element_type=F32
            ).astype(BF16)
        c_pr.append(go(rc(pb.at[k - 1], pr.at[k - 1], PR_ + k - 1, dev(x, y, mod4(z + k), core))))

    c_d2rp.wait_recv()
    c_d2rm.wait_recv()
    c_rr = []
    for k in (2, 1, 3):
        rb[k - 1] = jnp.dot(
            xb[mod4(z + k)], db[...].reshape(4 * PAD, 512), preferred_element_type=F32
        ).astype(BF16)
        c_rr.append(go(rc(rb.at[k - 1], rr.at[k - 1], RR_ + k - 1, dev(x, y, mod4(z + k), core))))
    relay_v1(2)
    relay_v0(0)
    relay_v0(1)
    relay_v0(3)
    relay_v0(2)
    rown[...] = jnp.dot(xb[z], db[...].reshape(4 * PAD, 512), preferred_element_type=F32)
    for j in range(2):
        pown[j] = jnp.dot(xb[z], wb[j].reshape(4 * PAD, OUT), preferred_element_type=F32)

    total = ss_own[...]
    for i in range(7):
        c_ss[i].wait_recv()
        total += ss_all[i]
    width = FEAT * 8
    scale = to_col(lax.rsqrt(total[0:1, :] / width + 1e-05), TOK)

    for cp in c_rr:
        cp.wait_recv()
    rfin[...] = (
        (rown[...] + rr[0].astype(F32) + rr[1].astype(F32) + rr[2].astype(F32)) * scale
    ).astype(BF16)
    c_ra = []
    for i in range(1, 8):
        rd = lax.rem(r + i, 8)
        c_ra.append(go(rc(rfin, rank_all.at[y, core], RA + i - 1, (rd, c))))
    l_b0 = pltpu.make_async_copy(rfin, rank_all.at[y, core], lsem.at[LB])
    l_b0.start()

    for cp in c_pr:
        cp.wait_recv()
    for j in range(2):
        bfin[j] = (
            pown[j] + pr[0, j].astype(F32) + pr[1, j].astype(F32) + pr[2, j].astype(F32)
        ) * scale
    l_b0.wait()
    l_b1 = pltpu.make_async_copy(bfin, base_out, lsem.at[LB])
    l_b1.start()

    for k in range(4):
        finish(c_v1, k)
        finish(c_v0, k)
    for cp in c_ra:
        cp.wait_recv()
    l_b1.wait()
    l_u.wait()
    l_pick.wait()
    for own, cp in some:

        @pl.when(jnp.logical_not(own))
        def _():
            cp.wait_send()

    for cp in sends:
        cp.wait_send()


def combine(
    up_hbm, rank_hbm, base_hbm, pick_hbm, q_out, v_out,
    up, rank, base, pick, mix, obuf, isem, osem,
):
    loads = []
    for n, (src, dst) in enumerate(
        [
            (rank_hbm.at[:, 0], rank.at[:, 0]),
            (base_hbm.at[0], base.at[0]),
        ]
        + [(up_hbm.at[i, :, 0], up.at[i, :, 0]) for i in range(4)]
        + [
            (pick_hbm, pick),
            (rank_hbm.at[:, 1], rank.at[:, 1]),
            (base_hbm.at[1], base.at[1]),
        ]
        + [(up_hbm.at[i, :, 1], up.at[i, :, 1]) for i in range(4)]
    ):
        cp = pltpu.make_async_copy(src, dst, isem.at[n])
        cp.start()
        loads.append(cp)

    outs = (q_out, v_out)
    for j in range(2):
        loads[7 * j].wait()
        loads[7 * j + 1].wait()
        for xo in range(4):
            loads[7 * j + 2 + xo].wait()
            for zo in range(4):
                a = 4 * xo + zo
                delta = jnp.dot(
                    rank[zo, j, :, RANK * xo : RANK * (xo + 1)],
                    up[xo, zo, j],
                    preferred_element_type=F32,
                )
                full = (base[j] + delta).astype(BF16)
                mix[:, 16 * a : 16 * (a + 1), :] = full.reshape(GROUPS, 16, OUT)
        if j == 0:
            loads[6].wait()

        def group(g, carry):
            slot = lax.rem(g, 2)
            rows = jnp.dot(pick[g], mix[g], preferred_element_type=F32).astype(BF16)

            @pl.when(g >= 2)
            def _():
                pltpu.make_async_copy(
                    obuf.at[slot], outs[j].at[pl.ds(16 * (g - 2), 16)], osem.at[slot]
                ).wait()

            obuf[slot] = rows.reshape(16, SLOTS, OUT)
            pltpu.make_async_copy(
                obuf.at[slot], outs[j].at[pl.ds(16 * g, 16)], osem.at[slot]
            ).start()
            return carry

        lax.fori_loop(0, GROUPS, group, 0)
        for g in (GROUPS - 2, GROUPS - 1):
            pltpu.make_async_copy(
                obuf.at[g % 2], outs[j].at[pl.ds(16 * g, 16)], osem.at[g % 2]
            ).wait()


def body(
    prompt_token_states,
    gain,
    projection_weight,
    adapter_down_maps,
    adapter_up_maps,
    prompt_token_length,
    prompt_of_request,
    adapter_of_request,
    adapter_slot_index,
):
    weight = jnp.transpose(projection_weight, (1, 0, 2))
    vmem = pl.BlockSpec(memory_space=pltpu.VMEM)
    anyw = pl.BlockSpec(memory_space=pl.ANY)
    up_all, rank_all, base, pick = pl.pallas_call(
        exchange,
        out_shape=(
            jax.ShapeDtypeStruct((4, 4, 2, RANK, OUT), BF16),
            jax.ShapeDtypeStruct((4, 2, TOK, 512), BF16),
            jax.ShapeDtypeStruct((2, TOK, OUT), F32),
            jax.ShapeDtypeStruct((GROUPS, 256, 256), BF16),
        ),
        in_specs=[vmem, vmem, anyw, anyw, anyw, vmem, vmem, vmem, vmem],
        out_specs=(anyw, anyw, anyw, anyw),
        scratch_shapes=[
            pltpu.VMEM((TOK, FEAT), BF16),
            pltpu.VMEM((4, TOK, 4 * PAD), BF16),
            pltpu.VMEM((2, 4, PAD, OUT), BF16),
            pltpu.VMEM((4, PAD, 512), BF16),
            pltpu.VMEM((3, 2, TOK, OUT), BF16),
            pltpu.VMEM((3, 2, TOK, OUT), BF16),
            pltpu.VMEM((2, TOK, OUT), F32),
            pltpu.VMEM((3, TOK, 512), BF16),
            pltpu.VMEM((3, TOK, 512), BF16),
            pltpu.VMEM((TOK, 512), F32),
            pltpu.VMEM((TOK, 512), BF16),
            pltpu.VMEM((8, TOK), F32),
            pltpu.VMEM((7, 8, TOK), F32),
            pltpu.VMEM((2, TOK, OUT), F32),
            pltpu.VMEM((GROUPS, 256, 256), BF16),
            pltpu.SemaphoreType.DMA((NSEM,)),
            pltpu.SemaphoreType.DMA((NSEM,)),
            pltpu.SemaphoreType.DMA((4,)),
        ],
        compiler_params=pltpu.CompilerParams(
            collective_id=0, has_side_effects=True, vmem_limit_bytes=48 << 20
        ),
        name="exchange",
    )(
        prompt_token_states,
        gain.reshape(1, FEAT),
        weight,
        adapter_down_maps.reshape(FEAT, 2 * RANK),
        adapter_up_maps.reshape(2, RANK, OUT),
        prompt_token_length.reshape(1, -1),
        prompt_of_request.reshape(1, -1),
        adapter_of_request.reshape(1, -1),
        adapter_slot_index.reshape(1, -1),
    )
    return pl.pallas_call(
        combine,
        out_shape=(
            jax.ShapeDtypeStruct((TOK, SLOTS, OUT), BF16),
            jax.ShapeDtypeStruct((TOK, SLOTS, OUT), BF16),
        ),
        in_specs=[anyw] * 4,
        out_specs=(anyw, anyw),
        scratch_shapes=[
            pltpu.VMEM((4, 4, 2, RANK, OUT), BF16),
            pltpu.VMEM((4, 2, TOK, 512), BF16),
            pltpu.VMEM((2, TOK, OUT), F32),
            pltpu.VMEM((GROUPS, 256, 256), BF16),
            pltpu.VMEM((GROUPS, 256, OUT), BF16),
            pltpu.VMEM((2, 16, SLOTS, OUT), BF16),
            pltpu.SemaphoreType.DMA((13,)),
            pltpu.SemaphoreType.DMA((2,)),
        ],
        compiler_params=pltpu.CompilerParams(vmem_limit_bytes=48 << 20),
        name="combine",
    )(up_all, rank_all, base, pick)


def solution(mesh):
    placed = (
        P("col", "row"),
        P("row"),
        P("col", None, "row"),
        P("col", "row", None),
        P("col", None, None, "row"),
        P(),
        P(),
        P(),
        P(),
    )
    return jax.shard_map(
        body,
        mesh=mesh,
        in_specs=placed,
        out_specs=(P("col", None, "row"), P("col", None, "row")),
        check_vma=False,
    )
```

```python
import functools

import jax
import jax.numpy as jnp
from jax import lax
from jax.experimental import pallas as pl
from jax.experimental.pallas import tpu as pltpu
from jax.sharding import PartitionSpec as P

F32 = jnp.float32
BF16 = jnp.bfloat16
MESH = pl.DeviceIdType.MESH

SLOTS = 16
TOK = 224
HALF = 112
FEAT = 640
BLK = 320
PAD = 384
OUT = 640
RANK = 128
GROUPS = 14

NAMES = (
    ["x1_%d" % i for i in range(4)]
    + ["d1_%d" % i for i in range(4)]
    + ["ss_%d" % i for i in range(7)]
    + ["w%d_%s" % (j, s) for j in range(2) for s in ("ap", "bp", "am", "bm", "rp", "rm")]
    + ["x2_%s" % s for s in ("p", "m", "rp", "rm")]
    + ["xc_%d" % i for i in range(5)]
    + ["d2_%s" % s for s in ("p", "m", "rp", "rm")]
    + ["u%d_%s" % (j, s) for j in range(2) for s in ("p", "m", "rp", "rm")]
    + ["v%d_%d_%s" % (j, k, s) for j in range(2) for k in range(4) for s in ("p", "m", "r")]
    + ["s%d_%s" % (j, s) for j in range(3) for s in ("fp", "fm", "np", "nm", "ap", "am")]
    + ["ra_%s" % s for s in ("p", "m", "rp", "rm", "c0", "c1", "c2", "c3", "c4")]
)
SEM = {name: i for i, name in enumerate(NAMES)}
NSEM = len(NAMES)


def to_col(row, n):
    same = lax.broadcasted_iota(jnp.int32, (n, n), 0) == lax.broadcasted_iota(jnp.int32, (n, n), 1)
    return jnp.sum(jnp.where(same, jnp.broadcast_to(row, (n, n)), 0.0), axis=1, keepdims=True)


def iota(shape, axis):
    return lax.broadcasted_iota(jnp.int32, shape, axis)


def targets(len_ref, por_ref, aor_ref, asi_ref, first_token):
    lens = len_ref[...].astype(F32)
    por = por_ref[...].astype(F32)
    aor = aor_ref[...].astype(F32)
    asi = asi_ref[...].astype(F32)
    n_prompt = lens.shape[1]
    n_req = por.shape[1]
    n_lib = asi.shape[1]
    before = jnp.sum(
        jnp.where(to_col(por, n_req) < por, 1.0, 0.0), axis=0, keepdims=True
    )
    position = iota((1, n_req), 1).astype(F32) - before
    hot = iota((n_lib, n_req), 0).astype(F32) == aor
    slot = jnp.sum(
        jnp.where(hot, jnp.broadcast_to(to_col(asi, n_lib), (n_lib, n_req)), 0.0),
        axis=0,
        keepdims=True,
    )
    by_prompt = jnp.where(iota((16, n_req), 0).astype(F32) == por, slot + 1.0, 0.0)
    by_place = jnp.where(iota((16, n_req), 0).astype(F32) == position, 1.0, 0.0)
    table = lax.dot_general(
        by_prompt.astype(BF16),
        by_place.astype(BF16),
        (((1,), (1,)), ((), ())),
        preferred_element_type=F32,
    )
    spread = jnp.where(iota((16, 256), 0) == iota((16, 256), 1) % 16, 1.0, 0.0)
    table = jnp.dot(table.astype(BF16), spread.astype(BF16), preferred_element_type=F32)
    ends = jnp.sum(
        jnp.where(
            iota((n_prompt, n_prompt), 0) <= iota((n_prompt, n_prompt), 1),
            jnp.broadcast_to(to_col(lens, n_prompt), (n_prompt, n_prompt)),
            0.0,
        ),
        axis=0,
        keepdims=True,
    )
    in_group = iota((16, 256), 1) // 16
    token = (first_token + 16 * iota((16, 256), 0) + in_group).astype(F32)
    prompt = jnp.zeros((16, 256), F32)
    for p in range(n_prompt):
        prompt += jnp.where(token >= ends[:, p : p + 1], 1.0, 0.0)
    chosen = jnp.zeros((16, 256), F32)
    for p in range(n_prompt):
        chosen += jnp.where(prompt == float(p), jnp.broadcast_to(table[p : p + 1, :], (16, 256)), 0.0)
    return jnp.where(chosen > 0.5, (chosen - 1.0) * 16.0 + in_group.astype(F32), -1.0)


def exchange(
    x_hbm, gain_ref, w_ref, d_ref, up_ref, len_hbm, por_hbm, aor_hbm, asi_hbm,
    up_all, rank_all, base_out, pick,
    xv, lenv, porv, aorv, asiv,
    xg, xb, wb, db, bfar, bfirst, blater, bnear, bsum, bfinal, bown,
    rfar, rfirst, rlater, rnear, rsum, rfinal, rown, ss_own, ss_all,
    ssem, rsem, lsem,
):
    r = lax.axis_index("row")
    c = lax.axis_index("col")
    y, core = lax.div(r, 2), lax.rem(r, 2)
    x, z = lax.div(c, 4), lax.rem(c, 4)

    def dev(x_, y_, z_, core_):
        return (y_ * 2 + core_, x_ * 4 + z_)

    def mod4(v):
        return lax.rem(v + 8, 4)

    def rc(src, dst, send, to, recv=None):
        return pltpu.make_async_remote_copy(
            src_ref=src,
            dst_ref=dst,
            send_sem=ssem.at[SEM[send]],
            recv_sem=rsem.at[SEM[send] if recv is None else recv],
            device_id=to,
            device_id_type=MESH,
        )

    xp, xm, x2 = mod4(x + 1), mod4(x - 1), mod4(x + 2)
    yp, ym, y2 = mod4(y + 1), mod4(y - 1), mod4(y + 2)
    zp, zm, z2 = mod4(z + 1), mod4(z - 1), mod4(z + 2)
    to_xp, to_xm = dev(xp, y, z, core), dev(xm, y, z, core)
    to_yp, to_ym = dev(x, yp, z, core), dev(x, ym, z, core)
    to_zp, to_zm = dev(x, y, zp, core), dev(x, y, zm, core)
    to_other = dev(x, y, z, 1 - core)
    copies = {}
    sends = []

    def go(src, dst, name, to):
        cp = rc(src, dst, name, to)
        cp.start()
        copies[name] = cp
        sends.append(cp)

    def got(*names):
        for name in names:
            copies[name].wait_recv()

    barrier = pltpu.get_barrier_semaphore()

    def greet(i, carry):
        k = lax.rem(y * 8 + z * 2 + core + i, 32)
        pl.semaphore_signal(
            barrier,
            inc=1,
            device_id=dev(x, lax.div(k, 8), lax.rem(lax.div(k, 2), 4), lax.rem(k, 2)),
            device_id_type=MESH,
        )
        return carry

    lax.fori_loop(1, 32, greet, 0)
    pl.semaphore_signal(barrier, inc=1, device_id=to_xp, device_id_type=MESH)
    pl.semaphore_signal(barrier, inc=1, device_id=to_xm, device_id_type=MESH)

    l_x = pltpu.make_async_copy(x_hbm, xv, lsem.at[0])
    l_x.start()
    l_small = []
    for i, (a, b) in enumerate(
        ((len_hbm, lenv), (por_hbm, porv), (aor_hbm, aorv), (asi_hbm, asiv))
    ):
        l_small.append(pltpu.make_async_copy(a, b, lsem.at[1 + i]))
        l_small[-1].start()

    odd = lax.rem(z, 2)
    off = pl.multiple_of(64 * odd, 64)
    pad_at = pl.multiple_of(BLK * (1 - odd), 64)
    for b in range(4):
        for j in range(2):
            wb[j, b, pl.ds(pad_at, 64), :] = jnp.zeros((64, OUT), BF16)
        db[b, pl.ds(pad_at, 64), :] = jnp.zeros((64, 512), BF16)

    l_x.wait()
    states = xv[...].astype(F32)
    xg[...] = (states * gain_ref[...].astype(F32)).astype(BF16)
    ss_own[...] = lax.dot_general(
        jnp.ones((8, FEAT), F32),
        states * states,
        (((1,), (1,)), ((), ())),
        precision=lax.Precision.HIGHEST,
        preferred_element_type=F32,
    )
    pl.semaphore_wait(barrier, 33)

    def u1(xo, a, n):
        return up_all.at[xo, z, 1, pl.ds(a, n), :]

    def u0(zo, a, n):
        return up_all.at[x, zo, 0, pl.ds(a, n), :]

    go(up_ref.at[1], u1(x, 0, 128), "u1_p", to_xp)
    go(up_ref.at[1], u1(x, 0, 128), "u1_m", to_xm)

    def wslot(j, xo, a):
        return wb.at[j, xo, pl.ds(pl.multiple_of(off + a, 32), 160), :]

    def weights(j):
        go(w_ref.at[j, pl.ds(0, 160), :], wslot(j, x, 0), "w%d_ap" % j, to_xp)
        go(w_ref.at[j, pl.ds(160, 160), :], wslot(j, x, 160), "w%d_bm" % j, to_xm)
        go(w_ref.at[j, pl.ds(160, 160), :], wslot(j, x, 160), "w%d_bp" % j, to_xp)
        go(w_ref.at[j, pl.ds(0, 160), :], wslot(j, x, 0), "w%d_am" % j, to_xm)

    def relay_weights(j):
        got("w%d_ap" % j)
        go(wslot(j, xm, 0), wslot(j, xm, 0), "w%d_rp" % j, to_xp)
        got("w%d_bm" % j)
        go(wslot(j, xp, 160), wslot(j, xp, 160), "w%d_rm" % j, to_xm)

    weights(0)

    some = []
    for h in range(2):
        for k in range(2):
            zd = 2 * core + h
            src = xg.at[pl.ds(HALF * k, HALF), pl.ds(256 * h, PAD)]
            dst = xb.at[z, pl.ds(HALF * k, HALF), pl.ds(pl.multiple_of(PAD * y, 128), PAD)]
            own = jnp.logical_and(zd == z, core == k)
            sem = SEM["x1_0"] + z
            cp = rc(src, dst, "x1_%d" % (2 * h + k), dev(x, y, zd, k), sem)
            some.append((own, cp))

            @pl.when(jnp.logical_not(own))
            def _():
                cp.start()

            @pl.when(own)
            def _():
                pltpu.make_async_copy(src, dst, rsem.at[sem]).start()

    for h in range(2):
        for k in range(2):
            zd = 2 * core + h
            src = d_ref.at[pl.ds(BLK * h, BLK), pl.ds(RANK * k, RANK)]
            dst = db.at[y, pl.ds(64 * h, BLK), pl.ds(pl.multiple_of(RANK * x, 128), RANK)]
            own = jnp.logical_and(jnp.logical_and(zd == z, core == k), y == z)
            sem = SEM["d1_0"] + y
            cp = rc(src, dst, "d1_%d" % (2 * h + k), dev(x, z, zd, k), sem)
            some.append((own, cp))

            @pl.when(jnp.logical_not(own))
            def _():
                cp.start()

            @pl.when(own)
            def _():
                pltpu.make_async_copy(src, dst, rsem.at[sem]).start()

    for i in range(1, 8):
        go(ss_own, ss_all.at[i - 1], "ss_%d" % (i - 1), (lax.rem(r + i, 8), c))

    go(up_ref.at[0], u0(z, 0, 128), "u0_p", to_zp)
    go(up_ref.at[0], u0(z, 0, 128), "u0_m", to_zm)

    def v1(xo, zo):
        return up_all.at[xo, zo, 1]

    def v0(xo, zo):
        return up_all.at[xo, zo, 0]

    def send_v1(k, src):
        xo = mod4(x + k)
        go(src, v1(xo, z), "v1_%d_p" % k, to_zp)
        go(src, v1(xo, z), "v1_%d_m" % k, to_zm)

    def relay_v1(k):
        xo = mod4(x + k)
        if k < 2:
            got("v1_%d_p" % k)
            go(v1(xo, zm), v1(xo, zm), "v1_%d_r" % k, to_zp)
        else:
            got("v1_%d_m" % k)
            go(v1(xo, zp), v1(xo, zp), "v1_%d_r" % k, to_zm)

    def send_v0(k, src):
        zo = mod4(z + k)
        go(src, v0(x, zo), "v0_%d_p" % k, to_xp)
        go(src, v0(x, zo), "v0_%d_m" % k, to_xm)

    def relay_v0(k):
        zo = mod4(z + k)
        if k < 2:
            got("v0_%d_p" % k)
            go(v0(xm, zo), v0(xm, zo), "v0_%d_r" % k, to_xp)
        else:
            got("v0_%d_m" % k)
            go(v0(xp, zo), v0(xp, zo), "v0_%d_r" % k, to_xm)

    def finish(j, k):
        got("v%d_%d_%s" % (j, k, "m" if k < 2 else "p"), "v%d_%d_r" % (j, k))

    send_v1(0, up_ref.at[1])

    l_w = pltpu.make_async_copy(w_ref, wb.at[:, x, pl.ds(off, BLK), :], lsem.at[5])
    l_w.start()
    l_u = pltpu.make_async_copy(up_ref, up_all.at[x, z], lsem.at[6])
    l_u.start()

    def unit(yo, a, n):
        return xb.at[
            pl.ds(a, n),
            pl.ds(pl.multiple_of(HALF * core, 16), HALF),
            pl.ds(pl.multiple_of(PAD * yo, 128), PAD),
        ]

    for zs in range(4):
        piece = xb.at[
            zs,
            pl.ds(pl.multiple_of(HALF * core, 16), HALF),
            pl.ds(pl.multiple_of(PAD * y, 128), PAD),
        ]
        rc(piece, piece, "x1_0", to_other, SEM["x1_0"] + zs).wait_recv()
    go(unit(y, 0, 4), unit(y, 0, 4), "x2_p", to_yp)
    go(unit(y, 0, 4), unit(y, 0, 4), "x2_m", to_ym)
    go(unit(y, 0, 4), unit(y, 0, 4), "xc_0", to_other)

    got("u1_p", "u1_m")
    send_v1(1, v1(xp, z))
    send_v1(3, v1(xm, z))
    got("u0_p", "u0_m")
    go(u0(zm, 0, 64), u0(zm, 0, 64), "u0_rp", to_zp)
    go(u0(zp, 64, 64), u0(zp, 64, 64), "u0_rm", to_zm)

    for cp in l_small:
        cp.wait()
    tgt = targets(lenv, porv, aorv, asiv, c * TOK)

    def picks(g):
        hit = jnp.where(
            iota((256, 256), 0).astype(F32) == tgt[g : g + 1, :], 1.0, 0.0
        )
        pick[g] = hit.T.astype(BF16)

    relay_weights(0)

    def dpart(xo, a, n):
        return db.at[pl.ds(a, n), pl.ds(off, BLK), pl.ds(pl.multiple_of(RANK * xo, 128), RANK)]

    for ys in range(4):
        piece = db.at[ys, pl.ds(off, BLK), pl.ds(pl.multiple_of(RANK * x, 128), RANK)]
        rc(piece, piece, "d1_0", to_other, SEM["d1_0"] + ys).wait_recv()
    go(dpart(x, 0, 4), dpart(x, 0, 4), "d2_p", to_xp)
    go(dpart(x, 0, 4), dpart(x, 0, 4), "d2_m", to_xm)
    go(u1(xm, 0, 64), u1(xm, 0, 64), "u1_rp", to_xp)
    go(u1(xp, 64, 64), u1(xp, 64, 64), "u1_rm", to_xm)

    got("x2_p")
    go(unit(ym, 0, 2), unit(ym, 0, 2), "x2_rp", to_yp)
    go(unit(ym, 0, 4), unit(ym, 0, 4), "xc_1", to_other)
    got("x2_m")
    go(unit(yp, 2, 2), unit(yp, 2, 2), "x2_rm", to_ym)
    go(unit(yp, 0, 4), unit(yp, 0, 4), "xc_2", to_other)
    relay_v1(0)
    for g in range(GROUPS // 2):
        picks(g)
    got("x2_rp")
    go(unit(y2, 0, 2), unit(y2, 0, 2), "xc_3", to_other)
    got("x2_rm")
    go(unit(y2, 2, 2), unit(y2, 2, 2), "xc_4", to_other)
    relay_v1(1)
    relay_v1(3)
    for i in range(5):
        got("xc_%d" % i)
    l_w.wait()

    up_rows, low_rows = pl.ds(0, HALF), pl.ds(HALF, HALF)

    def partials(s, product, far, first, later, near, final):
        far[...] = product(z2).astype(BF16)
        go(far.at[up_rows], first.at[0], "s%d_fp" % s, to_zp)
        go(far.at[low_rows], first.at[1], "s%d_fm" % s, to_zm)
        part = product(zp)
        near[0] = part[HALF:].astype(BF16)
        later[0] = part[:HALF]
        go(near.at[0], final.at[0, low_rows], "s%d_np" % s, to_zp)
        part = product(zm)
        near[1] = part[:HALF].astype(BF16)
        later[1] = part[HALF:]
        go(near.at[1], final.at[1, up_rows], "s%d_nm" % s, to_zm)

    def pass_on(s, first, later, total, final):
        got("s%d_fp" % s)
        total[0] = (later[0] + first[0].astype(F32)).astype(BF16)
        go(total.at[0], final.at[0, up_rows], "s%d_ap" % s, to_zp)
        got("s%d_fm" % s)
        total[1] = (later[1] + first[1].astype(F32)).astype(BF16)
        go(total.at[1], final.at[1, low_rows], "s%d_am" % s, to_zm)

    def arrived(s):
        got("s%d_np" % s, "s%d_nm" % s, "s%d_ap" % s, "s%d_am" % s)

    def base_part(j):
        def product(block):
            return jnp.dot(
                xb[block], wb[j].reshape(4 * PAD, OUT), preferred_element_type=F32
            )

        partials(j, product, bfar.at[j], bfirst.at[j], blater.at[j], bnear.at[j], bfinal.at[j])
        bown[j] = product(z)

    def base_pass(j):
        pass_on(j, bfirst.at[j], blater.at[j], bsum.at[j], bfinal.at[j])

    def base_done(j):
        arrived(j)
        base_out[j] = (
            bown[j] + bfinal[j, 0].astype(F32) + bfinal[j, 1].astype(F32)
        ) * scale

    got("w0_bp", "w0_am", "w0_rp", "w0_rm")
    base_part(0)

    got("d2_p")
    go(dpart(xm, 0, 2), dpart(xm, 0, 2), "d2_rp", to_xp)
    got("d2_m")
    go(dpart(xp, 2, 2), dpart(xp, 2, 2), "d2_rm", to_xm)
    weights(1)
    got("u0_rp", "u0_rm", "u1_rp", "u1_rm")
    send_v1(2, v1(x2, z))
    base_pass(0)

    def rank_product(block):
        return jnp.dot(xb[block], db[...].reshape(4 * PAD, 512), preferred_element_type=F32)

    got("d2_rp", "d2_rm")
    partials(2, rank_product, rfar, rfirst, rlater, rnear, rfinal)
    rown[...] = rank_product(z)
    relay_weights(1)
    for k in (0, 1, 3, 2):
        send_v0(k, up_ref.at[0] if k == 0 else v0(x, mod4(z + k)))
    pass_on(2, rfirst, rlater, rsum, rfinal)

    total = ss_own[...]
    for i in range(7):
        got("ss_%d" % i)
        total += ss_all[i]
    scale = to_col(lax.rsqrt(total[0:1, :] / (FEAT * 8) + 1e-05), TOK)
    for g in range(GROUPS // 2, GROUPS):
        picks(g)
    base_done(0)
    relay_v1(2)

    def ranks(yo, a, n):
        return rank_all.at[yo, core, pl.ds(a, n)]

    arrived(2)
    rank_all[y, core] = (
        (rown[...] + rfinal[0].astype(F32) + rfinal[1].astype(F32)) * scale
    ).astype(BF16)
    go(ranks(y, 0, TOK), ranks(y, 0, TOK), "ra_p", to_yp)
    go(ranks(y, 0, TOK), ranks(y, 0, TOK), "ra_m", to_ym)
    go(ranks(y, 0, TOK), ranks(y, 0, TOK), "ra_c0", to_other)

    got("w1_bp", "w1_am", "w1_rp", "w1_rm")
    base_part(1)

    got("ra_p")
    go(ranks(ym, 0, HALF), ranks(ym, 0, HALF), "ra_rp", to_yp)
    go(ranks(ym, 0, TOK), ranks(ym, 0, TOK), "ra_c1", to_other)
    got("ra_m")
    go(ranks(yp, HALF, HALF), ranks(yp, HALF, HALF), "ra_rm", to_ym)
    go(ranks(yp, 0, TOK), ranks(yp, 0, TOK), "ra_c2", to_other)
    base_pass(1)
    relay_v0(0)
    relay_v0(1)
    relay_v0(3)
    got("ra_rp")
    go(ranks(y2, 0, HALF), ranks(y2, 0, HALF), "ra_c3", to_other)
    got("ra_rm")
    go(ranks(y2, HALF, HALF), ranks(y2, HALF, HALF), "ra_c4", to_other)
    relay_v0(2)
    base_done(1)

    for k in range(4):
        finish(1, k)
        finish(0, k)
    for i in range(5):
        got("ra_c%d" % i)
    l_u.wait()
    for own, cp in some:

        @pl.when(jnp.logical_not(own))
        def _():
            cp.wait_send()

    for cp in sends:
        cp.wait_send()


def combine(up, rank, base, pick, q_out, v_out, mix, obuf, osem):
    outs = (q_out, v_out)
    for j in range(2):
        for a in range(16):
            xo, zo = a // 4, a % 4
            delta = jnp.dot(
                rank[zo, j, :, RANK * xo : RANK * (xo + 1)],
                up[xo, zo, j],
                preferred_element_type=F32,
            )
            full = (base[j] + delta).astype(BF16)
            mix[:, 16 * a : 16 * (a + 1), :] = full.reshape(GROUPS, 16, OUT)

        def group(g, carry):
            slot = lax.rem(g, 2)
            rows = jnp.dot(pick[g], mix[g], preferred_element_type=F32).astype(BF16)

            @pl.when(g >= 2)
            def _():
                pltpu.make_async_copy(
                    obuf.at[slot], outs[j].at[pl.ds(16 * (g - 2), 16)], osem.at[slot]
                ).wait()

            obuf[slot] = rows.reshape(16, SLOTS, OUT)
            pltpu.make_async_copy(
                obuf.at[slot], outs[j].at[pl.ds(16 * g, 16)], osem.at[slot]
            ).start()
            return carry

        lax.fori_loop(0, GROUPS, group, 0)
        for g in (GROUPS - 2, GROUPS - 1):
            pltpu.make_async_copy(
                obuf.at[g % 2], outs[j].at[pl.ds(16 * g, 16)], osem.at[g % 2]
            ).wait()


def stay(array):
    return pltpu.with_memory_space_constraint(array, pltpu.HBM)


def body(
    prompt_token_states,
    gain,
    projection_weight,
    adapter_down_maps,
    adapter_up_maps,
    prompt_token_length,
    prompt_of_request,
    adapter_of_request,
    adapter_slot_index,
):
    weight = jnp.transpose(projection_weight, (1, 0, 2))
    vmem = pl.BlockSpec(memory_space=pltpu.VMEM)
    hbm = pl.BlockSpec(memory_space=pltpu.HBM)
    anyw = pl.BlockSpec(memory_space=pl.ANY)
    lens = prompt_token_length.reshape(1, -1)
    por = prompt_of_request.reshape(1, -1)
    aor = adapter_of_request.reshape(1, -1)
    asi = adapter_slot_index.reshape(1, -1)
    gathered = pl.pallas_call(
        exchange,
        out_shape=(
            jax.ShapeDtypeStruct((4, 4, 2, RANK, OUT), BF16),
            jax.ShapeDtypeStruct((4, 2, TOK, 512), BF16),
            jax.ShapeDtypeStruct((2, TOK, OUT), F32),
            jax.ShapeDtypeStruct((GROUPS, 256, 256), BF16),
        ),
        in_specs=[hbm, vmem, anyw, hbm, hbm, hbm, hbm, hbm, hbm],
        out_specs=(vmem, vmem, vmem, vmem),
        scratch_shapes=[
            pltpu.VMEM((TOK, FEAT), BF16),
            pltpu.VMEM(lens.shape, jnp.int32),
            pltpu.VMEM(por.shape, jnp.int32),
            pltpu.VMEM(aor.shape, jnp.int32),
            pltpu.VMEM(asi.shape, jnp.int32),
            pltpu.VMEM((TOK, FEAT), BF16),
            pltpu.VMEM((4, TOK, 4 * PAD), BF16),
            pltpu.VMEM((2, 4, PAD, OUT), BF16),
            pltpu.VMEM((4, PAD, 512), BF16),
            pltpu.VMEM((2, TOK, OUT), BF16),
            pltpu.VMEM((2, 2, HALF, OUT), BF16),
            pltpu.VMEM((2, 2, HALF, OUT), F32),
            pltpu.VMEM((2, 2, HALF, OUT), BF16),
            pltpu.VMEM((2, 2, HALF, OUT), BF16),
            pltpu.VMEM((2, 2, TOK, OUT), BF16),
            pltpu.VMEM((2, TOK, OUT), F32),
            pltpu.VMEM((TOK, 512), BF16),
            pltpu.VMEM((2, HALF, 512), BF16),
            pltpu.VMEM((2, HALF, 512), F32),
            pltpu.VMEM((2, HALF, 512), BF16),
            pltpu.VMEM((2, HALF, 512), BF16),
            pltpu.VMEM((2, TOK, 512), BF16),
            pltpu.VMEM((TOK, 512), F32),
            pltpu.VMEM((8, TOK), F32),
            pltpu.VMEM((7, 8, TOK), F32),
            pltpu.SemaphoreType.DMA((NSEM,)),
            pltpu.SemaphoreType.DMA((NSEM,)),
            pltpu.SemaphoreType.DMA((7,)),
        ],
        compiler_params=pltpu.CompilerParams(
            collective_id=0, has_side_effects=True, vmem_limit_bytes=40 << 20
        ),
        name="exchange",
    )(
        stay(prompt_token_states),
        gain.reshape(1, FEAT),
        weight,
        stay(adapter_down_maps.reshape(FEAT, 2 * RANK)),
        stay(adapter_up_maps.reshape(2, RANK, OUT)),
        stay(lens),
        stay(por),
        stay(aor),
        stay(asi),
    )
    return pl.pallas_call(
        combine,
        out_shape=(
            jax.ShapeDtypeStruct((TOK, SLOTS, OUT), BF16),
            jax.ShapeDtypeStruct((TOK, SLOTS, OUT), BF16),
        ),
        in_specs=[vmem] * 4,
        out_specs=(anyw, anyw),
        scratch_shapes=[
            pltpu.VMEM((GROUPS, 256, OUT), BF16),
            pltpu.VMEM((2, 16, SLOTS, OUT), BF16),
            pltpu.SemaphoreType.DMA((2,)),
        ],
        compiler_params=pltpu.CompilerParams(vmem_limit_bytes=40 << 20),
        name="combine",
    )(*gathered)


def solution(mesh):
    placed = (
        P("col", "row"),
        P("row"),
        P("col", None, "row"),
        P("col", "row", None),
        P("col", None, None, "row"),
        P(),
        P(),
        P(),
        P(),
    )
    return jax.shard_map(
        body,
        mesh=mesh,
        in_specs=placed,
        out_specs=(P("col", None, "row"), P("col", None, "row")),
        check_vma=False,
    )
```

```python
import functools

import jax
import jax.numpy as jnp
from jax import lax
from jax.experimental import pallas as pl
from jax.experimental.pallas import tpu as pltpu
from jax.sharding import PartitionSpec as P

F32 = jnp.float32
BF16 = jnp.bfloat16
MESH = pl.DeviceIdType.MESH

SLOTS = 16
TOK = 224
HALF = 112
FEAT = 640
BLK = 320
PAD = 384
OUT = 640
RANK = 128
GROUPS = 14

NAMES = (
    ["x1_%d" % i for i in range(4)]
    + ["d1_%d" % i for i in range(4)]
    + ["db_%d" % i for i in range(4)]
    + ["ss_%d" % i for i in range(7)]
    + ["w%d_%s" % (j, s) for j in range(2) for s in ("ap", "bp", "am", "bm", "rp", "rm")]
    + ["x2_%s" % s for s in ("p", "m", "rp", "rm")]
    + ["xc_%d" % i for i in range(5)]
    + ["d2_%s" % s for s in ("p", "m", "rp", "rm")]
    + ["u%d_%s" % (j, s) for j in range(2) for s in ("p", "m", "rp", "rm")]
    + ["v%d_%d_%s" % (j, k, s) for j in range(2) for k in range(4) for s in ("p", "m", "r")]
    + ["s%d_%s" % (j, s) for j in range(3) for s in ("fp", "fm", "np", "nm", "ap", "am")]
    + ["ra_%s" % s for s in ("p", "m", "rp", "rm", "c0", "c1", "c2", "c3", "c4")]
)
SEM = {name: i for i, name in enumerate(NAMES)}
NSEM = len(NAMES)


def to_col(row, n):
    same = lax.broadcasted_iota(jnp.int32, (n, n), 0) == lax.broadcasted_iota(jnp.int32, (n, n), 1)
    return jnp.sum(jnp.where(same, jnp.broadcast_to(row, (n, n)), 0.0), axis=1, keepdims=True)


def iota(shape, axis):
    return lax.broadcasted_iota(jnp.int32, shape, axis)


def targets(len_ref, por_ref, aor_ref, asi_ref, first_token):
    lens = len_ref[...].astype(F32)
    por = por_ref[...].astype(F32)
    aor = aor_ref[...].astype(F32)
    asi = asi_ref[...].astype(F32)
    n_prompt = lens.shape[1]
    n_req = por.shape[1]
    n_lib = asi.shape[1]
    before = jnp.sum(
        jnp.where(to_col(por, n_req) < por, 1.0, 0.0), axis=0, keepdims=True
    )
    position = iota((1, n_req), 1).astype(F32) - before
    hot = iota((n_lib, n_req), 0).astype(F32) == aor
    slot = jnp.sum(
        jnp.where(hot, jnp.broadcast_to(to_col(asi, n_lib), (n_lib, n_req)), 0.0),
        axis=0,
        keepdims=True,
    )
    by_prompt = jnp.where(iota((16, n_req), 0).astype(F32) == por, slot + 1.0, 0.0)
    by_place = jnp.where(iota((16, n_req), 0).astype(F32) == position, 1.0, 0.0)
    table = lax.dot_general(
        by_prompt.astype(BF16),
        by_place.astype(BF16),
        (((1,), (1,)), ((), ())),
        preferred_element_type=F32,
    )
    spread = jnp.where(iota((16, 256), 0) == iota((16, 256), 1) % 16, 1.0, 0.0)
    table = jnp.dot(table.astype(BF16), spread.astype(BF16), preferred_element_type=F32)
    ends = jnp.sum(
        jnp.where(
            iota((n_prompt, n_prompt), 0) <= iota((n_prompt, n_prompt), 1),
            jnp.broadcast_to(to_col(lens, n_prompt), (n_prompt, n_prompt)),
            0.0,
        ),
        axis=0,
        keepdims=True,
    )
    in_group = iota((16, 256), 1) // 16
    token = (first_token + 16 * iota((16, 256), 0) + in_group).astype(F32)
    prompt = jnp.zeros((16, 256), F32)
    for p in range(n_prompt):
        prompt += jnp.where(token >= ends[:, p : p + 1], 1.0, 0.0)
    chosen = jnp.zeros((16, 256), F32)
    for p in range(n_prompt):
        chosen += jnp.where(prompt == float(p), jnp.broadcast_to(table[p : p + 1, :], (16, 256)), 0.0)
    return jnp.where(chosen > 0.5, (chosen - 1.0) * 16.0 + in_group.astype(F32), -1.0)


def blend(up, rank, base, mix, j):
    for a in range(16):
        xo, zo = a // 4, a % 4
        delta = jnp.dot(
            rank[zo, j, :, RANK * xo : RANK * (xo + 1)],
            up[xo, zo, j],
            preferred_element_type=F32,
        )
        full = (base[j] + delta).astype(BF16)
        mix[:, 16 * a : 16 * (a + 1), :] = full.reshape(GROUPS, 16, OUT)


def place(pick, mix, g):
    rows = jnp.dot(pick[g], mix[g], preferred_element_type=F32).astype(BF16)
    return rows.reshape(16, SLOTS, OUT)


def exchange(
    x_hbm, gain_ref, w_ref, d_ref, up_ref, len_hbm, por_hbm, aor_hbm, asi_hbm,
    up_all, rank_all, base_out, pick, done,
    xv, lenv, porv, aorv, asiv,
    xg, xb, wb, da, db, bfar, bfirst, blater, bnear, bsum, bfinal, bown,
    rfar, rfirst, rlater, rnear, rsum, rfinal, rown, ss_own, ss_all, mix,
    ssem, rsem, lsem,
):
    r = lax.axis_index("row")
    c = lax.axis_index("col")
    y, core = lax.div(r, 2), lax.rem(r, 2)
    x, z = lax.div(c, 4), lax.rem(c, 4)

    def dev(x_, y_, z_, core_):
        return (y_ * 2 + core_, x_ * 4 + z_)

    def mod4(v):
        return lax.rem(v + 8, 4)

    def rc(src, dst, send, to, recv=None):
        return pltpu.make_async_remote_copy(
            src_ref=src,
            dst_ref=dst,
            send_sem=ssem.at[SEM[send]],
            recv_sem=rsem.at[SEM[send] if recv is None else recv],
            device_id=to,
            device_id_type=MESH,
        )

    xp, xm, x2 = mod4(x + 1), mod4(x - 1), mod4(x + 2)
    yp, ym, y2 = mod4(y + 1), mod4(y - 1), mod4(y + 2)
    zp, zm, z2 = mod4(z + 1), mod4(z - 1), mod4(z + 2)
    to_xp, to_xm = dev(xp, y, z, core), dev(xm, y, z, core)
    to_yp, to_ym = dev(x, yp, z, core), dev(x, ym, z, core)
    to_zp, to_zm = dev(x, y, zp, core), dev(x, y, zm, core)
    to_other = dev(x, y, z, 1 - core)
    copies = {}
    sends = []

    def go(src, dst, name, to):
        cp = rc(src, dst, name, to)
        cp.start()
        copies[name] = cp
        sends.append(cp)

    def got(*names):
        for name in names:
            copies[name].wait_recv()

    barrier = pltpu.get_barrier_semaphore()

    partners = [to_xp, to_xm, to_other]
    for k in range(1, 4):
        for other in (core, 1 - core):
            partners.append(dev(x, y, mod4(z + k), other))
            partners.append(dev(x, mod4(y + k), z, other))
    for partner in partners:
        pl.semaphore_signal(barrier, inc=1, device_id=partner, device_id_type=MESH)

    l_x = pltpu.make_async_copy(x_hbm, xv, lsem.at[0])
    l_x.start()
    l_small = []
    for i, (a, b) in enumerate(
        ((len_hbm, lenv), (por_hbm, porv), (aor_hbm, aorv), (asi_hbm, asiv))
    ):
        l_small.append(pltpu.make_async_copy(a, b, lsem.at[1 + i]))
        l_small[-1].start()

    odd = lax.rem(z, 2)
    off = pl.multiple_of(64 * odd, 64)
    pad_at = pl.multiple_of(BLK * (1 - odd), 64)
    for b in range(4):
        for j in range(2):
            wb[j, b, pl.ds(pad_at, 64), :] = jnp.zeros((64, OUT), BF16)
        db[b, pl.ds(pad_at, 64), :] = jnp.zeros((64, 512), BF16)

    l_x.wait()
    states = xv[...].astype(F32)
    xg[...] = (states * gain_ref[...].astype(F32)).astype(BF16)
    ss_own[...] = lax.dot_general(
        jnp.ones((8, FEAT), F32),
        states * states,
        (((1,), (1,)), ((), ())),
        precision=lax.Precision.HIGHEST,
        preferred_element_type=F32,
    )
    pl.semaphore_wait(barrier, len(partners))

    def u1(xo, a, n):
        return up_all.at[xo, z, 1, pl.ds(a, n), :]

    def u0(zo, a, n):
        return up_all.at[x, zo, 0, pl.ds(a, n), :]

    go(up_ref.at[1], u1(x, 0, 128), "u1_p", to_xp)
    go(up_ref.at[1], u1(x, 0, 128), "u1_m", to_xm)

    def wslot(j, xo, a):
        return wb.at[j, xo, pl.ds(pl.multiple_of(off + a, 32), 160), :]

    def weights(j):
        go(w_ref.at[j, pl.ds(0, 160), :], wslot(j, x, 0), "w%d_ap" % j, to_xp)
        go(w_ref.at[j, pl.ds(160, 160), :], wslot(j, x, 160), "w%d_bm" % j, to_xm)
        go(w_ref.at[j, pl.ds(160, 160), :], wslot(j, x, 160), "w%d_bp" % j, to_xp)
        go(w_ref.at[j, pl.ds(0, 160), :], wslot(j, x, 0), "w%d_am" % j, to_xm)

    def relay_weights(j):
        got("w%d_ap" % j)
        go(wslot(j, xm, 0), wslot(j, xm, 0), "w%d_rp" % j, to_xp)
        got("w%d_bm" % j)
        go(wslot(j, xp, 160), wslot(j, xp, 160), "w%d_rm" % j, to_xm)

    weights(1)

    some = []
    for h in range(2):
        for k in range(2):
            zd = 2 * core + h
            src = xg.at[pl.ds(HALF * k, HALF), pl.ds(256 * h, PAD)]
            dst = xb.at[z, pl.ds(HALF * k, HALF), pl.ds(pl.multiple_of(PAD * y, 128), PAD)]
            own = jnp.logical_and(zd == z, core == k)
            sem = SEM["x1_0"] + z
            cp = rc(src, dst, "x1_%d" % (2 * h + k), dev(x, y, zd, k), sem)
            some.append((own, cp))

            @pl.when(jnp.logical_not(own))
            def _():
                cp.start()

            @pl.when(own)
            def _():
                pltpu.make_async_copy(src, dst, rsem.at[sem]).start()

    for h in range(2):
        for k in range(2):
            zd = 2 * core + h
            src = d_ref.at[pl.ds(BLK * h, BLK), pl.ds(RANK * k, RANK)]
            dst = da.at[z]
            own = jnp.logical_and(zd == z, core == k)
            sem = SEM["d1_0"] + z
            cp = rc(src, dst, "d1_%d" % (2 * h + k), dev(x, y, zd, k), sem)
            some.append((own, cp))

            @pl.when(jnp.logical_not(own))
            def _():
                cp.start()

            @pl.when(own)
            def _():
                pltpu.make_async_copy(src, dst, rsem.at[sem]).start()

    for i in range(1, 8):
        go(ss_own, ss_all.at[i - 1], "ss_%d" % (i - 1), (lax.rem(r + i, 8), c))

    go(up_ref.at[0], u0(z, 0, 128), "u0_p", to_zp)
    go(up_ref.at[0], u0(z, 0, 128), "u0_m", to_zm)

    def v1(xo, zo):
        return up_all.at[xo, zo, 1]

    def v0(xo, zo):
        return up_all.at[xo, zo, 0]

    def send_v1(k, src):
        xo = mod4(x + k)
        go(src, v1(xo, z), "v1_%d_p" % k, to_zp)
        go(src, v1(xo, z), "v1_%d_m" % k, to_zm)

    def relay_v1(k):
        xo = mod4(x + k)
        if k < 2:
            got("v1_%d_p" % k)
            go(v1(xo, zm), v1(xo, zm), "v1_%d_r" % k, to_zp)
        else:
            got("v1_%d_m" % k)
            go(v1(xo, zp), v1(xo, zp), "v1_%d_r" % k, to_zm)

    def send_v0(k, src):
        zo = mod4(z + k)
        go(src, v0(x, zo), "v0_%d_p" % k, to_xp)
        go(src, v0(x, zo), "v0_%d_m" % k, to_xm)

    def relay_v0(k):
        zo = mod4(z + k)
        if k < 2:
            got("v0_%d_p" % k)
            go(v0(xm, zo), v0(xm, zo), "v0_%d_r" % k, to_xp)
        else:
            got("v0_%d_m" % k)
            go(v0(xp, zo), v0(xp, zo), "v0_%d_r" % k, to_xm)

    def finish(j, k):
        got("v%d_%d_%s" % (j, k, "m" if k < 2 else "p"), "v%d_%d_r" % (j, k))

    send_v1(0, up_ref.at[1])

    l_w = pltpu.make_async_copy(w_ref, wb.at[:, x, pl.ds(off, BLK), :], lsem.at[5])
    l_w.start()
    l_u = pltpu.make_async_copy(up_ref, up_all.at[x, z], lsem.at[6])
    l_u.start()

    def unit(yo, a, n):
        return xb.at[
            pl.ds(a, n),
            pl.ds(pl.multiple_of(HALF * core, 16), HALF),
            pl.ds(pl.multiple_of(PAD * yo, 128), PAD),
        ]

    for zs in range(4):
        piece = xb.at[
            zs,
            pl.ds(pl.multiple_of(HALF * core, 16), HALF),
            pl.ds(pl.multiple_of(PAD * y, 128), PAD),
        ]
        rc(piece, piece, "x1_0", to_other, SEM["x1_0"] + zs).wait_recv()
    go(unit(y, 0, 4), unit(y, 0, 4), "x2_p", to_yp)
    go(unit(y, 0, 4), unit(y, 0, 4), "x2_m", to_ym)
    go(unit(y, 0, 4), unit(y, 0, 4), "xc_0", to_other)

    def dcols(xo):
        return pl.ds(pl.multiple_of(RANK * xo, 128), RANK)

    for zs in range(4):
        rc(da.at[zs], da.at[zs], "d1_0", to_other, SEM["d1_0"] + zs).wait_recv()
    for k in range(1, 4):
        yd = mod4(y + k)
        go(da.at[yd], db.at[y, pl.ds(off, BLK), dcols(x)], "db_%d" % k, dev(x, yd, z, core))
    l_d = pltpu.make_async_copy(da.at[y], db.at[y, pl.ds(off, BLK), dcols(x)], lsem.at[7])
    l_d.start()

    got("u1_p", "u1_m")
    send_v1(1, v1(xp, z))
    send_v1(3, v1(xm, z))
    got("u0_p", "u0_m")
    go(u0(zm, 0, 64), u0(zm, 0, 64), "u0_rp", to_zp)
    go(u0(zp, 64, 64), u0(zp, 64, 64), "u0_rm", to_zm)

    for cp in l_small:
        cp.wait()
    tgt = targets(lenv, porv, aorv, asiv, c * TOK)

    def picks(g):
        hit = jnp.where(
            iota((256, 256), 0).astype(F32) == tgt[g : g + 1, :], 1.0, 0.0
        )
        pick[g] = hit.T.astype(BF16)

    def dpart(xo, a, n):
        return db.at[pl.ds(a, n), pl.ds(off, BLK), dcols(xo)]

    l_d.wait()
    got("db_1", "db_2", "db_3")
    go(dpart(x, 0, 4), dpart(x, 0, 4), "d2_p", to_xp)
    go(dpart(x, 0, 4), dpart(x, 0, 4), "d2_m", to_xm)
    relay_weights(1)
    go(u1(xm, 0, 64), u1(xm, 0, 64), "u1_rp", to_xp)
    go(u1(xp, 64, 64), u1(xp, 64, 64), "u1_rm", to_xm)

    got("x2_p")
    go(unit(ym, 0, 2), unit(ym, 0, 2), "x2_rp", to_yp)
    go(unit(ym, 0, 4), unit(ym, 0, 4), "xc_1", to_other)
    got("x2_m")
    go(unit(yp, 2, 2), unit(yp, 2, 2), "x2_rm", to_ym)
    go(unit(yp, 0, 4), unit(yp, 0, 4), "xc_2", to_other)
    relay_v1(0)
    for g in range(GROUPS // 2):
        picks(g)
    got("x2_rp")
    go(unit(y2, 0, 2), unit(y2, 0, 2), "xc_3", to_other)
    got("x2_rm")
    go(unit(y2, 2, 2), unit(y2, 2, 2), "xc_4", to_other)
    got("d2_p")
    go(dpart(xm, 0, 2), dpart(xm, 0, 2), "d2_rp", to_xp)
    got("d2_m")
    go(dpart(xp, 2, 2), dpart(xp, 2, 2), "d2_rm", to_xm)
    weights(0)
    relay_v1(1)
    relay_v1(3)
    for i in range(5):
        got("xc_%d" % i)
    l_w.wait()

    up_rows, low_rows = pl.ds(0, HALF), pl.ds(HALF, HALF)

    def partials(s, product, far, first, later, near, final):
        far[...] = product(z2).astype(BF16)
        go(far.at[up_rows], first.at[0], "s%d_fp" % s, to_zp)
        go(far.at[low_rows], first.at[1], "s%d_fm" % s, to_zm)
        part = product(zp)
        near[0] = part[HALF:].astype(BF16)
        later[0] = part[:HALF]
        go(near.at[0], final.at[0, low_rows], "s%d_np" % s, to_zp)
        part = product(zm)
        near[1] = part[:HALF].astype(BF16)
        later[1] = part[HALF:]
        go(near.at[1], final.at[1, up_rows], "s%d_nm" % s, to_zm)

    def pass_on(s, first, later, total, final):
        got("s%d_fp" % s)
        total[0] = (later[0] + first[0].astype(F32)).astype(BF16)
        go(total.at[0], final.at[0, up_rows], "s%d_ap" % s, to_zp)
        got("s%d_fm" % s)
        total[1] = (later[1] + first[1].astype(F32)).astype(BF16)
        go(total.at[1], final.at[1, low_rows], "s%d_am" % s, to_zm)

    def arrived(s):
        got("s%d_np" % s, "s%d_nm" % s, "s%d_ap" % s, "s%d_am" % s)

    def base_part(j):
        def product(block):
            return jnp.dot(
                xb[block], wb[j].reshape(4 * PAD, OUT), preferred_element_type=F32
            )

        partials(j, product, bfar.at[j], bfirst.at[j], blater.at[j], bnear.at[j], bfinal.at[j])
        bown[j] = product(z)

    def base_pass(j):
        pass_on(j, bfirst.at[j], blater.at[j], bsum.at[j], bfinal.at[j])

    def base_done(j):
        arrived(j)
        base_out[j] = (
            bown[j] + bfinal[j, 0].astype(F32) + bfinal[j, 1].astype(F32)
        ) * scale

    def rank_product(block):
        return jnp.dot(xb[block], db[...].reshape(4 * PAD, 512), preferred_element_type=F32)

    got("w1_bp", "w1_am", "w1_rp", "w1_rm")
    base_part(1)
    got("d2_rp", "d2_rm")
    partials(2, rank_product, rfar, rfirst, rlater, rnear, rfinal)
    rown[...] = rank_product(z)
    base_pass(1)
    got("u0_rp", "u0_rm", "u1_rp", "u1_rm")
    send_v1(2, v1(x2, z))
    relay_weights(0)
    for k in (0, 1, 3, 2):
        send_v0(k, up_ref.at[0] if k == 0 else v0(x, mod4(z + k)))
    pass_on(2, rfirst, rlater, rsum, rfinal)

    total = ss_own[...]
    for i in range(7):
        got("ss_%d" % i)
        total += ss_all[i]
    scale = to_col(lax.rsqrt(total[0:1, :] / (FEAT * 8) + 1e-05), TOK)
    for g in range(GROUPS // 2, GROUPS):
        picks(g)
    base_done(1)
    relay_v1(2)

    def ranks(yo, a, n):
        return rank_all.at[yo, core, pl.ds(a, n)]

    arrived(2)
    rank_all[y, core] = (
        (rown[...] + rfinal[0].astype(F32) + rfinal[1].astype(F32)) * scale
    ).astype(BF16)
    go(ranks(y, 0, TOK), ranks(y, 0, TOK), "ra_p", to_yp)
    go(ranks(y, 0, TOK), ranks(y, 0, TOK), "ra_m", to_ym)
    go(ranks(y, 0, TOK), ranks(y, 0, TOK), "ra_c0", to_other)

    got("w0_bp", "w0_am", "w0_rp", "w0_rm")
    base_part(0)

    got("ra_p")
    go(ranks(ym, 0, HALF), ranks(ym, 0, HALF), "ra_rp", to_yp)
    go(ranks(ym, 0, TOK), ranks(ym, 0, TOK), "ra_c1", to_other)
    got("ra_m")
    go(ranks(yp, HALF, HALF), ranks(yp, HALF, HALF), "ra_rm", to_ym)
    go(ranks(yp, 0, TOK), ranks(yp, 0, TOK), "ra_c2", to_other)
    base_pass(0)
    got("ra_rp")
    go(ranks(y2, 0, HALF), ranks(y2, 0, HALF), "ra_c3", to_other)
    got("ra_rm")
    go(ranks(y2, HALF, HALF), ranks(y2, HALF, HALF), "ra_c4", to_other)
    relay_v0(0)
    relay_v0(1)

    for k in range(4):
        finish(1, k)
    for i in range(5):
        got("ra_c%d" % i)
    l_u.wait()
    blend(up_all, rank_all, base_out, mix, 1)

    def group(i, carry):
        for n in range(2):
            at = pl.multiple_of(32 * i + 16 * n, 16)
            done[pl.ds(at, 16)] = place(pick, mix, 2 * i + n)
        return carry

    lax.fori_loop(0, GROUPS // 2, group, 0)
    relay_v0(3)
    relay_v0(2)
    base_done(0)
    for k in range(4):
        finish(0, k)
    for own, cp in some:

        @pl.when(jnp.logical_not(own))
        def _():
            cp.wait_send()

    for cp in sends:
        cp.wait_send()


def combine(up, rank, base, pick, done, q_out, v_out, mix, obuf, osem, dsem):
    whole = pltpu.make_async_copy(done, v_out, dsem.at[0])
    whole.start()
    blend(up, rank, base, mix, 0)

    def put(i, slot):
        return pltpu.make_async_copy(
            obuf.at[slot], q_out.at[pl.ds(32 * i, 32)], osem.at[slot]
        )

    def group(i, carry):
        slot = lax.rem(i, 2)

        @pl.when(i >= 2)
        def _():
            put(i - 2, slot).wait()

        for n in range(2):
            obuf[slot, 16 * n : 16 * (n + 1)] = place(pick, mix, 2 * i + n)
        put(i, slot).start()
        return carry

    lax.fori_loop(0, GROUPS // 2, group, 0)
    for i in (GROUPS // 2 - 2, GROUPS // 2 - 1):
        put(i, i % 2).wait()
    whole.wait()


def stay(array):
    return pltpu.with_memory_space_constraint(array, pltpu.HBM)


def body(
    prompt_token_states,
    gain,
    projection_weight,
    adapter_down_maps,
    adapter_up_maps,
    prompt_token_length,
    prompt_of_request,
    adapter_of_request,
    adapter_slot_index,
):
    weight = jnp.transpose(projection_weight, (1, 0, 2))
    vmem = pl.BlockSpec(memory_space=pltpu.VMEM)
    hbm = pl.BlockSpec(memory_space=pltpu.HBM)
    anyw = pl.BlockSpec(memory_space=pl.ANY)
    lens = prompt_token_length.reshape(1, -1)
    por = prompt_of_request.reshape(1, -1)
    aor = adapter_of_request.reshape(1, -1)
    asi = adapter_slot_index.reshape(1, -1)
    gathered = pl.pallas_call(
        exchange,
        out_shape=(
            jax.ShapeDtypeStruct((4, 4, 2, RANK, OUT), BF16),
            jax.ShapeDtypeStruct((4, 2, TOK, 512), BF16),
            jax.ShapeDtypeStruct((2, TOK, OUT), F32),
            jax.ShapeDtypeStruct((GROUPS, 256, 256), BF16),
            jax.ShapeDtypeStruct((TOK, SLOTS, OUT), BF16),
        ),
        in_specs=[hbm, vmem, anyw, hbm, hbm, hbm, hbm, hbm, hbm],
        out_specs=(vmem, vmem, vmem, vmem, vmem),
        scratch_shapes=[
            pltpu.VMEM((TOK, FEAT), BF16),
            pltpu.VMEM(lens.shape, jnp.int32),
            pltpu.VMEM(por.shape, jnp.int32),
            pltpu.VMEM(aor.shape, jnp.int32),
            pltpu.VMEM(asi.shape, jnp.int32),
            pltpu.VMEM((TOK, FEAT), BF16),
            pltpu.VMEM((4, TOK, 4 * PAD), BF16),
            pltpu.VMEM((2, 4, PAD, OUT), BF16),
            pltpu.VMEM((4, BLK, RANK), BF16),
            pltpu.VMEM((4, PAD, 512), BF16),
            pltpu.VMEM((2, TOK, OUT), BF16),
            pltpu.VMEM((2, 2, HALF, OUT), BF16),
            pltpu.VMEM((2, 2, HALF, OUT), F32),
            pltpu.VMEM((2, 2, HALF, OUT), BF16),
            pltpu.VMEM((2, 2, HALF, OUT), BF16),
            pltpu.VMEM((2, 2, TOK, OUT), BF16),
            pltpu.VMEM((2, TOK, OUT), F32),
            pltpu.VMEM((TOK, 512), BF16),
            pltpu.VMEM((2, HALF, 512), BF16),
            pltpu.VMEM((2, HALF, 512), F32),
            pltpu.VMEM((2, HALF, 512), BF16),
            pltpu.VMEM((2, HALF, 512), BF16),
            pltpu.VMEM((2, TOK, 512), BF16),
            pltpu.VMEM((TOK, 512), F32),
            pltpu.VMEM((8, TOK), F32),
            pltpu.VMEM((7, 8, TOK), F32),
            pltpu.VMEM((GROUPS, 256, OUT), BF16),
            pltpu.SemaphoreType.DMA((NSEM,)),
            pltpu.SemaphoreType.DMA((NSEM,)),
            pltpu.SemaphoreType.DMA((8,)),
        ],
        compiler_params=pltpu.CompilerParams(
            collective_id=0, has_side_effects=True, vmem_limit_bytes=27 << 20
        ),
        name="exchange",
    )(
        stay(prompt_token_states),
        gain.reshape(1, FEAT),
        weight,
        stay(adapter_down_maps.reshape(FEAT, 2 * RANK)),
        stay(adapter_up_maps.reshape(2, RANK, OUT)),
        stay(lens),
        stay(por),
        stay(aor),
        stay(asi),
    )
    return pl.pallas_call(
        combine,
        out_shape=(
            jax.ShapeDtypeStruct((TOK, SLOTS, OUT), BF16),
            jax.ShapeDtypeStruct((TOK, SLOTS, OUT), BF16),
        ),
        in_specs=[vmem] * 5,
        out_specs=(anyw, anyw),
        scratch_shapes=[
            pltpu.VMEM((GROUPS, 256, OUT), BF16),
            pltpu.VMEM((2, 32, SLOTS, OUT), BF16),
            pltpu.SemaphoreType.DMA((2,)),
            pltpu.SemaphoreType.DMA((1,)),
        ],
        compiler_params=pltpu.CompilerParams(vmem_limit_bytes=20 << 20),
        name="combine",
    )(*gathered)


def solution(mesh):
    placed = (
        P("col", "row"),
        P("row"),
        P("col", None, "row"),
        P("col", "row", None),
        P("col", None, None, "row"),
        P(),
        P(),
        P(),
        P(),
    )
    return jax.shard_map(
        body,
        mesh=mesh,
        in_specs=placed,
        out_specs=(P("col", None, "row"), P("col", None, "row")),
        check_vma=False,
    )
```

```python
import functools

import jax
import jax.numpy as jnp
from jax import lax
from jax.experimental import pallas as pl
from jax.experimental.pallas import tpu as pltpu
from jax.sharding import PartitionSpec as P

F32 = jnp.float32
BF16 = jnp.bfloat16
MESH = pl.DeviceIdType.MESH

SLOTS = 16
TOK = 224
HALF = 112
FEAT = 640
BLK = 320
PAD = 384
OUT = 640
RANK = 128
GROUPS = 14

NAMES = (
    ["x1_%d" % i for i in range(4)]
    + ["d1_%d" % i for i in range(4)]
    + ["db_%d" % i for i in range(4)]
    + ["ss_%d" % i for i in range(7)]
    + ["w%d_%s" % (j, s) for j in range(2) for s in ("ap", "bp", "am", "bm", "rp", "rm")]
    + ["x2_%s" % s for s in ("p", "m", "rp", "rm")]
    + ["xc_%d" % i for i in range(5)]
    + ["d2_%s" % s for s in ("p", "m", "rp", "rm")]
    + ["u%d_%s" % (j, s) for j in range(2) for s in ("p", "m", "rp", "rm")]
    + ["v%d_%d_%s" % (j, k, s) for j in range(2) for k in range(4) for s in ("p", "m", "r")]
    + ["s%d_%s" % (j, s) for j in range(3) for s in ("fp", "fm", "np", "nm", "ap", "am")]
    + ["ra_%s" % s for s in ("p", "m", "rp", "rm", "c0", "c1", "c2", "c3", "c4")]
)
SEM = {name: i for i, name in enumerate(NAMES)}
NSEM = len(NAMES)


def to_col(row, n):
    same = lax.broadcasted_iota(jnp.int32, (n, n), 0) == lax.broadcasted_iota(jnp.int32, (n, n), 1)
    return jnp.sum(jnp.where(same, jnp.broadcast_to(row, (n, n)), 0.0), axis=1, keepdims=True)


def iota(shape, axis):
    return lax.broadcasted_iota(jnp.int32, shape, axis)


def targets(len_ref, por_ref, aor_ref, asi_ref, first_token):
    lens = len_ref[...].astype(F32)
    por = por_ref[...].astype(F32)
    aor = aor_ref[...].astype(F32)
    asi = asi_ref[...].astype(F32)
    n_prompt = lens.shape[1]
    n_req = por.shape[1]
    n_lib = asi.shape[1]
    before = jnp.sum(
        jnp.where(to_col(por, n_req) < por, 1.0, 0.0), axis=0, keepdims=True
    )
    position = iota((1, n_req), 1).astype(F32) - before
    hot = iota((n_lib, n_req), 0).astype(F32) == aor
    slot = jnp.sum(
        jnp.where(hot, jnp.broadcast_to(to_col(asi, n_lib), (n_lib, n_req)), 0.0),
        axis=0,
        keepdims=True,
    )
    by_prompt = jnp.where(iota((16, n_req), 0).astype(F32) == por, slot + 1.0, 0.0)
    by_place = jnp.where(iota((16, n_req), 0).astype(F32) == position, 1.0, 0.0)
    table = lax.dot_general(
        by_prompt.astype(BF16),
        by_place.astype(BF16),
        (((1,), (1,)), ((), ())),
        preferred_element_type=F32,
    )
    spread = jnp.where(iota((16, 256), 0) == iota((16, 256), 1) % 16, 1.0, 0.0)
    table = jnp.dot(table.astype(BF16), spread.astype(BF16), preferred_element_type=F32)
    ends = jnp.sum(
        jnp.where(
            iota((n_prompt, n_prompt), 0) <= iota((n_prompt, n_prompt), 1),
            jnp.broadcast_to(to_col(lens, n_prompt), (n_prompt, n_prompt)),
            0.0,
        ),
        axis=0,
        keepdims=True,
    )
    in_group = iota((16, 256), 1) // 16
    token = (first_token + 16 * iota((16, 256), 0) + in_group).astype(F32)
    prompt = jnp.zeros((16, 256), F32)
    for p in range(n_prompt):
        prompt += jnp.where(token >= ends[:, p : p + 1], 1.0, 0.0)
    chosen = jnp.zeros((16, 256), F32)
    for p in range(n_prompt):
        chosen += jnp.where(prompt == float(p), jnp.broadcast_to(table[p : p + 1, :], (16, 256)), 0.0)
    return jnp.where(chosen > 0.5, (chosen - 1.0) * 16.0 + in_group.astype(F32), -1.0)


def blend(up, rank, base, mix, j, adapters):
    for a in adapters:
        xo, zo = a // 4, a % 4
        delta = jnp.dot(
            rank[zo, j, :, RANK * xo : RANK * (xo + 1)],
            up[xo, zo, j],
            preferred_element_type=F32,
        )
        full = (base[j] + delta).astype(BF16)
        mix[:, 16 * a : 16 * (a + 1), :] = full.reshape(GROUPS, 16, OUT)


def place(pick, mix, g):
    rows = jnp.dot(pick[g], mix[g], preferred_element_type=F32).astype(BF16)
    return rows.reshape(16, SLOTS, OUT)


def exchange(
    x_hbm, gain_hbm, w_ref, d_ref, up_ref, len_hbm, por_hbm, aor_hbm, asi_hbm,
    up_all, rank_all, base_out, pick, done,
    xv, gainv, lenv, porv, aorv, asiv,
    xg, xb, wb, da, db, bfar, bfirst, blater, bnear, bsum, bfinal, bown,
    rfar, rfirst, rlater, rnear, rsum, rfinal, rown, ss_own, ss_all, mix,
    ssem, rsem, lsem,
):
    r = lax.axis_index("row")
    c = lax.axis_index("col")
    y, core = lax.div(r, 2), lax.rem(r, 2)
    x, z = lax.div(c, 4), lax.rem(c, 4)

    def dev(x_, y_, z_, core_):
        return (y_ * 2 + core_, x_ * 4 + z_)

    def mod4(v):
        return lax.rem(v + 8, 4)

    def rc(src, dst, send, to, recv=None):
        return pltpu.make_async_remote_copy(
            src_ref=src,
            dst_ref=dst,
            send_sem=ssem.at[SEM[send]],
            recv_sem=rsem.at[SEM[send] if recv is None else recv],
            device_id=to,
            device_id_type=MESH,
        )

    xp, xm, x2 = mod4(x + 1), mod4(x - 1), mod4(x + 2)
    yp, ym, y2 = mod4(y + 1), mod4(y - 1), mod4(y + 2)
    zp, zm, z2 = mod4(z + 1), mod4(z - 1), mod4(z + 2)
    to_xp, to_xm = dev(xp, y, z, core), dev(xm, y, z, core)
    to_yp, to_ym = dev(x, yp, z, core), dev(x, ym, z, core)
    to_zp, to_zm = dev(x, y, zp, core), dev(x, y, zm, core)
    to_other = dev(x, y, z, 1 - core)
    copies = {}
    sends = []

    def go(src, dst, name, to):
        cp = rc(src, dst, name, to)
        cp.start()
        copies[name] = cp
        sends.append(cp)

    def got(*names):
        for name in names:
            copies[name].wait_recv()

    barrier = pltpu.get_barrier_semaphore()

    partners = [to_xp, to_xm, to_other]
    for k in range(1, 4):
        for other in (core, 1 - core):
            partners.append(dev(x, y, mod4(z + k), other))
            partners.append(dev(x, mod4(y + k), z, other))
    for partner in partners:
        pl.semaphore_signal(barrier, inc=1, device_id=partner, device_id_type=MESH)

    l_x = pltpu.make_async_copy(x_hbm, xv, lsem.at[0])
    l_x.start()
    l_g = pltpu.make_async_copy(gain_hbm, gainv, lsem.at[8])
    l_g.start()
    l_small = []
    for i, (a, b) in enumerate(
        ((len_hbm, lenv), (por_hbm, porv), (aor_hbm, aorv), (asi_hbm, asiv))
    ):
        l_small.append(pltpu.make_async_copy(a, b, lsem.at[1 + i]))
        l_small[-1].start()

    odd = lax.rem(z, 2)
    off = pl.multiple_of(64 * odd, 64)
    pad_at = pl.multiple_of(BLK * (1 - odd), 64)
    for b in range(4):
        for j in range(2):
            wb[j, b, pl.ds(pad_at, 64), :] = jnp.zeros((64, OUT), BF16)
        db[b, pl.ds(pad_at, 64), :] = jnp.zeros((64, 512), BF16)

    l_x.wait()
    l_g.wait()
    states = xv[...].astype(F32)
    xg[...] = (states * gainv[...].astype(F32).reshape(1, FEAT)).astype(BF16)
    ss_own[...] = lax.dot_general(
        jnp.ones((8, FEAT), F32),
        states * states,
        (((1,), (1,)), ((), ())),
        precision=lax.Precision.HIGHEST,
        preferred_element_type=F32,
    )
    pl.semaphore_wait(barrier, len(partners))

    def u1(xo, a, n):
        return up_all.at[xo, z, 1, pl.ds(a, n), :]

    def u0(zo, a, n):
        return up_all.at[x, zo, 0, pl.ds(a, n), :]

    go(up_ref.at[1], u1(x, 0, 128), "u1_p", to_xp)
    go(up_ref.at[1], u1(x, 0, 128), "u1_m", to_xm)

    def wslot(j, xo, a):
        return wb.at[j, xo, pl.ds(pl.multiple_of(off + a, 32), 160), :]

    def weights(j):
        go(w_ref.at[j, pl.ds(0, 160), :], wslot(j, x, 0), "w%d_ap" % j, to_xp)
        go(w_ref.at[j, pl.ds(160, 160), :], wslot(j, x, 160), "w%d_bm" % j, to_xm)
        go(w_ref.at[j, pl.ds(160, 160), :], wslot(j, x, 160), "w%d_bp" % j, to_xp)
        go(w_ref.at[j, pl.ds(0, 160), :], wslot(j, x, 0), "w%d_am" % j, to_xm)

    def relay_weights(j):
        got("w%d_ap" % j)
        go(wslot(j, xm, 0), wslot(j, xm, 0), "w%d_rp" % j, to_xp)
        got("w%d_bm" % j)
        go(wslot(j, xp, 160), wslot(j, xp, 160), "w%d_rm" % j, to_xm)

    weights(1)

    some = []
    for h in range(2):
        for k in range(2):
            zd = 2 * core + h
            src = d_ref.at[pl.ds(BLK * h, BLK), pl.ds(RANK * k, RANK)]
            dst = da.at[z]
            own = jnp.logical_and(zd == z, core == k)
            sem = SEM["d1_0"] + z
            cp = rc(src, dst, "d1_%d" % (2 * h + k), dev(x, y, zd, k), sem)
            some.append((own, cp))

            @pl.when(jnp.logical_not(own))
            def _():
                cp.start()

            @pl.when(own)
            def _():
                pltpu.make_async_copy(src, dst, rsem.at[sem]).start()

    for h in range(2):
        for k in range(2):
            zd = 2 * core + h
            src = xg.at[pl.ds(HALF * k, HALF), pl.ds(256 * h, PAD)]
            dst = xb.at[z, pl.ds(HALF * k, HALF), pl.ds(pl.multiple_of(PAD * y, 128), PAD)]
            own = jnp.logical_and(zd == z, core == k)
            sem = SEM["x1_0"] + z
            cp = rc(src, dst, "x1_%d" % (2 * h + k), dev(x, y, zd, k), sem)
            some.append((own, cp))

            @pl.when(jnp.logical_not(own))
            def _():
                cp.start()

            @pl.when(own)
            def _():
                pltpu.make_async_copy(src, dst, rsem.at[sem]).start()

    for i in range(1, 8):
        go(ss_own, ss_all.at[i - 1], "ss_%d" % (i - 1), (lax.rem(r + i, 8), c))

    go(up_ref.at[0], u0(z, 0, 128), "u0_p", to_zp)
    go(up_ref.at[0], u0(z, 0, 128), "u0_m", to_zm)

    def v1(xo, zo):
        return up_all.at[xo, zo, 1]

    def v0(xo, zo):
        return up_all.at[xo, zo, 0]

    def send_v1(k, src):
        xo = mod4(x + k)
        go(src, v1(xo, z), "v1_%d_p" % k, to_zp)
        go(src, v1(xo, z), "v1_%d_m" % k, to_zm)

    def relay_v1(k):
        xo = mod4(x + k)
        if k < 2:
            got("v1_%d_p" % k)
            go(v1(xo, zm), v1(xo, zm), "v1_%d_r" % k, to_zp)
        else:
            got("v1_%d_m" % k)
            go(v1(xo, zp), v1(xo, zp), "v1_%d_r" % k, to_zm)

    def send_v0(k, src):
        zo = mod4(z + k)
        go(src, v0(x, zo), "v0_%d_p" % k, to_xp)
        go(src, v0(x, zo), "v0_%d_m" % k, to_xm)

    def relay_v0(k):
        zo = mod4(z + k)
        if k < 2:
            got("v0_%d_p" % k)
            go(v0(xm, zo), v0(xm, zo), "v0_%d_r" % k, to_xp)
        else:
            got("v0_%d_m" % k)
            go(v0(xp, zo), v0(xp, zo), "v0_%d_r" % k, to_xm)

    def finish(j, k):
        got("v%d_%d_%s" % (j, k, "m" if k < 2 else "p"), "v%d_%d_r" % (j, k))

    send_v1(0, up_ref.at[1])

    l_w = pltpu.make_async_copy(w_ref, wb.at[:, x, pl.ds(off, BLK), :], lsem.at[5])
    l_w.start()
    l_u = pltpu.make_async_copy(up_ref, up_all.at[x, z], lsem.at[6])
    l_u.start()

    def dcols(xo):
        return pl.ds(pl.multiple_of(RANK * xo, 128), RANK)

    for zs in range(4):
        rc(da.at[zs], da.at[zs], "d1_0", to_other, SEM["d1_0"] + zs).wait_recv()
    for k in range(1, 4):
        yd = mod4(y + k)
        go(da.at[yd], db.at[y, pl.ds(off, BLK), dcols(x)], "db_%d" % k, dev(x, yd, z, core))
    l_d = pltpu.make_async_copy(da.at[y], db.at[y, pl.ds(off, BLK), dcols(x)], lsem.at[7])
    l_d.start()

    def unit(yo, a, n):
        return xb.at[
            pl.ds(a, n),
            pl.ds(pl.multiple_of(HALF * core, 16), HALF),
            pl.ds(pl.multiple_of(PAD * yo, 128), PAD),
        ]

    for zs in range(4):
        piece = xb.at[
            zs,
            pl.ds(pl.multiple_of(HALF * core, 16), HALF),
            pl.ds(pl.multiple_of(PAD * y, 128), PAD),
        ]
        rc(piece, piece, "x1_0", to_other, SEM["x1_0"] + zs).wait_recv()
    go(unit(y, 0, 4), unit(y, 0, 4), "x2_p", to_yp)
    go(unit(y, 0, 4), unit(y, 0, 4), "x2_m", to_ym)
    go(unit(y, 0, 4), unit(y, 0, 4), "xc_0", to_other)

    got("u1_p", "u1_m")
    send_v1(1, v1(xp, z))
    send_v1(3, v1(xm, z))

    def dpart(xo, a, n):
        return db.at[pl.ds(a, n), pl.ds(off, BLK), dcols(xo)]

    l_d.wait()
    got("db_1", "db_2", "db_3")
    go(dpart(x, 0, 4), dpart(x, 0, 4), "d2_p", to_xp)
    go(dpart(x, 0, 4), dpart(x, 0, 4), "d2_m", to_xm)
    send_v0(0, up_ref.at[0])
    got("u0_p", "u0_m")
    go(u0(zm, 0, 64), u0(zm, 0, 64), "u0_rp", to_zp)
    go(u0(zp, 64, 64), u0(zp, 64, 64), "u0_rm", to_zm)
    relay_weights(1)

    for cp in l_small:
        cp.wait()
    tgt = targets(lenv, porv, aorv, asiv, c * TOK)

    def picks(g):
        hit = jnp.where(
            iota((256, 256), 0).astype(F32) == tgt[g : g + 1, :], 1.0, 0.0
        )
        pick[g] = hit.T.astype(BF16)

    got("x2_p")
    go(unit(ym, 0, 2), unit(ym, 0, 2), "x2_rp", to_yp)
    go(unit(ym, 0, 4), unit(ym, 0, 4), "xc_1", to_other)
    got("x2_m")
    go(unit(yp, 2, 2), unit(yp, 2, 2), "x2_rm", to_ym)
    go(unit(yp, 0, 4), unit(yp, 0, 4), "xc_2", to_other)
    relay_v1(0)
    for g in range(GROUPS // 2):
        picks(g)
    got("x2_rp")
    go(unit(y2, 0, 2), unit(y2, 0, 2), "xc_3", to_other)
    got("x2_rm")
    go(unit(y2, 2, 2), unit(y2, 2, 2), "xc_4", to_other)
    got("d2_p")
    go(dpart(xm, 0, 2), dpart(xm, 0, 2), "d2_rp", to_xp)
    got("d2_m")
    go(dpart(xp, 2, 2), dpart(xp, 2, 2), "d2_rm", to_xm)
    go(u1(xm, 0, 64), u1(xm, 0, 64), "u1_rp", to_xp)
    go(u1(xp, 64, 64), u1(xp, 64, 64), "u1_rm", to_xm)
    weights(0)
    send_v0(1, v0(x, zp))
    relay_v1(1)
    relay_v1(3)
    for g in range(GROUPS // 2, GROUPS):
        picks(g)
    for i in range(5):
        got("xc_%d" % i)
    l_w.wait()

    up_rows, low_rows = pl.ds(0, HALF), pl.ds(HALF, HALF)

    def partials(s, product, far, first, later, near, final):
        far[...] = product(z2).astype(BF16)
        go(far.at[up_rows], first.at[0], "s%d_fp" % s, to_zp)
        go(far.at[low_rows], first.at[1], "s%d_fm" % s, to_zm)
        part = product(zp)
        near[0] = part[HALF:].astype(BF16)
        later[0] = part[:HALF]
        go(near.at[0], final.at[0, low_rows], "s%d_np" % s, to_zp)
        part = product(zm)
        near[1] = part[:HALF].astype(BF16)
        later[1] = part[HALF:]
        go(near.at[1], final.at[1, up_rows], "s%d_nm" % s, to_zm)

    def pass_on(s, first, later, total, final):
        got("s%d_fp" % s)
        total[0] = (later[0] + first[0].astype(F32)).astype(BF16)
        go(total.at[0], final.at[0, up_rows], "s%d_ap" % s, to_zp)
        got("s%d_fm" % s)
        total[1] = (later[1] + first[1].astype(F32)).astype(BF16)
        go(total.at[1], final.at[1, low_rows], "s%d_am" % s, to_zm)

    def arrived(s):
        got("s%d_np" % s, "s%d_nm" % s, "s%d_ap" % s, "s%d_am" % s)

    def base_part(j):
        def product(block):
            return jnp.dot(
                xb[block], wb[j].reshape(4 * PAD, OUT), preferred_element_type=F32
            )

        partials(j, product, bfar.at[j], bfirst.at[j], blater.at[j], bnear.at[j], bfinal.at[j])
        bown[j] = product(z)

    def base_pass(j):
        pass_on(j, bfirst.at[j], blater.at[j], bsum.at[j], bfinal.at[j])

    def base_done(j):
        arrived(j)
        base_out[j] = (
            bown[j] + bfinal[j, 0].astype(F32) + bfinal[j, 1].astype(F32)
        ) * scale

    def rank_product(block):
        return jnp.dot(xb[block], db[...].reshape(4 * PAD, 512), preferred_element_type=F32)

    got("w1_bp", "w1_am", "w1_rp", "w1_rm")
    base_part(1)
    got("d2_rp", "d2_rm")
    partials(2, rank_product, rfar, rfirst, rlater, rnear, rfinal)
    rown[...] = rank_product(z)
    base_pass(1)
    got("u0_rp", "u0_rm", "u1_rp", "u1_rm")
    send_v1(2, v1(x2, z))
    relay_weights(0)
    send_v0(3, v0(x, zm))
    send_v0(2, v0(x, z2))
    relay_v0(0)
    relay_v0(1)
    pass_on(2, rfirst, rlater, rsum, rfinal)

    total = ss_own[...]
    for i in range(7):
        got("ss_%d" % i)
        total += ss_all[i]
    scale = to_col(lax.rsqrt(total[0:1, :] / (FEAT * 8) + 1e-05), TOK)
    base_done(1)
    relay_v1(2)

    def ranks(yo, a, n):
        return rank_all.at[yo, core, pl.ds(a, n)]

    arrived(2)
    rank_all[y, core] = (
        (rown[...] + rfinal[0].astype(F32) + rfinal[1].astype(F32)) * scale
    ).astype(BF16)
    go(ranks(y, 0, TOK), ranks(y, 0, TOK), "ra_p", to_yp)
    go(ranks(y, 0, TOK), ranks(y, 0, TOK), "ra_m", to_ym)
    go(ranks(y, 0, TOK), ranks(y, 0, TOK), "ra_c0", to_other)

    got("w0_bp", "w0_am", "w0_rp", "w0_rm")
    base_part(0)

    relay_v0(3)
    relay_v0(2)
    got("ra_p")
    go(ranks(ym, 0, HALF), ranks(ym, 0, HALF), "ra_rp", to_yp)
    go(ranks(ym, 0, TOK), ranks(ym, 0, TOK), "ra_c1", to_other)
    got("ra_m")
    go(ranks(yp, HALF, HALF), ranks(yp, HALF, HALF), "ra_rm", to_ym)
    go(ranks(yp, 0, TOK), ranks(yp, 0, TOK), "ra_c2", to_other)
    base_pass(0)
    got("ra_rp")
    go(ranks(y2, 0, HALF), ranks(y2, 0, HALF), "ra_c3", to_other)
    got("ra_rm")
    go(ranks(y2, HALF, HALF), ranks(y2, HALF, HALF), "ra_c4", to_other)

    for k in range(4):
        finish(1, k)
    for i in range(5):
        got("ra_c%d" % i)
    l_u.wait()
    blend(up_all, rank_all, base_out, mix, 1, range(16))

    def group(i, carry):
        for n in range(2):
            at = pl.multiple_of(32 * i + 16 * n, 16)
            done[pl.ds(at, 16)] = place(pick, mix, 2 * i + n)
        return carry

    lax.fori_loop(0, GROUPS // 2, group, 0)
    base_done(0)
    for k in range(4):
        finish(0, k)
    for own, cp in some:

        @pl.when(jnp.logical_not(own))
        def _():
            cp.wait_send()

    for cp in sends:
        cp.wait_send()


def combine(up, rank, base, pick, done, q_out, v_out, mix, obuf, osem, dsem):
    whole = pltpu.make_async_copy(done, v_out, dsem.at[0])
    whole.start()
    blend(up, rank, base, mix, 0, range(16))

    def put(i, slot):
        return pltpu.make_async_copy(
            obuf.at[slot], q_out.at[pl.ds(32 * i, 32)], osem.at[slot]
        )

    def group(i, carry):
        slot = lax.rem(i, 2)

        @pl.when(i >= 2)
        def _():
            put(i - 2, slot).wait()

        for n in range(2):
            obuf[slot, 16 * n : 16 * (n + 1)] = place(pick, mix, 2 * i + n)
        put(i, slot).start()
        return carry

    lax.fori_loop(0, GROUPS // 2, group, 0)
    for i in (GROUPS // 2 - 2, GROUPS // 2 - 1):
        put(i, i % 2).wait()
    whole.wait()


def stay(array):
    return pltpu.with_memory_space_constraint(array, pltpu.HBM)


def body(
    prompt_token_states,
    gain,
    projection_weight,
    adapter_down_maps,
    adapter_up_maps,
    prompt_token_length,
    prompt_of_request,
    adapter_of_request,
    adapter_slot_index,
):
    weight = jnp.transpose(projection_weight, (1, 0, 2))
    vmem = pl.BlockSpec(memory_space=pltpu.VMEM)
    hbm = pl.BlockSpec(memory_space=pltpu.HBM)
    anyw = pl.BlockSpec(memory_space=pl.ANY)
    lens = prompt_token_length.reshape(1, -1)
    por = prompt_of_request.reshape(1, -1)
    aor = adapter_of_request.reshape(1, -1)
    asi = adapter_slot_index.reshape(1, -1)
    gathered = pl.pallas_call(
        exchange,
        out_shape=(
            jax.ShapeDtypeStruct((4, 4, 2, RANK, OUT), BF16),
            jax.ShapeDtypeStruct((4, 2, TOK, 512), BF16),
            jax.ShapeDtypeStruct((2, TOK, OUT), F32),
            jax.ShapeDtypeStruct((GROUPS, 256, 256), BF16),
            jax.ShapeDtypeStruct((TOK, SLOTS, OUT), BF16),
        ),
        in_specs=[hbm, hbm, anyw, hbm, hbm, hbm, hbm, hbm, hbm],
        out_specs=(vmem, vmem, vmem, vmem, vmem),
        scratch_shapes=[
            pltpu.VMEM((TOK, FEAT), BF16),
            pltpu.VMEM((FEAT,), BF16),
            pltpu.VMEM(lens.shape, jnp.int32),
            pltpu.VMEM(por.shape, jnp.int32),
            pltpu.VMEM(aor.shape, jnp.int32),
            pltpu.VMEM(asi.shape, jnp.int32),
            pltpu.VMEM((TOK, FEAT), BF16),
            pltpu.VMEM((4, TOK, 4 * PAD), BF16),
            pltpu.VMEM((2, 4, PAD, OUT), BF16),
            pltpu.VMEM((4, BLK, RANK), BF16),
            pltpu.VMEM((4, PAD, 512), BF16),
            pltpu.VMEM((2, TOK, OUT), BF16),
            pltpu.VMEM((2, 2, HALF, OUT), BF16),
            pltpu.VMEM((2, 2, HALF, OUT), F32),
            pltpu.VMEM((2, 2, HALF, OUT), BF16),
            pltpu.VMEM((2, 2, HALF, OUT), BF16),
            pltpu.VMEM((2, 2, TOK, OUT), BF16),
            pltpu.VMEM((2, TOK, OUT), F32),
            pltpu.VMEM((TOK, 512), BF16),
            pltpu.VMEM((2, HALF, 512), BF16),
            pltpu.VMEM((2, HALF, 512), F32),
            pltpu.VMEM((2, HALF, 512), BF16),
            pltpu.VMEM((2, HALF, 512), BF16),
            pltpu.VMEM((2, TOK, 512), BF16),
            pltpu.VMEM((TOK, 512), F32),
            pltpu.VMEM((8, TOK), F32),
            pltpu.VMEM((7, 8, TOK), F32),
            pltpu.VMEM((GROUPS, 256, OUT), BF16),
            pltpu.SemaphoreType.DMA((NSEM,)),
            pltpu.SemaphoreType.DMA((NSEM,)),
            pltpu.SemaphoreType.DMA((9,)),
        ],
        compiler_params=pltpu.CompilerParams(
            collective_id=0, has_side_effects=True, vmem_limit_bytes=27 << 20
        ),
        name="exchange",
    )(
        stay(prompt_token_states),
        stay(gain),
        weight,
        stay(adapter_down_maps.reshape(FEAT, 2 * RANK)),
        stay(adapter_up_maps.reshape(2, RANK, OUT)),
        stay(lens),
        stay(por),
        stay(aor),
        stay(asi),
    )
    return pl.pallas_call(
        combine,
        out_shape=(
            jax.ShapeDtypeStruct((TOK, SLOTS, OUT), BF16),
            jax.ShapeDtypeStruct((TOK, SLOTS, OUT), BF16),
        ),
        in_specs=[vmem] * 5,
        out_specs=(anyw, anyw),
        scratch_shapes=[
            pltpu.VMEM((GROUPS, 256, OUT), BF16),
            pltpu.VMEM((2, 32, SLOTS, OUT), BF16),
            pltpu.SemaphoreType.DMA((2,)),
            pltpu.SemaphoreType.DMA((1,)),
        ],
        compiler_params=pltpu.CompilerParams(vmem_limit_bytes=20 << 20),
        name="combine",
    )(*gathered)


def solution(mesh):
    placed = (
        P("col", "row"),
        P("row"),
        P("col", None, "row"),
        P("col", "row", None),
        P("col", None, None, "row"),
        P(),
        P(),
        P(),
        P(),
    )
    return jax.shard_map(
        body,
        mesh=mesh,
        in_specs=placed,
        out_specs=(P("col", None, "row"), P("col", None, "row")),
        check_vma=False,
    )
```

```python
import functools

import jax
import jax.numpy as jnp
from jax import lax
from jax.experimental import pallas as pl
from jax.experimental.pallas import tpu as pltpu
from jax.sharding import PartitionSpec as P

F32 = jnp.float32
BF16 = jnp.bfloat16
MESH = pl.DeviceIdType.MESH

SLOTS = 16
TOK = 224
HALF = 112
FEAT = 640
BLK = 320
PAD = 384
OUT = 640
RANK = 128
GROUPS = 14

NAMES = (
    ["x1_%d" % i for i in range(4)]
    + ["d1_%d" % i for i in range(4)]
    + ["db_%d" % i for i in range(4)]
    + ["ss_%d" % i for i in range(7)]
    + ["w%d_%s" % (j, s) for j in range(2) for s in ("ap", "bp", "am", "bm", "rp", "rm")]
    + ["x2_%s" % s for s in ("p", "m", "rp", "rm")]
    + ["xc_%d" % i for i in range(5)]
    + ["d2_%s" % s for s in ("p", "m", "rp", "rm")]
    + ["u%d_%s" % (j, s) for j in range(2) for s in ("p", "m", "rp", "rm")]
    + ["v%d_%d_%s" % (j, k, s) for j in range(2) for k in range(4) for s in ("p", "m", "r")]
    + ["s%d_%s" % (j, s) for j in range(3) for s in ("fp", "fm", "np", "nm", "ap", "am")]
    + ["ra_%s" % s for s in ("p", "m", "rp", "rm", "c0", "c1", "c2", "c3", "c4")]
)
SEM = {name: i for i, name in enumerate(NAMES)}
NSEM = len(NAMES)


def to_col(row, n):
    same = lax.broadcasted_iota(jnp.int32, (n, n), 0) == lax.broadcasted_iota(jnp.int32, (n, n), 1)
    return jnp.sum(jnp.where(same, jnp.broadcast_to(row, (n, n)), 0.0), axis=1, keepdims=True)


def iota(shape, axis):
    return lax.broadcasted_iota(jnp.int32, shape, axis)


def targets(len_ref, por_ref, aor_ref, asi_ref, first_token):
    lens = len_ref[...].astype(F32)
    por = por_ref[...].astype(F32)
    aor = aor_ref[...].astype(F32)
    asi = asi_ref[...].astype(F32)
    n_prompt = lens.shape[1]
    n_req = por.shape[1]
    n_lib = asi.shape[1]
    before = jnp.sum(
        jnp.where(to_col(por, n_req) < por, 1.0, 0.0), axis=0, keepdims=True
    )
    position = iota((1, n_req), 1).astype(F32) - before
    hot = iota((n_lib, n_req), 0).astype(F32) == aor
    slot = jnp.sum(
        jnp.where(hot, jnp.broadcast_to(to_col(asi, n_lib), (n_lib, n_req)), 0.0),
        axis=0,
        keepdims=True,
    )
    by_prompt = jnp.where(iota((16, n_req), 0).astype(F32) == por, slot + 1.0, 0.0)
    by_place = jnp.where(iota((16, n_req), 0).astype(F32) == position, 1.0, 0.0)
    table = lax.dot_general(
        by_prompt.astype(BF16),
        by_place.astype(BF16),
        (((1,), (1,)), ((), ())),
        preferred_element_type=F32,
    )
    spread = jnp.where(iota((16, 256), 0) == iota((16, 256), 1) % 16, 1.0, 0.0)
    table = jnp.dot(table.astype(BF16), spread.astype(BF16), preferred_element_type=F32)
    ends = jnp.sum(
        jnp.where(
            iota((n_prompt, n_prompt), 0) <= iota((n_prompt, n_prompt), 1),
            jnp.broadcast_to(to_col(lens, n_prompt), (n_prompt, n_prompt)),
            0.0,
        ),
        axis=0,
        keepdims=True,
    )
    in_group = iota((16, 256), 1) // 16
    token = (first_token + 16 * iota((16, 256), 0) + in_group).astype(F32)
    prompt = jnp.zeros((16, 256), F32)
    for p in range(n_prompt):
        prompt += jnp.where(token >= ends[:, p : p + 1], 1.0, 0.0)
    chosen = jnp.zeros((16, 256), F32)
    for p in range(n_prompt):
        chosen += jnp.where(prompt == float(p), jnp.broadcast_to(table[p : p + 1, :], (16, 256)), 0.0)
    return jnp.where(chosen > 0.5, (chosen - 1.0) * 16.0 + in_group.astype(F32), -1.0)


def blend(up, rank, base, mix, j, adapters):
    for a in adapters:
        xo, zo = a // 4, a % 4
        delta = jnp.dot(
            rank[zo, j, :, RANK * xo : RANK * (xo + 1)],
            up[xo, zo, j],
            preferred_element_type=F32,
        )
        full = (base[j] + delta).astype(BF16)
        mix[:, 16 * a : 16 * (a + 1), :] = full.reshape(GROUPS, 16, OUT)


def place(pick, mix, g):
    rows = jnp.dot(pick[g], mix[g], preferred_element_type=F32).astype(BF16)
    return rows.reshape(16, SLOTS, OUT)


def exchange(
    x_hbm, gain_hbm, w_ref, d_ref, up_ref, len_hbm, por_hbm, aor_hbm, asi_hbm,
    up_all, rank_all, base_out, pick, done,
    xv, gainv, lenv, porv, aorv, asiv,
    xg, xb, wb, da, db, bfar, bfirst, blater, bnear, bsum, bfinal, bown,
    rfar, rfirst, rlater, rnear, rsum, rfinal, rown, ss_own, ss_all, mix,
    ssem, rsem, lsem,
):
    r = lax.axis_index("row")
    c = lax.axis_index("col")
    y, core = lax.div(r, 2), lax.rem(r, 2)
    x, z = lax.div(c, 4), lax.rem(c, 4)

    def dev(x_, y_, z_, core_):
        return (y_ * 2 + core_, x_ * 4 + z_)

    def mod4(v):
        return lax.rem(v + 8, 4)

    def rc(src, dst, send, to, recv=None):
        return pltpu.make_async_remote_copy(
            src_ref=src,
            dst_ref=dst,
            send_sem=ssem.at[SEM[send]],
            recv_sem=rsem.at[SEM[send] if recv is None else recv],
            device_id=to,
            device_id_type=MESH,
        )

    xp, xm, x2 = mod4(x + 1), mod4(x - 1), mod4(x + 2)
    yp, ym, y2 = mod4(y + 1), mod4(y - 1), mod4(y + 2)
    zp, zm, z2 = mod4(z + 1), mod4(z - 1), mod4(z + 2)
    to_xp, to_xm = dev(xp, y, z, core), dev(xm, y, z, core)
    to_yp, to_ym = dev(x, yp, z, core), dev(x, ym, z, core)
    to_zp, to_zm = dev(x, y, zp, core), dev(x, y, zm, core)
    to_other = dev(x, y, z, 1 - core)
    copies = {}
    sends = []

    def go(src, dst, name, to):
        cp = rc(src, dst, name, to)
        cp.start()
        copies[name] = cp
        sends.append(cp)

    def got(*names):
        for name in names:
            copies[name].wait_recv()

    barrier = pltpu.get_barrier_semaphore()

    partners = [to_xp, to_xm, to_other]
    for k in range(1, 4):
        for other in (core, 1 - core):
            partners.append(dev(x, y, mod4(z + k), other))
            partners.append(dev(x, mod4(y + k), z, other))
    for partner in partners:
        pl.semaphore_signal(barrier, inc=1, device_id=partner, device_id_type=MESH)

    l_x = pltpu.make_async_copy(x_hbm, xv, lsem.at[0])
    l_x.start()
    l_g = pltpu.make_async_copy(gain_hbm, gainv, lsem.at[8])
    l_g.start()
    l_small = []
    for i, (a, b) in enumerate(
        ((len_hbm, lenv), (por_hbm, porv), (aor_hbm, aorv), (asi_hbm, asiv))
    ):
        l_small.append(pltpu.make_async_copy(a, b, lsem.at[1 + i]))
        l_small[-1].start()

    odd = lax.rem(z, 2)
    off = pl.multiple_of(64 * odd, 64)
    pad_at = pl.multiple_of(BLK * (1 - odd), 64)
    for b in range(4):
        for j in range(2):
            wb[j, b, pl.ds(pad_at, 64), :] = jnp.zeros((64, OUT), BF16)
        db[b, pl.ds(pad_at, 64), :] = jnp.zeros((64, 512), BF16)

    l_x.wait()
    l_g.wait()
    states = xv[...].astype(F32)
    xg[...] = (states * gainv[...].astype(F32).reshape(1, FEAT)).astype(BF16)
    ss_own[...] = lax.dot_general(
        jnp.ones((8, FEAT), F32),
        states * states,
        (((1,), (1,)), ((), ())),
        precision=lax.Precision.HIGHEST,
        preferred_element_type=F32,
    )
    pl.semaphore_wait(barrier, len(partners))

    def u1(xo, a, n):
        return up_all.at[xo, z, 1, pl.ds(a, n), :]

    def u0(zo, a, n):
        return up_all.at[x, zo, 0, pl.ds(a, n), :]

    go(up_ref.at[1], u1(x, 0, 128), "u1_p", to_xp)
    go(up_ref.at[1], u1(x, 0, 128), "u1_m", to_xm)

    def wslot(j, xo, a):
        return wb.at[j, xo, pl.ds(pl.multiple_of(off + a, 32), 160), :]

    def weights(j):
        go(w_ref.at[j, pl.ds(0, 160), :], wslot(j, x, 0), "w%d_ap" % j, to_xp)
        go(w_ref.at[j, pl.ds(160, 160), :], wslot(j, x, 160), "w%d_bm" % j, to_xm)
        go(w_ref.at[j, pl.ds(160, 160), :], wslot(j, x, 160), "w%d_bp" % j, to_xp)
        go(w_ref.at[j, pl.ds(0, 160), :], wslot(j, x, 0), "w%d_am" % j, to_xm)

    def relay_weights(j):
        got("w%d_ap" % j)
        go(wslot(j, xm, 0), wslot(j, xm, 0), "w%d_rp" % j, to_xp)
        got("w%d_bm" % j)
        go(wslot(j, xp, 160), wslot(j, xp, 160), "w%d_rm" % j, to_xm)

    weights(1)

    some = []
    for h in range(2):
        for k in range(2):
            zd = 2 * core + h
            src = d_ref.at[pl.ds(BLK * h, BLK), pl.ds(RANK * k, RANK)]
            dst = da.at[z]
            own = jnp.logical_and(zd == z, core == k)
            sem = SEM["d1_0"] + z
            cp = rc(src, dst, "d1_%d" % (2 * h + k), dev(x, y, zd, k), sem)
            some.append((own, cp))

            @pl.when(jnp.logical_not(own))
            def _():
                cp.start()

            @pl.when(own)
            def _():
                pltpu.make_async_copy(src, dst, rsem.at[sem]).start()

    for h in range(2):
        for k in range(2):
            zd = 2 * core + h
            src = xg.at[pl.ds(HALF * k, HALF), pl.ds(256 * h, PAD)]
            dst = xb.at[z, pl.ds(HALF * k, HALF), pl.ds(pl.multiple_of(PAD * y, 128), PAD)]
            own = jnp.logical_and(zd == z, core == k)
            sem = SEM["x1_0"] + z
            cp = rc(src, dst, "x1_%d" % (2 * h + k), dev(x, y, zd, k), sem)
            some.append((own, cp))

            @pl.when(jnp.logical_not(own))
            def _():
                cp.start()

            @pl.when(own)
            def _():
                pltpu.make_async_copy(src, dst, rsem.at[sem]).start()

    for i in range(1, 8):
        go(ss_own, ss_all.at[i - 1], "ss_%d" % (i - 1), (lax.rem(r + i, 8), c))

    go(up_ref.at[0], u0(z, 0, 128), "u0_p", to_zp)
    go(up_ref.at[0], u0(z, 0, 128), "u0_m", to_zm)

    def v1(xo, zo):
        return up_all.at[xo, zo, 1]

    def v0(xo, zo):
        return up_all.at[xo, zo, 0]

    def send_v1(k, src):
        xo = mod4(x + k)
        go(src, v1(xo, z), "v1_%d_p" % k, to_zp)
        go(src, v1(xo, z), "v1_%d_m" % k, to_zm)

    def relay_v1(k):
        xo = mod4(x + k)
        if k < 2:
            got("v1_%d_p" % k)
            go(v1(xo, zm), v1(xo, zm), "v1_%d_r" % k, to_zp)
        else:
            got("v1_%d_m" % k)
            go(v1(xo, zp), v1(xo, zp), "v1_%d_r" % k, to_zm)

    def send_v0(k, src):
        zo = mod4(z + k)
        go(src, v0(x, zo), "v0_%d_p" % k, to_xp)
        go(src, v0(x, zo), "v0_%d_m" % k, to_xm)

    def relay_v0(k):
        zo = mod4(z + k)
        if k < 2:
            got("v0_%d_p" % k)
            go(v0(xm, zo), v0(xm, zo), "v0_%d_r" % k, to_xp)
        else:
            got("v0_%d_m" % k)
            go(v0(xp, zo), v0(xp, zo), "v0_%d_r" % k, to_xm)

    def finish(j, k):
        got("v%d_%d_%s" % (j, k, "m" if k < 2 else "p"), "v%d_%d_r" % (j, k))

    send_v1(0, up_ref.at[1])

    l_w = pltpu.make_async_copy(w_ref, wb.at[:, x, pl.ds(off, BLK), :], lsem.at[5])
    l_w.start()
    l_u = pltpu.make_async_copy(up_ref, up_all.at[x, z], lsem.at[6])
    l_u.start()

    def dcols(xo):
        return pl.ds(pl.multiple_of(RANK * xo, 128), RANK)

    for zs in range(4):
        rc(da.at[zs], da.at[zs], "d1_0", to_other, SEM["d1_0"] + zs).wait_recv()
    for k in range(1, 4):
        yd = mod4(y + k)
        go(da.at[yd], db.at[y, pl.ds(off, BLK), dcols(x)], "db_%d" % k, dev(x, yd, z, core))
    l_d = pltpu.make_async_copy(da.at[y], db.at[y, pl.ds(off, BLK), dcols(x)], lsem.at[7])
    l_d.start()

    def unit(yo, a, n):
        return xb.at[
            pl.ds(a, n),
            pl.ds(pl.multiple_of(HALF * core, 16), HALF),
            pl.ds(pl.multiple_of(PAD * yo, 128), PAD),
        ]

    for zs in range(4):
        piece = xb.at[
            zs,
            pl.ds(pl.multiple_of(HALF * core, 16), HALF),
            pl.ds(pl.multiple_of(PAD * y, 128), PAD),
        ]
        rc(piece, piece, "x1_0", to_other, SEM["x1_0"] + zs).wait_recv()
    go(unit(y, 0, 4), unit(y, 0, 4), "x2_p", to_yp)
    go(unit(y, 0, 4), unit(y, 0, 4), "x2_m", to_ym)
    go(unit(y, 0, 4), unit(y, 0, 4), "xc_0", to_other)

    got("u1_p", "u1_m")
    send_v1(1, v1(xp, z))
    send_v1(3, v1(xm, z))

    def dpart(xo, a, n):
        return db.at[pl.ds(a, n), pl.ds(off, BLK), dcols(xo)]

    l_d.wait()
    got("db_1", "db_2", "db_3")
    go(dpart(x, 0, 4), dpart(x, 0, 4), "d2_p", to_xp)
    go(dpart(x, 0, 4), dpart(x, 0, 4), "d2_m", to_xm)
    send_v0(0, up_ref.at[0])
    got("u0_p", "u0_m")
    go(u0(zm, 0, 64), u0(zm, 0, 64), "u0_rp", to_zp)
    go(u0(zp, 64, 64), u0(zp, 64, 64), "u0_rm", to_zm)
    relay_weights(1)

    for cp in l_small:
        cp.wait()
    tgt = targets(lenv, porv, aorv, asiv, c * TOK)

    def picks(g):
        hit = jnp.where(
            iota((256, 256), 0).astype(F32) == tgt[g : g + 1, :], 1.0, 0.0
        )
        pick[g] = hit.T.astype(BF16)

    got("x2_p")
    go(unit(ym, 0, 2), unit(ym, 0, 2), "x2_rp", to_yp)
    go(unit(ym, 0, 4), unit(ym, 0, 4), "xc_1", to_other)
    got("x2_m")
    go(unit(yp, 2, 2), unit(yp, 2, 2), "x2_rm", to_ym)
    go(unit(yp, 0, 4), unit(yp, 0, 4), "xc_2", to_other)
    relay_v1(0)
    for g in range(GROUPS // 2):
        picks(g)
    got("x2_rp")
    go(unit(y2, 0, 2), unit(y2, 0, 2), "xc_3", to_other)
    got("x2_rm")
    go(unit(y2, 2, 2), unit(y2, 2, 2), "xc_4", to_other)
    got("d2_p")
    go(dpart(xm, 0, 2), dpart(xm, 0, 2), "d2_rp", to_xp)
    got("d2_m")
    go(dpart(xp, 2, 2), dpart(xp, 2, 2), "d2_rm", to_xm)
    go(u1(xm, 0, 64), u1(xm, 0, 64), "u1_rp", to_xp)
    go(u1(xp, 64, 64), u1(xp, 64, 64), "u1_rm", to_xm)
    weights(0)
    send_v0(1, v0(x, zp))
    relay_v1(1)
    relay_v1(3)
    for g in range(GROUPS // 2, GROUPS):
        picks(g)
    for i in range(5):
        got("xc_%d" % i)
    l_w.wait()

    up_rows, low_rows = pl.ds(0, HALF), pl.ds(HALF, HALF)

    def partials(s, product, far, first, later, near, final):
        far[...] = product(z2).astype(BF16)
        go(far.at[up_rows], first.at[0], "s%d_fp" % s, to_zp)
        go(far.at[low_rows], first.at[1], "s%d_fm" % s, to_zm)
        part = product(zp)
        near[0] = part[HALF:].astype(BF16)
        later[0] = part[:HALF]
        go(near.at[0], final.at[0, low_rows], "s%d_np" % s, to_zp)
        part = product(zm)
        near[1] = part[:HALF].astype(BF16)
        later[1] = part[HALF:]
        go(near.at[1], final.at[1, up_rows], "s%d_nm" % s, to_zm)

    def pass_on(s, first, later, total, final):
        got("s%d_fp" % s)
        total[0] = (later[0] + first[0].astype(F32)).astype(BF16)
        go(total.at[0], final.at[0, up_rows], "s%d_ap" % s, to_zp)
        got("s%d_fm" % s)
        total[1] = (later[1] + first[1].astype(F32)).astype(BF16)
        go(total.at[1], final.at[1, low_rows], "s%d_am" % s, to_zm)

    def arrived(s):
        got("s%d_np" % s, "s%d_nm" % s, "s%d_ap" % s, "s%d_am" % s)

    def base_part(j):
        def product(block):
            return jnp.dot(
                xb[block], wb[j].reshape(4 * PAD, OUT), preferred_element_type=F32
            )

        partials(j, product, bfar.at[j], bfirst.at[j], blater.at[j], bnear.at[j], bfinal.at[j])
        bown[j] = product(z)

    def base_pass(j):
        pass_on(j, bfirst.at[j], blater.at[j], bsum.at[j], bfinal.at[j])

    def base_done(j):
        arrived(j)
        base_out[j] = (
            bown[j] + bfinal[j, 0].astype(F32) + bfinal[j, 1].astype(F32)
        ) * scale

    def rank_product(block):
        return jnp.dot(xb[block], db[...].reshape(4 * PAD, 512), preferred_element_type=F32)

    got("w1_bp", "w1_am", "w1_rp", "w1_rm")
    base_part(1)
    got("d2_rp", "d2_rm")
    partials(2, rank_product, rfar, rfirst, rlater, rnear, rfinal)
    rown[...] = rank_product(z)
    base_pass(1)
    got("u0_rp", "u0_rm", "u1_rp", "u1_rm")
    relay_weights(0)
    send_v0(3, v0(x, zm))
    send_v0(2, v0(x, z2))
    relay_v0(0)
    relay_v0(1)
    pass_on(2, rfirst, rlater, rsum, rfinal)
    send_v1(2, v1(x2, z))

    total = ss_own[...]
    for i in range(7):
        got("ss_%d" % i)
        total += ss_all[i]
    scale = to_col(lax.rsqrt(total[0:1, :] / (FEAT * 8) + 1e-05), TOK)

    def ranks(yo, a, n):
        return rank_all.at[yo, core, pl.ds(a, n)]

    arrived(2)
    rank_all[y, core] = (
        (rown[...] + rfinal[0].astype(F32) + rfinal[1].astype(F32)) * scale
    ).astype(BF16)
    go(ranks(y, 0, TOK), ranks(y, 0, TOK), "ra_p", to_yp)
    go(ranks(y, 0, TOK), ranks(y, 0, TOK), "ra_m", to_ym)
    go(ranks(y, 0, TOK), ranks(y, 0, TOK), "ra_c0", to_other)

    base_done(1)
    relay_v1(2)
    got("w0_bp", "w0_am", "w0_rp", "w0_rm")
    base_part(0)

    relay_v0(3)
    relay_v0(2)
    got("ra_p")
    go(ranks(ym, 0, HALF), ranks(ym, 0, HALF), "ra_rp", to_yp)
    go(ranks(ym, 0, TOK), ranks(ym, 0, TOK), "ra_c1", to_other)
    got("ra_m")
    go(ranks(yp, HALF, HALF), ranks(yp, HALF, HALF), "ra_rm", to_ym)
    go(ranks(yp, 0, TOK), ranks(yp, 0, TOK), "ra_c2", to_other)
    base_pass(0)
    got("ra_rp")
    go(ranks(y2, 0, HALF), ranks(y2, 0, HALF), "ra_c3", to_other)
    got("ra_rm")
    go(ranks(y2, HALF, HALF), ranks(y2, HALF, HALF), "ra_c4", to_other)

    for k in range(4):
        finish(1, k)
    for i in range(5):
        got("ra_c%d" % i)
    l_u.wait()
    blend(up_all, rank_all, base_out, mix, 1, range(16))

    def group(i, carry):
        for n in range(2):
            at = pl.multiple_of(32 * i + 16 * n, 16)
            done[pl.ds(at, 16)] = place(pick, mix, 2 * i + n)
        return carry

    lax.fori_loop(0, GROUPS // 2, group, 0)
    base_done(0)
    for k in range(4):
        finish(0, k)
    for own, cp in some:

        @pl.when(jnp.logical_not(own))
        def _():
            cp.wait_send()

    for cp in sends:
        cp.wait_send()


def combine(up, rank, base, pick, done, q_out, v_out, mix, obuf, osem, dsem):
    whole = pltpu.make_async_copy(done, v_out, dsem.at[0])
    whole.start()
    blend(up, rank, base, mix, 0, range(16))

    def put(i, slot):
        return pltpu.make_async_copy(
            obuf.at[slot], q_out.at[pl.ds(32 * i, 32)], osem.at[slot]
        )

    def group(i, carry):
        slot = lax.rem(i, 2)

        @pl.when(i >= 2)
        def _():
            put(i - 2, slot).wait()

        for n in range(2):
            obuf[slot, 16 * n : 16 * (n + 1)] = place(pick, mix, 2 * i + n)
        put(i, slot).start()
        return carry

    lax.fori_loop(0, GROUPS // 2, group, 0)
    for i in (GROUPS // 2 - 2, GROUPS // 2 - 1):
        put(i, i % 2).wait()
    whole.wait()


def stay(array):
    return pltpu.with_memory_space_constraint(array, pltpu.HBM)


def body(
    prompt_token_states,
    gain,
    projection_weight,
    adapter_down_maps,
    adapter_up_maps,
    prompt_token_length,
    prompt_of_request,
    adapter_of_request,
    adapter_slot_index,
):
    weight = jnp.transpose(projection_weight, (1, 0, 2))
    vmem = pl.BlockSpec(memory_space=pltpu.VMEM)
    hbm = pl.BlockSpec(memory_space=pltpu.HBM)
    anyw = pl.BlockSpec(memory_space=pl.ANY)
    lens = prompt_token_length.reshape(1, -1)
    por = prompt_of_request.reshape(1, -1)
    aor = adapter_of_request.reshape(1, -1)
    asi = adapter_slot_index.reshape(1, -1)
    gathered = pl.pallas_call(
        exchange,
        out_shape=(
            jax.ShapeDtypeStruct((4, 4, 2, RANK, OUT), BF16),
            jax.ShapeDtypeStruct((4, 2, TOK, 512), BF16),
            jax.ShapeDtypeStruct((2, TOK, OUT), F32),
            jax.ShapeDtypeStruct((GROUPS, 256, 256), BF16),
            jax.ShapeDtypeStruct((TOK, SLOTS, OUT), BF16),
        ),
        in_specs=[hbm, hbm, anyw, hbm, hbm, hbm, hbm, hbm, hbm],
        out_specs=(vmem, vmem, vmem, vmem, vmem),
        scratch_shapes=[
            pltpu.VMEM((TOK, FEAT), BF16),
            pltpu.VMEM((FEAT,), BF16),
            pltpu.VMEM(lens.shape, jnp.int32),
            pltpu.VMEM(por.shape, jnp.int32),
            pltpu.VMEM(aor.shape, jnp.int32),
            pltpu.VMEM(asi.shape, jnp.int32),
            pltpu.VMEM((TOK, FEAT), BF16),
            pltpu.VMEM((4, TOK, 4 * PAD), BF16),
            pltpu.VMEM((2, 4, PAD, OUT), BF16),
            pltpu.VMEM((4, BLK, RANK), BF16),
            pltpu.VMEM((4, PAD, 512), BF16),
            pltpu.VMEM((2, TOK, OUT), BF16),
            pltpu.VMEM((2, 2, HALF, OUT), BF16),
            pltpu.VMEM((2, 2, HALF, OUT), F32),
            pltpu.VMEM((2, 2, HALF, OUT), BF16),
            pltpu.VMEM((2, 2, HALF, OUT), BF16),
            pltpu.VMEM((2, 2, TOK, OUT), BF16),
            pltpu.VMEM((2, TOK, OUT), F32),
            pltpu.VMEM((TOK, 512), BF16),
            pltpu.VMEM((2, HALF, 512), BF16),
            pltpu.VMEM((2, HALF, 512), F32),
            pltpu.VMEM((2, HALF, 512), BF16),
            pltpu.VMEM((2, HALF, 512), BF16),
            pltpu.VMEM((2, TOK, 512), BF16),
            pltpu.VMEM((TOK, 512), F32),
            pltpu.VMEM((8, TOK), F32),
            pltpu.VMEM((7, 8, TOK), F32),
            pltpu.VMEM((GROUPS, 256, OUT), BF16),
            pltpu.SemaphoreType.DMA((NSEM,)),
            pltpu.SemaphoreType.DMA((NSEM,)),
            pltpu.SemaphoreType.DMA((9,)),
        ],
        compiler_params=pltpu.CompilerParams(
            collective_id=0, has_side_effects=True, vmem_limit_bytes=27 << 20
        ),
        name="exchange",
    )(
        stay(prompt_token_states),
        stay(gain),
        weight,
        stay(adapter_down_maps.reshape(FEAT, 2 * RANK)),
        stay(adapter_up_maps.reshape(2, RANK, OUT)),
        stay(lens),
        stay(por),
        stay(aor),
        stay(asi),
    )
    return pl.pallas_call(
        combine,
        out_shape=(
            jax.ShapeDtypeStruct((TOK, SLOTS, OUT), BF16),
            jax.ShapeDtypeStruct((TOK, SLOTS, OUT), BF16),
        ),
        in_specs=[vmem] * 5,
        out_specs=(anyw, anyw),
        scratch_shapes=[
            pltpu.VMEM((GROUPS, 256, OUT), BF16),
            pltpu.VMEM((2, 32, SLOTS, OUT), BF16),
            pltpu.SemaphoreType.DMA((2,)),
            pltpu.SemaphoreType.DMA((1,)),
        ],
        compiler_params=pltpu.CompilerParams(vmem_limit_bytes=20 << 20),
        name="combine",
    )(*gathered)


def solution(mesh):
    placed = (
        P("col", "row"),
        P("row"),
        P("col", None, "row"),
        P("col", "row", None),
        P("col", None, None, "row"),
        P(),
        P(),
        P(),
        P(),
    )
    return jax.shard_map(
        body,
        mesh=mesh,
        in_specs=placed,
        out_specs=(P("col", None, "row"), P("col", None, "row")),
        check_vma=False,
    )
```

```python
import functools

import jax
import jax.numpy as jnp
from jax import lax
from jax.experimental import pallas as pl
from jax.experimental.pallas import tpu as pltpu
from jax.sharding import PartitionSpec as P

F32 = jnp.float32
BF16 = jnp.bfloat16
MESH = pl.DeviceIdType.MESH

SLOTS = 16
TOK = 224
HALF = 112
FEAT = 640
BLK = 320
PAD = 384
OUT = 640
RANK = 128
GROUPS = 14

NAMES = (
    ["x1_%d" % i for i in range(4)]
    + ["d1_%d" % i for i in range(4)]
    + ["db_%d" % i for i in range(4)]
    + ["ss_%d" % i for i in range(7)]
    + ["w%d_%s" % (j, s) for j in range(2) for s in ("ap", "bp", "am", "bm", "rp", "rm")]
    + ["x2_%s" % s for s in ("p", "m", "rp", "rm")]
    + ["xc_%d" % i for i in range(5)]
    + ["d2_%s" % s for s in ("p", "m", "rp", "rm")]
    + ["u%d_%s" % (j, s) for j in range(2) for s in ("p", "m", "rp", "rm")]
    + ["v%d_%d_%s" % (j, k, s) for j in range(2) for k in range(4) for s in ("p", "m", "r")]
    + ["s%d_%s" % (j, s) for j in range(3) for s in ("fp", "fm", "np", "nm", "ap", "am")]
    + ["ra_%s" % s for s in ("p", "m", "rp", "rm", "c0", "c1", "c2", "c3", "c4")]
)
SEM = {name: i for i, name in enumerate(NAMES)}
NSEM = len(NAMES)


def to_col(row, n):
    same = lax.broadcasted_iota(jnp.int32, (n, n), 0) == lax.broadcasted_iota(jnp.int32, (n, n), 1)
    return jnp.sum(jnp.where(same, jnp.broadcast_to(row, (n, n)), 0.0), axis=1, keepdims=True)


def iota(shape, axis):
    return lax.broadcasted_iota(jnp.int32, shape, axis)


def targets(len_ref, por_ref, aor_ref, asi_ref, first_token):
    lens = len_ref[...].astype(F32)
    por = por_ref[...].astype(F32)
    aor = aor_ref[...].astype(F32)
    asi = asi_ref[...].astype(F32)
    n_prompt = lens.shape[1]
    n_req = por.shape[1]
    n_lib = asi.shape[1]
    before = jnp.sum(
        jnp.where(to_col(por, n_req) < por, 1.0, 0.0), axis=0, keepdims=True
    )
    position = iota((1, n_req), 1).astype(F32) - before
    hot = iota((n_lib, n_req), 0).astype(F32) == aor
    slot = jnp.sum(
        jnp.where(hot, jnp.broadcast_to(to_col(asi, n_lib), (n_lib, n_req)), 0.0),
        axis=0,
        keepdims=True,
    )
    by_prompt = jnp.where(iota((16, n_req), 0).astype(F32) == por, slot + 1.0, 0.0)
    by_place = jnp.where(iota((16, n_req), 0).astype(F32) == position, 1.0, 0.0)
    table = lax.dot_general(
        by_prompt.astype(BF16),
        by_place.astype(BF16),
        (((1,), (1,)), ((), ())),
        preferred_element_type=F32,
    )
    spread = jnp.where(iota((16, 256), 0) == iota((16, 256), 1) % 16, 1.0, 0.0)
    table = jnp.dot(table.astype(BF16), spread.astype(BF16), preferred_element_type=F32)
    ends = jnp.sum(
        jnp.where(
            iota((n_prompt, n_prompt), 0) <= iota((n_prompt, n_prompt), 1),
            jnp.broadcast_to(to_col(lens, n_prompt), (n_prompt, n_prompt)),
            0.0,
        ),
        axis=0,
        keepdims=True,
    )
    in_group = iota((16, 256), 1) // 16
    token = (first_token + 16 * iota((16, 256), 0) + in_group).astype(F32)
    prompt = jnp.zeros((16, 256), F32)
    for p in range(n_prompt):
        prompt += jnp.where(token >= ends[:, p : p + 1], 1.0, 0.0)
    chosen = jnp.zeros((16, 256), F32)
    for p in range(n_prompt):
        chosen += jnp.where(prompt == float(p), jnp.broadcast_to(table[p : p + 1, :], (16, 256)), 0.0)
    return jnp.where(chosen > 0.5, (chosen - 1.0) * 16.0 + in_group.astype(F32), -1.0)


def blend(up, rank, base, mix, j, adapters):
    for a in adapters:
        xo, zo = a // 4, a % 4
        delta = jnp.dot(
            rank[zo, j, :, RANK * xo : RANK * (xo + 1)],
            up[xo, zo, j],
            preferred_element_type=F32,
        )
        full = (base[j] + delta).astype(BF16)
        mix[:, 16 * a : 16 * (a + 1), :] = full.reshape(GROUPS, 16, OUT)


def place(pick, mix, g):
    rows = jnp.dot(pick[g], mix[g], preferred_element_type=F32).astype(BF16)
    return rows.reshape(16, SLOTS, OUT)


def exchange(
    x_hbm, gain_hbm, w_hbm, d_ref, up_ref, len_hbm, por_hbm, aor_hbm, asi_hbm,
    up_all, rank_all, base_out, pick, done,
    w3, w_ref, xv, gainv, lenv, porv, aorv, asiv,
    xg, xb, wb, da, db, bfar, bfirst, blater, bnear, bsum, bfinal, bown,
    rfar, rfirst, rlater, rnear, rsum, rfinal, rown, ss_own, ss_all, mix,
    ssem, rsem, lsem,
):
    r = lax.axis_index("row")
    c = lax.axis_index("col")
    y, core = lax.div(r, 2), lax.rem(r, 2)
    x, z = lax.div(c, 4), lax.rem(c, 4)

    def dev(x_, y_, z_, core_):
        return (y_ * 2 + core_, x_ * 4 + z_)

    def mod4(v):
        return lax.rem(v + 8, 4)

    def rc(src, dst, send, to, recv=None):
        return pltpu.make_async_remote_copy(
            src_ref=src,
            dst_ref=dst,
            send_sem=ssem.at[SEM[send]],
            recv_sem=rsem.at[SEM[send] if recv is None else recv],
            device_id=to,
            device_id_type=MESH,
        )

    xp, xm, x2 = mod4(x + 1), mod4(x - 1), mod4(x + 2)
    yp, ym, y2 = mod4(y + 1), mod4(y - 1), mod4(y + 2)
    zp, zm, z2 = mod4(z + 1), mod4(z - 1), mod4(z + 2)
    to_xp, to_xm = dev(xp, y, z, core), dev(xm, y, z, core)
    to_yp, to_ym = dev(x, yp, z, core), dev(x, ym, z, core)
    to_zp, to_zm = dev(x, y, zp, core), dev(x, y, zm, core)
    to_other = dev(x, y, z, 1 - core)
    copies = {}
    sends = []

    def go(src, dst, name, to):
        cp = rc(src, dst, name, to)
        cp.start()
        copies[name] = cp
        sends.append(cp)

    def got(*names):
        for name in names:
            copies[name].wait_recv()

    barrier = pltpu.get_barrier_semaphore()

    partners = [to_xp, to_xm, to_other]
    for k in range(1, 4):
        for other in (core, 1 - core):
            partners.append(dev(x, y, mod4(z + k), other))
            partners.append(dev(x, mod4(y + k), z, other))
    for partner in partners:
        pl.semaphore_signal(barrier, inc=1, device_id=partner, device_id_type=MESH)

    l_v = pltpu.make_async_copy(w_hbm, w3, lsem.at[9])
    l_v.start()
    l_x = pltpu.make_async_copy(x_hbm, xv, lsem.at[0])
    l_x.start()
    l_g = pltpu.make_async_copy(gain_hbm, gainv, lsem.at[8])
    l_g.start()
    l_small = []
    for i, (a, b) in enumerate(
        ((len_hbm, lenv), (por_hbm, porv), (aor_hbm, aorv), (asi_hbm, asiv))
    ):
        l_small.append(pltpu.make_async_copy(a, b, lsem.at[1 + i]))
        l_small[-1].start()

    odd = lax.rem(z, 2)
    off = pl.multiple_of(64 * odd, 64)
    pad_at = pl.multiple_of(BLK * (1 - odd), 64)
    for b in range(4):
        for j in range(2):
            wb[j, b, pl.ds(pad_at, 64), :] = jnp.zeros((64, OUT), BF16)
        db[b, pl.ds(pad_at, 64), :] = jnp.zeros((64, 512), BF16)

    l_v.wait()
    for j in (1, 0):
        w_ref[j] = w3[:, j, :]
    l_x.wait()
    l_g.wait()
    states = xv[...].astype(F32)
    xg[...] = (states * gainv[...].astype(F32).reshape(1, FEAT)).astype(BF16)
    ss_own[...] = lax.dot_general(
        jnp.ones((8, FEAT), F32),
        states * states,
        (((1,), (1,)), ((), ())),
        precision=lax.Precision.HIGHEST,
        preferred_element_type=F32,
    )
    pl.semaphore_wait(barrier, len(partners))

    def u1(xo, a, n):
        return up_all.at[xo, z, 1, pl.ds(a, n), :]

    def u0(zo, a, n):
        return up_all.at[x, zo, 0, pl.ds(a, n), :]

    go(up_ref.at[1], u1(x, 0, 128), "u1_p", to_xp)
    go(up_ref.at[1], u1(x, 0, 128), "u1_m", to_xm)

    def wslot(j, xo, a):
        return wb.at[j, xo, pl.ds(pl.multiple_of(off + a, 32), 160), :]

    def weights(j):
        go(w_ref.at[j, pl.ds(0, 160), :], wslot(j, x, 0), "w%d_ap" % j, to_xp)
        go(w_ref.at[j, pl.ds(160, 160), :], wslot(j, x, 160), "w%d_bm" % j, to_xm)
        go(w_ref.at[j, pl.ds(160, 160), :], wslot(j, x, 160), "w%d_bp" % j, to_xp)
        go(w_ref.at[j, pl.ds(0, 160), :], wslot(j, x, 0), "w%d_am" % j, to_xm)

    def relay_weights(j):
        got("w%d_ap" % j)
        go(wslot(j, xm, 0), wslot(j, xm, 0), "w%d_rp" % j, to_xp)
        got("w%d_bm" % j)
        go(wslot(j, xp, 160), wslot(j, xp, 160), "w%d_rm" % j, to_xm)

    weights(1)

    some = []
    for h in range(2):
        for k in range(2):
            zd = 2 * core + h
            src = d_ref.at[pl.ds(BLK * h, BLK), pl.ds(RANK * k, RANK)]
            dst = da.at[z]
            own = jnp.logical_and(zd == z, core == k)
            sem = SEM["d1_0"] + z
            cp = rc(src, dst, "d1_%d" % (2 * h + k), dev(x, y, zd, k), sem)
            some.append((own, cp))

            @pl.when(jnp.logical_not(own))
            def _():
                cp.start()

            @pl.when(own)
            def _():
                pltpu.make_async_copy(src, dst, rsem.at[sem]).start()

    for h in range(2):
        for k in range(2):
            zd = 2 * core + h
            src = xg.at[pl.ds(HALF * k, HALF), pl.ds(256 * h, PAD)]
            dst = xb.at[z, pl.ds(HALF * k, HALF), pl.ds(pl.multiple_of(PAD * y, 128), PAD)]
            own = jnp.logical_and(zd == z, core == k)
            sem = SEM["x1_0"] + z
            cp = rc(src, dst, "x1_%d" % (2 * h + k), dev(x, y, zd, k), sem)
            some.append((own, cp))

            @pl.when(jnp.logical_not(own))
            def _():
                cp.start()

            @pl.when(own)
            def _():
                pltpu.make_async_copy(src, dst, rsem.at[sem]).start()

    for i in range(1, 8):
        go(ss_own, ss_all.at[i - 1], "ss_%d" % (i - 1), (lax.rem(r + i, 8), c))

    go(up_ref.at[0], u0(z, 0, 128), "u0_p", to_zp)
    go(up_ref.at[0], u0(z, 0, 128), "u0_m", to_zm)

    def v1(xo, zo):
        return up_all.at[xo, zo, 1]

    def v0(xo, zo):
        return up_all.at[xo, zo, 0]

    def send_v1(k, src):
        xo = mod4(x + k)
        go(src, v1(xo, z), "v1_%d_p" % k, to_zp)
        go(src, v1(xo, z), "v1_%d_m" % k, to_zm)

    def relay_v1(k):
        xo = mod4(x + k)
        if k < 2:
            got("v1_%d_p" % k)
            go(v1(xo, zm), v1(xo, zm), "v1_%d_r" % k, to_zp)
        else:
            got("v1_%d_m" % k)
            go(v1(xo, zp), v1(xo, zp), "v1_%d_r" % k, to_zm)

    def send_v0(k, src):
        zo = mod4(z + k)
        go(src, v0(x, zo), "v0_%d_p" % k, to_xp)
        go(src, v0(x, zo), "v0_%d_m" % k, to_xm)

    def relay_v0(k):
        zo = mod4(z + k)
        if k < 2:
            got("v0_%d_p" % k)
            go(v0(xm, zo), v0(xm, zo), "v0_%d_r" % k, to_xp)
        else:
            got("v0_%d_m" % k)
            go(v0(xp, zo), v0(xp, zo), "v0_%d_r" % k, to_xm)

    def finish(j, k):
        got("v%d_%d_%s" % (j, k, "m" if k < 2 else "p"), "v%d_%d_r" % (j, k))

    send_v1(0, up_ref.at[1])

    l_w = pltpu.make_async_copy(w_ref, wb.at[:, x, pl.ds(off, BLK), :], lsem.at[5])
    l_w.start()
    l_u = pltpu.make_async_copy(up_ref, up_all.at[x, z], lsem.at[6])
    l_u.start()

    def dcols(xo):
        return pl.ds(pl.multiple_of(RANK * xo, 128), RANK)

    for zs in range(4):
        rc(da.at[zs], da.at[zs], "d1_0", to_other, SEM["d1_0"] + zs).wait_recv()
    for k in range(1, 4):
        yd = mod4(y + k)
        go(da.at[yd], db.at[y, pl.ds(off, BLK), dcols(x)], "db_%d" % k, dev(x, yd, z, core))
    l_d = pltpu.make_async_copy(da.at[y], db.at[y, pl.ds(off, BLK), dcols(x)], lsem.at[7])
    l_d.start()

    def unit(yo, a, n):
        return xb.at[
            pl.ds(a, n),
            pl.ds(pl.multiple_of(HALF * core, 16), HALF),
            pl.ds(pl.multiple_of(PAD * yo, 128), PAD),
        ]

    for zs in range(4):
        piece = xb.at[
            zs,
            pl.ds(pl.multiple_of(HALF * core, 16), HALF),
            pl.ds(pl.multiple_of(PAD * y, 128), PAD),
        ]
        rc(piece, piece, "x1_0", to_other, SEM["x1_0"] + zs).wait_recv()
    go(unit(y, 0, 4), unit(y, 0, 4), "x2_p", to_yp)
    go(unit(y, 0, 4), unit(y, 0, 4), "x2_m", to_ym)
    go(unit(y, 0, 4), unit(y, 0, 4), "xc_0", to_other)

    got("u1_p", "u1_m")
    send_v1(1, v1(xp, z))
    send_v1(3, v1(xm, z))

    def dpart(xo, a, n):
        return db.at[pl.ds(a, n), pl.ds(off, BLK), dcols(xo)]

    l_d.wait()
    got("db_1", "db_2", "db_3")
    go(dpart(x, 0, 4), dpart(x, 0, 4), "d2_p", to_xp)
    go(dpart(x, 0, 4), dpart(x, 0, 4), "d2_m", to_xm)
    send_v0(0, up_ref.at[0])
    got("u0_p", "u0_m")
    go(u0(zm, 0, 64), u0(zm, 0, 64), "u0_rp", to_zp)
    go(u0(zp, 64, 64), u0(zp, 64, 64), "u0_rm", to_zm)
    relay_weights(1)

    for cp in l_small:
        cp.wait()
    tgt = targets(lenv, porv, aorv, asiv, c * TOK)

    def picks(g):
        hit = jnp.where(
            iota((256, 256), 0).astype(F32) == tgt[g : g + 1, :], 1.0, 0.0
        )
        pick[g] = hit.T.astype(BF16)

    got("x2_p")
    go(unit(ym, 0, 2), unit(ym, 0, 2), "x2_rp", to_yp)
    go(unit(ym, 0, 4), unit(ym, 0, 4), "xc_1", to_other)
    got("x2_m")
    go(unit(yp, 2, 2), unit(yp, 2, 2), "x2_rm", to_ym)
    go(unit(yp, 0, 4), unit(yp, 0, 4), "xc_2", to_other)
    relay_v1(0)
    for g in range(GROUPS // 2):
        picks(g)
    got("x2_rp")
    go(unit(y2, 0, 2), unit(y2, 0, 2), "xc_3", to_other)
    got("x2_rm")
    go(unit(y2, 2, 2), unit(y2, 2, 2), "xc_4", to_other)
    got("d2_p")
    go(dpart(xm, 0, 2), dpart(xm, 0, 2), "d2_rp", to_xp)
    got("d2_m")
    go(dpart(xp, 2, 2), dpart(xp, 2, 2), "d2_rm", to_xm)
    go(u1(xm, 0, 64), u1(xm, 0, 64), "u1_rp", to_xp)
    go(u1(xp, 64, 64), u1(xp, 64, 64), "u1_rm", to_xm)
    weights(0)
    send_v0(1, v0(x, zp))
    relay_v1(1)
    relay_v1(3)
    for g in range(GROUPS // 2, GROUPS):
        picks(g)
    for i in range(5):
        got("xc_%d" % i)
    l_w.wait()

    up_rows, low_rows = pl.ds(0, HALF), pl.ds(HALF, HALF)

    def partials(s, product, far, first, later, near, final):
        far[...] = product(z2).astype(BF16)
        go(far.at[up_rows], first.at[0], "s%d_fp" % s, to_zp)
        go(far.at[low_rows], first.at[1], "s%d_fm" % s, to_zm)
        part = product(zp)
        near[0] = part[HALF:].astype(BF16)
        later[0] = part[:HALF]
        go(near.at[0], final.at[0, low_rows], "s%d_np" % s, to_zp)
        part = product(zm)
        near[1] = part[:HALF].astype(BF16)
        later[1] = part[HALF:]
        go(near.at[1], final.at[1, up_rows], "s%d_nm" % s, to_zm)

    def pass_on(s, first, later, total, final):
        got("s%d_fp" % s)
        total[0] = (later[0] + first[0].astype(F32)).astype(BF16)
        go(total.at[0], final.at[0, up_rows], "s%d_ap" % s, to_zp)
        got("s%d_fm" % s)
        total[1] = (later[1] + first[1].astype(F32)).astype(BF16)
        go(total.at[1], final.at[1, low_rows], "s%d_am" % s, to_zm)

    def arrived(s):
        got("s%d_np" % s, "s%d_nm" % s, "s%d_ap" % s, "s%d_am" % s)

    def base_part(j):
        def product(block):
            return jnp.dot(
                xb[block], wb[j].reshape(4 * PAD, OUT), preferred_element_type=F32
            )

        partials(j, product, bfar.at[j], bfirst.at[j], blater.at[j], bnear.at[j], bfinal.at[j])
        bown[j] = product(z)

    def base_pass(j):
        pass_on(j, bfirst.at[j], blater.at[j], bsum.at[j], bfinal.at[j])

    def base_done(j):
        arrived(j)
        base_out[j] = (
            bown[j] + bfinal[j, 0].astype(F32) + bfinal[j, 1].astype(F32)
        ) * scale

    def rank_product(block):
        return jnp.dot(xb[block], db[...].reshape(4 * PAD, 512), preferred_element_type=F32)

    got("w1_bp", "w1_am", "w1_rp", "w1_rm")
    base_part(1)
    got("d2_rp", "d2_rm")
    partials(2, rank_product, rfar, rfirst, rlater, rnear, rfinal)
    rown[...] = rank_product(z)
    base_pass(1)
    got("u0_rp", "u0_rm", "u1_rp", "u1_rm")
    relay_weights(0)
    send_v0(3, v0(x, zm))
    send_v0(2, v0(x, z2))
    relay_v0(0)
    relay_v0(1)
    pass_on(2, rfirst, rlater, rsum, rfinal)
    send_v1(2, v1(x2, z))

    total = ss_own[...]
    for i in range(7):
        got("ss_%d" % i)
        total += ss_all[i]
    scale = to_col(lax.rsqrt(total[0:1, :] / (FEAT * 8) + 1e-05), TOK)

    def ranks(yo, a, n):
        return rank_all.at[yo, core, pl.ds(a, n)]

    arrived(2)
    rank_all[y, core] = (
        (rown[...] + rfinal[0].astype(F32) + rfinal[1].astype(F32)) * scale
    ).astype(BF16)
    go(ranks(y, 0, TOK), ranks(y, 0, TOK), "ra_p", to_yp)
    go(ranks(y, 0, TOK), ranks(y, 0, TOK), "ra_m", to_ym)
    go(ranks(y, 0, TOK), ranks(y, 0, TOK), "ra_c0", to_other)

    base_done(1)
    relay_v1(2)
    got("w0_bp", "w0_am", "w0_rp", "w0_rm")
    base_part(0)

    relay_v0(3)
    relay_v0(2)
    got("ra_p")
    go(ranks(ym, 0, HALF), ranks(ym, 0, HALF), "ra_rp", to_yp)
    go(ranks(ym, 0, TOK), ranks(ym, 0, TOK), "ra_c1", to_other)
    got("ra_m")
    go(ranks(yp, HALF, HALF), ranks(yp, HALF, HALF), "ra_rm", to_ym)
    go(ranks(yp, 0, TOK), ranks(yp, 0, TOK), "ra_c2", to_other)
    base_pass(0)
    got("ra_rp")
    go(ranks(y2, 0, HALF), ranks(y2, 0, HALF), "ra_c3", to_other)
    got("ra_rm")
    go(ranks(y2, HALF, HALF), ranks(y2, HALF, HALF), "ra_c4", to_other)

    for k in range(4):
        finish(1, k)
    for i in range(5):
        got("ra_c%d" % i)
    l_u.wait()
    blend(up_all, rank_all, base_out, mix, 1, range(16))

    def group(i, carry):
        for n in range(2):
            at = pl.multiple_of(32 * i + 16 * n, 16)
            done[pl.ds(at, 16)] = place(pick, mix, 2 * i + n)
        return carry

    lax.fori_loop(0, GROUPS // 2, group, 0)
    base_done(0)
    for k in range(4):
        finish(0, k)
    for own, cp in some:

        @pl.when(jnp.logical_not(own))
        def _():
            cp.wait_send()

    for cp in sends:
        cp.wait_send()


def combine(up, rank, base, pick, done, q_out, v_out, mix, obuf, osem, dsem):
    whole = pltpu.make_async_copy(done, v_out, dsem.at[0])
    whole.start()
    blend(up, rank, base, mix, 0, range(16))

    def put(i, slot):
        return pltpu.make_async_copy(
            obuf.at[slot], q_out.at[pl.ds(32 * i, 32)], osem.at[slot]
        )

    def group(i, carry):
        slot = lax.rem(i, 2)

        @pl.when(i >= 2)
        def _():
            put(i - 2, slot).wait()

        for n in range(2):
            obuf[slot, 16 * n : 16 * (n + 1)] = place(pick, mix, 2 * i + n)
        put(i, slot).start()
        return carry

    lax.fori_loop(0, GROUPS // 2, group, 0)
    for i in (GROUPS // 2 - 2, GROUPS // 2 - 1):
        put(i, i % 2).wait()
    whole.wait()


def stay(array):
    return pltpu.with_memory_space_constraint(array, pltpu.HBM)


def body(
    prompt_token_states,
    gain,
    projection_weight,
    adapter_down_maps,
    adapter_up_maps,
    prompt_token_length,
    prompt_of_request,
    adapter_of_request,
    adapter_slot_index,
):
    vmem = pl.BlockSpec(memory_space=pltpu.VMEM)
    hbm = pl.BlockSpec(memory_space=pltpu.HBM)
    anyw = pl.BlockSpec(memory_space=pl.ANY)
    lens = prompt_token_length.reshape(1, -1)
    por = prompt_of_request.reshape(1, -1)
    aor = adapter_of_request.reshape(1, -1)
    asi = adapter_slot_index.reshape(1, -1)
    gathered = pl.pallas_call(
        exchange,
        out_shape=(
            jax.ShapeDtypeStruct((4, 4, 2, RANK, OUT), BF16),
            jax.ShapeDtypeStruct((4, 2, TOK, 512), BF16),
            jax.ShapeDtypeStruct((2, TOK, OUT), F32),
            jax.ShapeDtypeStruct((GROUPS, 256, 256), BF16),
            jax.ShapeDtypeStruct((TOK, SLOTS, OUT), BF16),
        ),
        in_specs=[hbm, hbm, hbm, hbm, hbm, hbm, hbm, hbm, hbm],
        out_specs=(vmem, vmem, vmem, vmem, vmem),
        scratch_shapes=[
            pltpu.VMEM((BLK, 2, OUT), BF16),
            pltpu.VMEM((2, BLK, OUT), BF16),
            pltpu.VMEM((TOK, FEAT), BF16),
            pltpu.VMEM((FEAT,), BF16),
            pltpu.VMEM(lens.shape, jnp.int32),
            pltpu.VMEM(por.shape, jnp.int32),
            pltpu.VMEM(aor.shape, jnp.int32),
            pltpu.VMEM(asi.shape, jnp.int32),
            pltpu.VMEM((TOK, FEAT), BF16),
            pltpu.VMEM((4, TOK, 4 * PAD), BF16),
            pltpu.VMEM((2, 4, PAD, OUT), BF16),
            pltpu.VMEM((4, BLK, RANK), BF16),
            pltpu.VMEM((4, PAD, 512), BF16),
            pltpu.VMEM((2, TOK, OUT), BF16),
            pltpu.VMEM((2, 2, HALF, OUT), BF16),
            pltpu.VMEM((2, 2, HALF, OUT), F32),
            pltpu.VMEM((2, 2, HALF, OUT), BF16),
            pltpu.VMEM((2, 2, HALF, OUT), BF16),
            pltpu.VMEM((2, 2, TOK, OUT), BF16),
            pltpu.VMEM((2, TOK, OUT), F32),
            pltpu.VMEM((TOK, 512), BF16),
            pltpu.VMEM((2, HALF, 512), BF16),
            pltpu.VMEM((2, HALF, 512), F32),
            pltpu.VMEM((2, HALF, 512), BF16),
            pltpu.VMEM((2, HALF, 512), BF16),
            pltpu.VMEM((2, TOK, 512), BF16),
            pltpu.VMEM((TOK, 512), F32),
            pltpu.VMEM((8, TOK), F32),
            pltpu.VMEM((7, 8, TOK), F32),
            pltpu.VMEM((GROUPS, 256, OUT), BF16),
            pltpu.SemaphoreType.DMA((NSEM,)),
            pltpu.SemaphoreType.DMA((NSEM,)),
            pltpu.SemaphoreType.DMA((10,)),
        ],
        compiler_params=pltpu.CompilerParams(
            collective_id=0, has_side_effects=True, vmem_limit_bytes=29 << 20
        ),
        name="exchange",
    )(
        stay(prompt_token_states),
        stay(gain),
        stay(projection_weight),
        stay(adapter_down_maps.reshape(FEAT, 2 * RANK)),
        stay(adapter_up_maps.reshape(2, RANK, OUT)),
        stay(lens),
        stay(por),
        stay(aor),
        stay(asi),
    )
    return pl.pallas_call(
        combine,
        out_shape=(
            jax.ShapeDtypeStruct((TOK, SLOTS, OUT), BF16),
            jax.ShapeDtypeStruct((TOK, SLOTS, OUT), BF16),
        ),
        in_specs=[vmem] * 5,
        out_specs=(anyw, anyw),
        scratch_shapes=[
            pltpu.VMEM((GROUPS, 256, OUT), BF16),
            pltpu.VMEM((2, 32, SLOTS, OUT), BF16),
            pltpu.SemaphoreType.DMA((2,)),
            pltpu.SemaphoreType.DMA((1,)),
        ],
        compiler_params=pltpu.CompilerParams(vmem_limit_bytes=20 << 20),
        name="combine",
    )(*gathered)


def solution(mesh):
    placed = (
        P("col", "row"),
        P("row"),
        P("col", None, "row"),
        P("col", "row", None),
        P("col", None, None, "row"),
        P(),
        P(),
        P(),
        P(),
    )
    return jax.shard_map(
        body,
        mesh=mesh,
        in_specs=placed,
        out_specs=(P("col", None, "row"), P("col", None, "row")),
        check_vma=False,
    )
```

```python
import functools

import jax
import jax.numpy as jnp
from jax import lax
from jax.experimental import pallas as pl
from jax.experimental.pallas import tpu as pltpu
from jax.sharding import PartitionSpec as P

F32 = jnp.float32
BF16 = jnp.bfloat16
MESH = pl.DeviceIdType.MESH

SLOTS = 16
TOK = 224
HALF = 112
FEAT = 640
BLK = 320
PAD = 384
OUT = 640
RANK = 128
GROUPS = 14

NAMES = (
    ["x1_%d" % i for i in range(4)]
    + ["d1_%d" % i for i in range(4)]
    + ["db_%d" % i for i in range(4)]
    + ["ss_%d" % i for i in range(7)]
    + ["w%d_%s" % (j, s) for j in range(2) for s in ("ap", "bp", "am", "bm", "rp", "rm")]
    + ["x2_%s" % s for s in ("p", "m", "rp", "rm")]
    + ["xc_%d" % i for i in range(5)]
    + ["d2_%s" % s for s in ("p", "m", "rp", "rm")]
    + ["u%d_%s" % (j, s) for j in range(2) for s in ("p", "m", "rp", "rm")]
    + ["v%d_%d_%s" % (j, k, s) for j in range(2) for k in range(4) for s in ("p", "m", "r")]
    + ["s%d_%s" % (j, s) for j in range(3) for s in ("fp", "fm", "np", "nm", "ap", "am")]
    + ["ra_%s" % s for s in ("p", "m", "rp", "rm", "c0", "c1", "c2", "c3", "c4")]
)
SEM = {name: i for i, name in enumerate(NAMES)}
NSEM = len(NAMES)


def to_col(row, n):
    same = lax.broadcasted_iota(jnp.int32, (n, n), 0) == lax.broadcasted_iota(jnp.int32, (n, n), 1)
    return jnp.sum(jnp.where(same, jnp.broadcast_to(row, (n, n)), 0.0), axis=1, keepdims=True)


def iota(shape, axis):
    return lax.broadcasted_iota(jnp.int32, shape, axis)


def targets(len_ref, por_ref, aor_ref, asi_ref, first_token):
    lens = len_ref[...].astype(F32)
    por = por_ref[...].astype(F32)
    aor = aor_ref[...].astype(F32)
    asi = asi_ref[...].astype(F32)
    n_prompt = lens.shape[1]
    n_req = por.shape[1]
    n_lib = asi.shape[1]
    before = jnp.sum(
        jnp.where(to_col(por, n_req) < por, 1.0, 0.0), axis=0, keepdims=True
    )
    position = iota((1, n_req), 1).astype(F32) - before
    hot = iota((n_lib, n_req), 0).astype(F32) == aor
    slot = jnp.sum(
        jnp.where(hot, jnp.broadcast_to(to_col(asi, n_lib), (n_lib, n_req)), 0.0),
        axis=0,
        keepdims=True,
    )
    by_prompt = jnp.where(iota((16, n_req), 0).astype(F32) == por, slot + 1.0, 0.0)
    by_place = jnp.where(iota((16, n_req), 0).astype(F32) == position, 1.0, 0.0)
    table = lax.dot_general(
        by_prompt.astype(BF16),
        by_place.astype(BF16),
        (((1,), (1,)), ((), ())),
        preferred_element_type=F32,
    )
    spread = jnp.where(iota((16, 256), 0) == iota((16, 256), 1) % 16, 1.0, 0.0)
    table = jnp.dot(table.astype(BF16), spread.astype(BF16), preferred_element_type=F32)
    ends = jnp.sum(
        jnp.where(
            iota((n_prompt, n_prompt), 0) <= iota((n_prompt, n_prompt), 1),
            jnp.broadcast_to(to_col(lens, n_prompt), (n_prompt, n_prompt)),
            0.0,
        ),
        axis=0,
        keepdims=True,
    )
    in_group = iota((16, 256), 1) // 16
    token = (first_token + 16 * iota((16, 256), 0) + in_group).astype(F32)
    prompt = jnp.zeros((16, 256), F32)
    for p in range(n_prompt):
        prompt += jnp.where(token >= ends[:, p : p + 1], 1.0, 0.0)
    chosen = jnp.zeros((16, 256), F32)
    for p in range(n_prompt):
        chosen += jnp.where(prompt == float(p), jnp.broadcast_to(table[p : p + 1, :], (16, 256)), 0.0)
    return jnp.where(chosen > 0.5, (chosen - 1.0) * 16.0 + in_group.astype(F32), -1.0)


def blend(up, rank, base, mix, j, adapters):
    for a in adapters:
        xo, zo = a // 4, a % 4
        delta = jnp.dot(
            rank[zo, j, :, RANK * xo : RANK * (xo + 1)],
            up[xo, zo, j],
            preferred_element_type=F32,
        )
        full = (base[j] + delta).astype(BF16)
        mix[:, 16 * a : 16 * (a + 1), :] = full.reshape(GROUPS, 16, OUT)


def place(pick, mix, g):
    rows = jnp.dot(pick[g], mix[g], preferred_element_type=F32).astype(BF16)
    return rows.reshape(16, SLOTS, OUT)


def exchange(
    x_hbm, gain_hbm, w_ref, d_ref, up_ref, len_hbm, por_hbm, aor_hbm, asi_hbm,
    up_all, rank_all, base_out, pick, done,
    xv, gainv, lenv, porv, aorv, asiv,
    xg, xb, wb, da, db, bfar, bfirst, blater, bnear, bsum, bfinal, bown,
    rfar, rfirst, rlater, rnear, rsum, rfinal, rown, ss_own, ss_all, mix,
    ssem, rsem, lsem,
):
    r = lax.axis_index("row")
    c = lax.axis_index("col")
    y, core = lax.div(r, 2), lax.rem(r, 2)
    x, z = lax.div(c, 4), lax.rem(c, 4)

    def dev(x_, y_, z_, core_):
        return (y_ * 2 + core_, x_ * 4 + z_)

    def mod4(v):
        return lax.rem(v + 8, 4)

    def rc(src, dst, send, to, recv=None):
        return pltpu.make_async_remote_copy(
            src_ref=src,
            dst_ref=dst,
            send_sem=ssem.at[SEM[send]],
            recv_sem=rsem.at[SEM[send] if recv is None else recv],
            device_id=to,
            device_id_type=MESH,
        )

    xp, xm, x2 = mod4(x + 1), mod4(x - 1), mod4(x + 2)
    yp, ym, y2 = mod4(y + 1), mod4(y - 1), mod4(y + 2)
    zp, zm, z2 = mod4(z + 1), mod4(z - 1), mod4(z + 2)
    to_xp, to_xm = dev(xp, y, z, core), dev(xm, y, z, core)
    to_yp, to_ym = dev(x, yp, z, core), dev(x, ym, z, core)
    to_zp, to_zm = dev(x, y, zp, core), dev(x, y, zm, core)
    to_other = dev(x, y, z, 1 - core)
    copies = {}
    sends = []

    def go(src, dst, name, to):
        cp = rc(src, dst, name, to)
        cp.start()
        copies[name] = cp
        sends.append(cp)

    def got(*names):
        for name in names:
            copies[name].wait_recv()

    barrier = pltpu.get_barrier_semaphore()

    partners = [to_xp, to_xm, to_other]
    for k in range(1, 4):
        for other in (core, 1 - core):
            partners.append(dev(x, y, mod4(z + k), other))
            partners.append(dev(x, mod4(y + k), z, other))
    for partner in partners:
        pl.semaphore_signal(barrier, inc=1, device_id=partner, device_id_type=MESH)

    l_x = pltpu.make_async_copy(x_hbm, xv, lsem.at[0])
    l_x.start()
    l_g = pltpu.make_async_copy(gain_hbm, gainv, lsem.at[8])
    l_g.start()
    l_small = []
    for i, (a, b) in enumerate(
        ((len_hbm, lenv), (por_hbm, porv), (aor_hbm, aorv), (asi_hbm, asiv))
    ):
        l_small.append(pltpu.make_async_copy(a, b, lsem.at[1 + i]))
        l_small[-1].start()

    odd = lax.rem(z, 2)
    off = pl.multiple_of(64 * odd, 64)
    pad_at = pl.multiple_of(BLK * (1 - odd), 64)
    for b in range(4):
        for j in range(2):
            wb[j, b, pl.ds(pad_at, 64), :] = jnp.zeros((64, OUT), BF16)
        db[b, pl.ds(pad_at, 64), :] = jnp.zeros((64, 512), BF16)

    l_x.wait()
    l_g.wait()
    states = xv[...].astype(F32)
    xg[...] = (states * gainv[...].astype(F32).reshape(1, FEAT)).astype(BF16)
    ss_own[...] = lax.dot_general(
        jnp.ones((8, FEAT), F32),
        states * states,
        (((1,), (1,)), ((), ())),
        precision=lax.Precision.HIGHEST,
        preferred_element_type=F32,
    )
    pl.semaphore_wait(barrier, len(partners))

    def u1(xo, a, n):
        return up_all.at[xo, z, 1, pl.ds(a, n), :]

    def u0(zo, a, n):
        return up_all.at[x, zo, 0, pl.ds(a, n), :]

    go(up_ref.at[1], u1(x, 0, 128), "u1_p", to_xp)
    go(up_ref.at[1], u1(x, 0, 128), "u1_m", to_xm)

    def wslot(j, xo, a):
        return wb.at[j, xo, pl.ds(pl.multiple_of(off + a, 32), 160), :]

    def weights(j):
        go(w_ref.at[j, pl.ds(0, 160), :], wslot(j, x, 0), "w%d_ap" % j, to_xp)
        go(w_ref.at[j, pl.ds(160, 160), :], wslot(j, x, 160), "w%d_bm" % j, to_xm)
        go(w_ref.at[j, pl.ds(160, 160), :], wslot(j, x, 160), "w%d_bp" % j, to_xp)
        go(w_ref.at[j, pl.ds(0, 160), :], wslot(j, x, 0), "w%d_am" % j, to_xm)

    def relay_weights(j):
        got("w%d_ap" % j)
        go(wslot(j, xm, 0), wslot(j, xm, 0), "w%d_rp" % j, to_xp)
        got("w%d_bm" % j)
        go(wslot(j, xp, 160), wslot(j, xp, 160), "w%d_rm" % j, to_xm)

    weights(1)

    some = []
    for h in range(2):
        for k in range(2):
            zd = 2 * core + h
            src = d_ref.at[pl.ds(BLK * h, BLK), pl.ds(RANK * k, RANK)]
            dst = da.at[z]
            own = jnp.logical_and(zd == z, core == k)
            sem = SEM["d1_0"] + z
            cp = rc(src, dst, "d1_%d" % (2 * h + k), dev(x, y, zd, k), sem)
            some.append((own, cp))

            @pl.when(jnp.logical_not(own))
            def _():
                cp.start()

            @pl.when(own)
            def _():
                pltpu.make_async_copy(src, dst, rsem.at[sem]).start()

    for h in range(2):
        for k in range(2):
            zd = 2 * core + h
            src = xg.at[pl.ds(HALF * k, HALF), pl.ds(256 * h, PAD)]
            dst = xb.at[z, pl.ds(HALF * k, HALF), pl.ds(pl.multiple_of(PAD * y, 128), PAD)]
            own = jnp.logical_and(zd == z, core == k)
            sem = SEM["x1_0"] + z
            cp = rc(src, dst, "x1_%d" % (2 * h + k), dev(x, y, zd, k), sem)
            some.append((own, cp))

            @pl.when(jnp.logical_not(own))
            def _():
                cp.start()

            @pl.when(own)
            def _():
                pltpu.make_async_copy(src, dst, rsem.at[sem]).start()

    for i in range(1, 8):
        go(ss_own, ss_all.at[i - 1], "ss_%d" % (i - 1), (lax.rem(r + i, 8), c))

    go(up_ref.at[0], u0(z, 0, 128), "u0_p", to_zp)
    go(up_ref.at[0], u0(z, 0, 128), "u0_m", to_zm)

    def v1(xo, zo):
        return up_all.at[xo, zo, 1]

    def v0(xo, zo):
        return up_all.at[xo, zo, 0]

    def send_v1(k, src):
        xo = mod4(x + k)
        go(src, v1(xo, z), "v1_%d_p" % k, to_zp)
        go(src, v1(xo, z), "v1_%d_m" % k, to_zm)

    def relay_v1(k):
        xo = mod4(x + k)
        if k < 2:
            got("v1_%d_p" % k)
            go(v1(xo, zm), v1(xo, zm), "v1_%d_r" % k, to_zp)
        else:
            got("v1_%d_m" % k)
            go(v1(xo, zp), v1(xo, zp), "v1_%d_r" % k, to_zm)

    def send_v0(k, src):
        zo = mod4(z + k)
        go(src, v0(x, zo), "v0_%d_p" % k, to_xp)
        go(src, v0(x, zo), "v0_%d_m" % k, to_xm)

    def relay_v0(k):
        zo = mod4(z + k)
        if k < 2:
            got("v0_%d_p" % k)
            go(v0(xm, zo), v0(xm, zo), "v0_%d_r" % k, to_xp)
        else:
            got("v0_%d_m" % k)
            go(v0(xp, zo), v0(xp, zo), "v0_%d_r" % k, to_xm)

    def finish(j, k):
        got("v%d_%d_%s" % (j, k, "m" if k < 2 else "p"), "v%d_%d_r" % (j, k))

    send_v1(0, up_ref.at[1])

    l_w = pltpu.make_async_copy(w_ref, wb.at[:, x, pl.ds(off, BLK), :], lsem.at[5])
    l_w.start()
    l_u = pltpu.make_async_copy(up_ref, up_all.at[x, z], lsem.at[6])
    l_u.start()

    def dcols(xo):
        return pl.ds(pl.multiple_of(RANK * xo, 128), RANK)

    for zs in range(4):
        rc(da.at[zs], da.at[zs], "d1_0", to_other, SEM["d1_0"] + zs).wait_recv()
    for k in range(1, 4):
        yd = mod4(y + k)
        go(da.at[yd], db.at[y, pl.ds(off, BLK), dcols(x)], "db_%d" % k, dev(x, yd, z, core))
    l_d = pltpu.make_async_copy(da.at[y], db.at[y, pl.ds(off, BLK), dcols(x)], lsem.at[7])
    l_d.start()

    def unit(yo, a, n):
        return xb.at[
            pl.ds(a, n),
            pl.ds(pl.multiple_of(HALF * core, 16), HALF),
            pl.ds(pl.multiple_of(PAD * yo, 128), PAD),
        ]

    for zs in range(4):
        piece = xb.at[
            zs,
            pl.ds(pl.multiple_of(HALF * core, 16), HALF),
            pl.ds(pl.multiple_of(PAD * y, 128), PAD),
        ]
        rc(piece, piece, "x1_0", to_other, SEM["x1_0"] + zs).wait_recv()
    go(unit(y, 0, 4), unit(y, 0, 4), "x2_p", to_yp)
    go(unit(y, 0, 4), unit(y, 0, 4), "x2_m", to_ym)
    go(unit(y, 0, 4), unit(y, 0, 4), "xc_0", to_other)

    got("u1_p", "u1_m")
    send_v1(1, v1(xp, z))
    send_v1(3, v1(xm, z))

    def dpart(xo, a, n):
        return db.at[pl.ds(a, n), pl.ds(off, BLK), dcols(xo)]

    l_d.wait()
    got("db_1", "db_2", "db_3")
    go(dpart(x, 0, 4), dpart(x, 0, 4), "d2_p", to_xp)
    go(dpart(x, 0, 4), dpart(x, 0, 4), "d2_m", to_xm)
    send_v0(0, up_ref.at[0])
    got("u0_p", "u0_m")
    go(u0(zm, 0, 64), u0(zm, 0, 64), "u0_rp", to_zp)
    go(u0(zp, 64, 64), u0(zp, 64, 64), "u0_rm", to_zm)
    relay_weights(1)

    for cp in l_small:
        cp.wait()
    tgt = targets(lenv, porv, aorv, asiv, c * TOK)

    def picks(g):
        hit = jnp.where(
            iota((256, 256), 0).astype(F32) == tgt[g : g + 1, :], 1.0, 0.0
        )
        pick[g] = hit.T.astype(BF16)

    got("x2_p")
    go(unit(ym, 0, 2), unit(ym, 0, 2), "x2_rp", to_yp)
    go(unit(ym, 0, 4), unit(ym, 0, 4), "xc_1", to_other)
    got("x2_m")
    go(unit(yp, 2, 2), unit(yp, 2, 2), "x2_rm", to_ym)
    go(unit(yp, 0, 4), unit(yp, 0, 4), "xc_2", to_other)
    relay_v1(0)
    for g in range(GROUPS // 2):
        picks(g)
    got("x2_rp")
    go(unit(y2, 0, 2), unit(y2, 0, 2), "xc_3", to_other)
    got("x2_rm")
    go(unit(y2, 2, 2), unit(y2, 2, 2), "xc_4", to_other)
    got("d2_p")
    go(dpart(xm, 0, 2), dpart(xm, 0, 2), "d2_rp", to_xp)
    got("d2_m")
    go(dpart(xp, 2, 2), dpart(xp, 2, 2), "d2_rm", to_xm)
    go(u1(xm, 0, 64), u1(xm, 0, 64), "u1_rp", to_xp)
    go(u1(xp, 64, 64), u1(xp, 64, 64), "u1_rm", to_xm)
    weights(0)
    send_v0(1, v0(x, zp))
    relay_v1(1)
    relay_v1(3)
    for g in range(GROUPS // 2, GROUPS):
        picks(g)
    for i in range(5):
        got("xc_%d" % i)
    l_w.wait()

    up_rows, low_rows = pl.ds(0, HALF), pl.ds(HALF, HALF)

    def partials(s, product, far, first, later, near, final):
        far[...] = product(z2).astype(BF16)
        go(far.at[up_rows], first.at[0], "s%d_fp" % s, to_zp)
        go(far.at[low_rows], first.at[1], "s%d_fm" % s, to_zm)
        part = product(zp)
        near[0] = part[HALF:].astype(BF16)
        later[0] = part[:HALF]
        go(near.at[0], final.at[0, low_rows], "s%d_np" % s, to_zp)
        part = product(zm)
        near[1] = part[:HALF].astype(BF16)
        later[1] = part[HALF:]
        go(near.at[1], final.at[1, up_rows], "s%d_nm" % s, to_zm)

    def pass_on(s, first, later, total, final):
        got("s%d_fp" % s)
        total[0] = (later[0] + first[0].astype(F32)).astype(BF16)
        go(total.at[0], final.at[0, up_rows], "s%d_ap" % s, to_zp)
        got("s%d_fm" % s)
        total[1] = (later[1] + first[1].astype(F32)).astype(BF16)
        go(total.at[1], final.at[1, low_rows], "s%d_am" % s, to_zm)

    def arrived(s):
        got("s%d_np" % s, "s%d_nm" % s, "s%d_ap" % s, "s%d_am" % s)

    def base_part(j):
        def product(block):
            return jnp.dot(
                xb[block], wb[j].reshape(4 * PAD, OUT), preferred_element_type=F32
            )

        partials(j, product, bfar.at[j], bfirst.at[j], blater.at[j], bnear.at[j], bfinal.at[j])
        bown[j] = product(z)

    def base_pass(j):
        pass_on(j, bfirst.at[j], blater.at[j], bsum.at[j], bfinal.at[j])

    def base_done(j):
        arrived(j)
        base_out[j] = (
            bown[j] + bfinal[j, 0].astype(F32) + bfinal[j, 1].astype(F32)
        ) * scale

    def rank_product(block):
        return jnp.dot(xb[block], db[...].reshape(4 * PAD, 512), preferred_element_type=F32)

    got("w1_bp", "w1_am", "w1_rp", "w1_rm")
    base_part(1)
    got("d2_rp", "d2_rm")
    partials(2, rank_product, rfar, rfirst, rlater, rnear, rfinal)
    rown[...] = rank_product(z)
    base_pass(1)
    got("u0_rp", "u0_rm", "u1_rp", "u1_rm")
    relay_weights(0)
    send_v0(3, v0(x, zm))
    send_v0(2, v0(x, z2))
    relay_v0(0)
    relay_v0(1)
    pass_on(2, rfirst, rlater, rsum, rfinal)
    send_v1(2, v1(x2, z))

    total = ss_own[...]
    for i in range(7):
        got("ss_%d" % i)
        total += ss_all[i]
    scale = to_col(lax.rsqrt(total[0:1, :] / (FEAT * 8) + 1e-05), TOK)

    def ranks(yo, a, n):
        return rank_all.at[yo, core, pl.ds(a, n)]

    arrived(2)
    rank_all[y, core] = (
        (rown[...] + rfinal[0].astype(F32) + rfinal[1].astype(F32)) * scale
    ).astype(BF16)
    go(ranks(y, 0, TOK), ranks(y, 0, TOK), "ra_p", to_yp)
    go(ranks(y, 0, TOK), ranks(y, 0, TOK), "ra_m", to_ym)
    go(ranks(y, 0, TOK), ranks(y, 0, TOK), "ra_c0", to_other)

    base_done(1)
    relay_v1(2)
    got("w0_bp", "w0_am", "w0_rp", "w0_rm")
    base_part(0)

    got("ra_p")
    go(ranks(ym, 0, HALF), ranks(ym, 0, HALF), "ra_rp", to_yp)
    go(ranks(ym, 0, TOK), ranks(ym, 0, TOK), "ra_c1", to_other)
    got("ra_m")
    go(ranks(yp, HALF, HALF), ranks(yp, HALF, HALF), "ra_rm", to_ym)
    go(ranks(yp, 0, TOK), ranks(yp, 0, TOK), "ra_c2", to_other)
    base_pass(0)
    relay_v0(3)
    relay_v0(2)
    got("ra_rp")
    go(ranks(y2, 0, HALF), ranks(y2, 0, HALF), "ra_c3", to_other)
    got("ra_rm")
    go(ranks(y2, HALF, HALF), ranks(y2, HALF, HALF), "ra_c4", to_other)

    for k in range(4):
        finish(1, k)
    for i in range(5):
        got("ra_c%d" % i)
    l_u.wait()
    blend(up_all, rank_all, base_out, mix, 1, range(16))

    def group(i, carry):
        for n in range(2):
            at = pl.multiple_of(32 * i + 16 * n, 16)
            done[pl.ds(at, 16)] = place(pick, mix, 2 * i + n)
        return carry

    lax.fori_loop(0, GROUPS // 2, group, 0)
    base_done(0)
    for k in range(4):
        finish(0, k)
    for own, cp in some:

        @pl.when(jnp.logical_not(own))
        def _():
            cp.wait_send()

    for cp in sends:
        cp.wait_send()


def combine(up, rank, base, pick, done, q_out, v_out, mix, obuf, osem, dsem):
    whole = pltpu.make_async_copy(done, v_out, dsem.at[0])
    whole.start()
    blend(up, rank, base, mix, 0, range(16))

    def put(i, slot):
        return pltpu.make_async_copy(
            obuf.at[slot], q_out.at[pl.ds(32 * i, 32)], osem.at[slot]
        )

    def group(i, carry):
        slot = lax.rem(i, 2)

        @pl.when(i >= 2)
        def _():
            put(i - 2, slot).wait()

        for n in range(2):
            obuf[slot, 16 * n : 16 * (n + 1)] = place(pick, mix, 2 * i + n)
        put(i, slot).start()
        return carry

    lax.fori_loop(0, GROUPS // 2, group, 0)
    for i in (GROUPS // 2 - 2, GROUPS // 2 - 1):
        put(i, i % 2).wait()
    whole.wait()


def stay(array):
    return pltpu.with_memory_space_constraint(array, pltpu.HBM)


def body(
    prompt_token_states,
    gain,
    projection_weight,
    adapter_down_maps,
    adapter_up_maps,
    prompt_token_length,
    prompt_of_request,
    adapter_of_request,
    adapter_slot_index,
):
    weight = jnp.transpose(projection_weight, (1, 0, 2))
    vmem = pl.BlockSpec(memory_space=pltpu.VMEM)
    hbm = pl.BlockSpec(memory_space=pltpu.HBM)
    anyw = pl.BlockSpec(memory_space=pl.ANY)
    lens = prompt_token_length.reshape(1, -1)
    por = prompt_of_request.reshape(1, -1)
    aor = adapter_of_request.reshape(1, -1)
    asi = adapter_slot_index.reshape(1, -1)
    gathered = pl.pallas_call(
        exchange,
        out_shape=(
            jax.ShapeDtypeStruct((4, 4, 2, RANK, OUT), BF16),
            jax.ShapeDtypeStruct((4, 2, TOK, 512), BF16),
            jax.ShapeDtypeStruct((2, TOK, OUT), F32),
            jax.ShapeDtypeStruct((GROUPS, 256, 256), BF16),
            jax.ShapeDtypeStruct((TOK, SLOTS, OUT), BF16),
        ),
        in_specs=[hbm, hbm, anyw, hbm, hbm, hbm, hbm, hbm, hbm],
        out_specs=(vmem, vmem, vmem, vmem, vmem),
        scratch_shapes=[
            pltpu.VMEM((TOK, FEAT), BF16),
            pltpu.VMEM((FEAT,), BF16),
            pltpu.VMEM(lens.shape, jnp.int32),
            pltpu.VMEM(por.shape, jnp.int32),
            pltpu.VMEM(aor.shape, jnp.int32),
            pltpu.VMEM(asi.shape, jnp.int32),
            pltpu.VMEM((TOK, FEAT), BF16),
            pltpu.VMEM((4, TOK, 4 * PAD), BF16),
            pltpu.VMEM((2, 4, PAD, OUT), BF16),
            pltpu.VMEM((4, BLK, RANK), BF16),
            pltpu.VMEM((4, PAD, 512), BF16),
            pltpu.VMEM((2, TOK, OUT), BF16),
            pltpu.VMEM((2, 2, HALF, OUT), BF16),
            pltpu.VMEM((2, 2, HALF, OUT), F32),
            pltpu.VMEM((2, 2, HALF, OUT), BF16),
            pltpu.VMEM((2, 2, HALF, OUT), BF16),
            pltpu.VMEM((2, 2, TOK, OUT), BF16),
            pltpu.VMEM((2, TOK, OUT), F32),
            pltpu.VMEM((TOK, 512), BF16),
            pltpu.VMEM((2, HALF, 512), BF16),
            pltpu.VMEM((2, HALF, 512), F32),
            pltpu.VMEM((2, HALF, 512), BF16),
            pltpu.VMEM((2, HALF, 512), BF16),
            pltpu.VMEM((2, TOK, 512), BF16),
            pltpu.VMEM((TOK, 512), F32),
            pltpu.VMEM((8, TOK), F32),
            pltpu.VMEM((7, 8, TOK), F32),
            pltpu.VMEM((GROUPS, 256, OUT), BF16),
            pltpu.SemaphoreType.DMA((NSEM,)),
            pltpu.SemaphoreType.DMA((NSEM,)),
            pltpu.SemaphoreType.DMA((9,)),
        ],
        compiler_params=pltpu.CompilerParams(
            collective_id=0, has_side_effects=True, vmem_limit_bytes=27 << 20
        ),
        name="exchange",
    )(
        stay(prompt_token_states),
        stay(gain),
        weight,
        stay(adapter_down_maps.reshape(FEAT, 2 * RANK)),
        stay(adapter_up_maps.reshape(2, RANK, OUT)),
        stay(lens),
        stay(por),
        stay(aor),
        stay(asi),
    )
    return pl.pallas_call(
        combine,
        out_shape=(
            jax.ShapeDtypeStruct((TOK, SLOTS, OUT), BF16),
            jax.ShapeDtypeStruct((TOK, SLOTS, OUT), BF16),
        ),
        in_specs=[vmem] * 5,
        out_specs=(anyw, anyw),
        scratch_shapes=[
            pltpu.VMEM((GROUPS, 256, OUT), BF16),
            pltpu.VMEM((2, 32, SLOTS, OUT), BF16),
            pltpu.SemaphoreType.DMA((2,)),
            pltpu.SemaphoreType.DMA((1,)),
        ],
        compiler_params=pltpu.CompilerParams(vmem_limit_bytes=20 << 20),
        name="combine",
    )(*gathered)


def solution(mesh):
    placed = (
        P("col", "row"),
        P("row"),
        P("col", None, "row"),
        P("col", "row", None),
        P("col", None, None, "row"),
        P(),
        P(),
        P(),
        P(),
    )
    return jax.shard_map(
        body,
        mesh=mesh,
        in_specs=placed,
        out_specs=(P("col", None, "row"), P("col", None, "row")),
        check_vma=False,
    )
```
